512 devices in a mesh: grp: 32 (over z, x_lo), ep: 16 (over y, x_hi, core).
Axes of the slice: x: 4 (x_hi: 2, x_lo: 2; x = x_hi * 2 + x_lo), y: 4, z: 16, core: 2. Of those that a mesh axis runs over, the one named last changes fastest.
Arguments:
- hidden: bfloat16 [256, 1536], P('grp', 'ep'), may hold values from -12 to 12
- query: bfloat16 [256, 1536], P('grp'), may hold values from -16 to 16
- new_kv: bfloat16 [256, 2, 512], P('grp'), may hold values from -4 to 4
- key_cache: bfloat16 [98304, 512], P(('grp', 'ep')), may hold values from -6 to 6
- value_cache: bfloat16 [98304, 512], P(('grp', 'ep')), may hold values from -4 to 4
- page_owner: int32 [6144], P(('grp', 'ep')), may hold values from 0 to 15, as said below
- page_fill: int32 [6144], P(('grp', 'ep')), may hold values from 1 to 16, as said below
- out_weight: bfloat16 [1536, 1536], P('grp', 'ep'), may hold values from -0.75 to 0.75
- norm_gain: float32 [1536], P('ep'), may hold values from 0.25 to 1.75
- gate_up: bfloat16 [32, 1536, 1024], P('grp'), may hold values from -0.15625 to 0.15625
- down: bfloat16 [32, 512, 1536], P('grp'), may hold values from -0.25 to 0.25
- routes: int32 [256, 8], P('grp'), may hold values from 0 to 31, all different within a row; in each aligned block of 8 rows (0 to 7, 8 to 15, ...) at most 4 rows name the same one
- route_weight: bfloat16 [256, 8], P('grp'), may hold values from 0.049804688 to 0.3984375
Outputs:
- layer_out: bfloat16 [256, 1536], P('grp', 'ep')
- attn_out: bfloat16 [256, 1536], P('grp')
The draws below stay inside these ranges and needn't reach their ends.
Inputs may be any that keep to these rules, and one draw needn't show every extreme that they name: `routes`: each row names 8 different experts. In each group's 8 rows (aligned blocks of 8 rows) no expert is named by more than 4 rows, a bound that some block reaches. `page_owner`: A value r under 8 names row r of the page's own group; a value 8 + r names row r of the partner group, whose index differs in the lowest bit. The first page_fill[p] tokens of page p are cached; the rest of the page is unused. The first page of every device is full.
All inputs are finite; a program needn't handle non-finite values.
Results may differ from the reference program's by a relative error of at most 0.017.
Values may be sent and summed in bfloat16 or wider, within the bound.
A program may use at most 64 MiB of HBM per device.

```python
import math
import jax
import jax.numpy as jnp
import numpy as np
from jax import lax

D = 1536
HEADS = 24
KV_HEADS = 8
HD = 64
FF = 512
TOP = 8
PAGE = 16
ROWS = 8
PAGES_DEV = 12
GROUPS = 32
EXPERTS = 32
CAP = 4
REQUESTS = 256
PAGES_GRP = 192
PAGES = 6144
CACHE_TOK = 98304


def draw_hidden(key, part):
    first_key, second_key, third_key = jax.random.split(jax.random.fold_in(key, 3), 3)
    base = jnp.clip(jax.random.normal(first_key, (REQUESTS, D), jnp.float32), -4.0, 4.0)
    row_scale = jnp.exp(jax.random.uniform(second_key, (REQUESTS, 1), jnp.float32, math.log(0.5), math.log(2.5)))
    column_rise = 0.6 * jnp.exp(math.log(3.0) * jnp.arange(D, dtype=jnp.float32) / D)
    column_scale = column_rise[None, :] * jnp.exp(jax.random.uniform(third_key, (1, D), jnp.float32, math.log(0.7), math.log(1.4)))
    return jnp.clip(base * row_scale * column_scale, -12.0, 12.0).astype(jnp.bfloat16)


def draw_query(key, part):
    first_key = jax.random.fold_in(jax.random.fold_in(key, 7), 0)
    return jnp.clip(jax.random.normal(first_key, (REQUESTS, HEADS * HD), jnp.float32), -4.0, 4.0).astype(jnp.bfloat16)


def draw_key_cache(key, part):
    noise_key = jax.random.fold_in(key, 9)
    noise = jnp.clip(jax.random.normal(noise_key, (CACHE_TOK, KV_HEADS, HD), jnp.float32), -4.0, 4.0)
    return noise.reshape(CACHE_TOK, KV_HEADS * HD).astype(jnp.bfloat16)


def draw_page_owner(key, part):
    split_rows = jax.random.randint(jax.random.fold_in(key, 21), (GROUPS, ROWS), 0, 2)
    first_pick = jax.random.randint(jax.random.fold_in(key, 22), (GROUPS, PAGES_GRP), 0, 2 * ROWS)
    second_pick = jax.random.randint(jax.random.fold_in(key, 23), (GROUPS, PAGES_GRP), 0, 2 * ROWS)
    raw_owner = jnp.minimum(first_pick, second_pick)
    partner = jnp.bitwise_xor(jnp.arange(GROUPS, dtype=jnp.int32), 1)
    partner_split = split_rows[partner]
    local_row = raw_owner % ROWS
    allowed = jnp.take_along_axis(partner_split, local_row, axis=1) == 1
    owner = jnp.where((raw_owner >= ROWS) & jnp.logical_not(allowed), local_row, raw_owner)
    return owner.reshape(PAGES).astype(jnp.int32)


def draw_page_fill(key, part):
    full_page = jax.random.randint(jax.random.fold_in(key, 11), (PAGES,), 0, 4) > 0
    partial_value = jax.random.randint(jax.random.fold_in(key, 12), (PAGES,), 1, PAGE + 1)
    fill_count = jnp.where(full_page, PAGE, partial_value)
    first_page = jnp.arange(PAGES, dtype=jnp.int32) % PAGES_DEV == 0
    return jnp.where(first_page, PAGE, fill_count).astype(jnp.int32)


def levels(key, dims, cuts, low, largest):
    def one(position, parts):
        heights = jax.random.uniform(jax.random.fold_in(jax.random.fold_in(key, 6), position), (parts,), jnp.float32, low / len(cuts), largest / len(cuts))
        return jnp.repeat(jnp.exp(heights), dims[position] // parts).reshape((-1,) + (1,) * (len(dims) - position - 1))

    factor_of = one(*cuts[0])
    for cut in cuts[1:]:
        factor_of = factor_of * one(*cut)
    return factor_of


def deal_out(stream_key, own, number, rows, count, top, most, slope):
    sequence = jax.random.permutation(stream_key, count)
    heavy_load, ordinary = portions_of(count, rows * top, most, slope, True), portions_of(count, rows * top, most, slope, False)
    places = jnp.arange(count)

    def named(tallies, rotation):
        used = int((tallies > 0).sum())
        fixed = max(1, used // 4)
        shifted = fixed + (places - fixed + rotation * (used - fixed)) % max(1, count - fixed)
        return jnp.zeros((count,), jnp.int32).at[sequence[jnp.where(places < fixed, places, shifted)]].set(jnp.asarray(tallies, jnp.int32))

    tallies = jnp.where(number % 4 == 0, named(heavy_load, number // 4), named(ordinary, number - number // 4 - 1))
    mixed = jax.random.permutation(jax.random.fold_in(own, 3), count)
    donor, sink = mixed[0:count // 2 * 2:2], mixed[1:count // 2 * 2:2]
    slack = jnp.minimum(tallies[donor] - 1, most - tallies[sink]) // 2
    slack = jnp.where((donor == sequence[0]) | (sink == sequence[0]) | (tallies[sink] == 0), 0, jnp.maximum(slack, 0))
    shifted = jax.random.randint(jax.random.fold_in(own, 4), (count // 2,), 0, 1 << 20) % (slack + 1)
    tallies = tallies.at[donor].add(-shifted).at[sink].add(shifted)
    members = jnp.searchsorted(jnp.cumsum(tallies), jnp.arange(rows * top), side="right").astype(jnp.int32)
    table = members.reshape(top, rows).T
    table = table[jax.random.permutation(jax.random.fold_in(own, 1), rows)]
    rotation = jax.random.randint(jax.random.fold_in(own, 2), (rows, 1), 0, top)
    return jnp.take_along_axis(table, (jnp.arange(top)[None, :] + rotation) % top, axis=1)


def portions_of(number_of, total, bound, skew, full):
    loads = [(1 << 20) // math.isqrt(standing ** skew) + 1 for standing in range(1, number_of + 1)]
    largest = bound if full else min(bound, max(-(-total // number_of), total * loads[0] // sum(loads)))
    least = 1 if total - largest >= number_of - 1 else 0
    counts, rest = [largest] + [least] * (number_of - 1), total - largest - least * (number_of - 1)
    while rest > 0:
        candidates = [i for i in range(1, number_of) if counts[i] < largest] or [i for i in range(1, number_of) if counts[i] < bound]
        whole, remaining = sum([loads[i] for i in candidates]), rest
        for i in candidates:
            more = min(bound - counts[i], max(1, remaining * loads[i] // whole), rest)
            counts[i] = counts[i] + more
            rest = rest - more
    return np.array(counts)


def centred(rng, dims, spread, reach, cuts=(), kind=jnp.bfloat16):
    values = spread * jax.random.normal(rng, dims, jnp.float32)
    if cuts:
        values = values * levels(rng, dims, cuts, -0.22, 0.18)
    return jnp.clip(values, -reach, reach).astype(kind)


def setup_inputs(seed: int = 0) -> dict:
    streams_of = jax.random.split(jax.random.key(seed), 14)
    hidden = draw_hidden(jax.random.fold_in(streams_of[13], 71), 0)
    query = draw_query(jax.random.fold_in(streams_of[13], 71), 0)
    new_kv = centred(streams_of[2], (REQUESTS, 2, KV_HEADS * HD), 1.0, 4.0, ((0, 32),))
    key_cache = draw_key_cache(jax.random.fold_in(streams_of[13], 71), 0)
    value_cache = centred(streams_of[4], (CACHE_TOK, KV_HEADS * HD), 1.0, 4.0, ((0, 512),))
    page_owner = draw_page_owner(jax.random.fold_in(streams_of[13], 71), 0)
    page_fill = draw_page_fill(jax.random.fold_in(streams_of[13], 71), 0)
    out_weight = centred(streams_of[7], (HEADS * HD, D), HD ** -0.5, 0.75, ((0, 32), (1, 16)))
    norm_gain = jnp.clip(1.0 + 0.15 * jax.random.normal(streams_of[8], (D,), jnp.float32), 0.25, 1.75)
    gate_up = centred(streams_of[9], (EXPERTS, D, 2 * FF), D ** -0.5, 0.15625, ((0, 32),))
    down = centred(streams_of[10], (EXPERTS, FF, D), FF ** -0.5, 0.25, ((0, 32),))
    routes_keys = jax.random.split(jax.random.fold_in(streams_of[11], 1), REQUESTS // ROWS)
    routes_turns = jax.random.permutation(jax.random.fold_in(streams_of[11], 3), REQUESTS // ROWS)
    routes = jax.vmap(lambda own, number: deal_out(jax.random.fold_in(streams_of[11], 2), own, number, ROWS, EXPERTS, TOP, CAP, 2))(routes_keys, routes_turns).reshape((REQUESTS, TOP))
    route_weight = jnp.clip(0.049804688 + 0.3486328 * jax.random.uniform(streams_of[12], (REQUESTS, TOP), jnp.float32) ** levels(streams_of[12], (REQUESTS, TOP), ((0, 32),), -0.2, 0.2), 0.049804688, 0.3984375).astype(jnp.bfloat16)
    return dict(hidden=hidden, query=query, new_kv=new_kv, key_cache=key_cache, value_cache=value_cache, page_owner=page_owner, page_fill=page_fill, out_weight=out_weight, norm_gain=norm_gain, gate_up=gate_up, down=down, routes=routes, route_weight=route_weight)


masked_score = -1e+30
norm_epsilon = 1e-05

def reference(hidden, query, new_kv, key_cache, value_cache, page_owner, page_fill, out_weight, norm_gain, gate_up, down, routes, route_weight):
    head_group = HEADS // KV_HEADS
    scale = HD ** (-0.5)
    group_ids = jnp.arange(GROUPS, dtype=jnp.int32)[:, None]
    owners = page_owner.reshape(GROUPS, PAGES_GRP)
    partner = jnp.bitwise_xor(group_ids, 1)
    request = jnp.where(owners < ROWS, group_ids * ROWS + owners, partner * ROWS + owners - ROWS).astype(jnp.int32)
    in_page = jnp.arange(PAGE, dtype=jnp.int32)
    usable = in_page[None, None, :] < page_fill.reshape(GROUPS, PAGES_GRP)[:, :, None]
    key_pages = key_cache.reshape(GROUPS, PAGES_GRP, PAGE, KV_HEADS, HD)
    value_pages = value_cache.reshape(GROUPS, PAGES_GRP, PAGE, KV_HEADS, HD)
    query_heads = query.reshape(REQUESTS, KV_HEADS, head_group, HD)

    def page_scores(block_request, block_keys, block_usable):
        page_query = query_heads[block_request].astype(jnp.float32)
        scores = jnp.einsum('pkgd,pjkd->pjkg', page_query, block_keys.astype(jnp.float32), precision=lax.Precision.HIGHEST) * scale
        return jnp.where(block_usable[:, :, None, None], scores, masked_score)

    def max_step(carry, inputs):
        block_request, block_keys, block_usable = inputs
        page_top = lax.optimization_barrier(jnp.max(page_scores(block_request, block_keys, block_usable), 1))
        found = jax.ops.segment_max(page_top, block_request, num_segments=REQUESTS)
        return (jnp.maximum(carry, found), None)
    start_top = jnp.full((REQUESTS, KV_HEADS, head_group), masked_score, jnp.float32)
    cache_top, _ = lax.scan(max_step, start_top, (request, key_pages, usable))
    fresh = new_kv.astype(jnp.float32)
    fresh_key = fresh[:, 0].reshape(REQUESTS, KV_HEADS, HD)
    fresh_value = fresh[:, 1].reshape(REQUESTS, KV_HEADS, HD)
    own_score = jnp.einsum('rkgd,rkd->rkg', query_heads.astype(jnp.float32), fresh_key, precision=lax.Precision.HIGHEST) * scale
    highest = jnp.maximum(cache_top, own_score)

    def sum_step(carry, inputs):
        total, accum = carry
        block_request, block_keys, block_values, block_usable = inputs
        scores = page_scores(block_request, block_keys, block_usable)
        weights = jnp.where(block_usable[:, :, None, None], jnp.exp(scores - highest[block_request][:, None]), 0.0)
        rounded = lax.optimization_barrier(weights.astype(jnp.bfloat16))
        page_accum = jnp.einsum('pjkg,pjkd->pkgd', rounded.astype(jnp.float32), block_values.astype(jnp.float32), precision=lax.Precision.HIGHEST)
        total = total + jax.ops.segment_sum(lax.optimization_barrier(jnp.sum(weights, 1)), block_request, num_segments=REQUESTS)
        accum = accum + jax.ops.segment_sum(page_accum, block_request, num_segments=REQUESTS)
        return ((total, accum), None)
    start_sum = (jnp.zeros((REQUESTS, KV_HEADS, head_group), jnp.float32), jnp.zeros((REQUESTS, KV_HEADS, head_group, HD), jnp.float32))
    (cache_total, cache_accum), _ = lax.scan(sum_step, start_sum, (request, key_pages, value_pages, usable))
    own_weight = jnp.exp(own_score - highest)
    denominator = cache_total + own_weight
    numerator = cache_accum + own_weight[..., None] * fresh_value[:, :, None, :]
    attn_out = (numerator / denominator[..., None]).reshape(REQUESTS, HEADS * HD).astype(jnp.bfloat16)
    mixed = hidden.astype(jnp.float32) + jnp.dot(attn_out, out_weight, preferred_element_type=jnp.float32)
    normed = (mixed * lax.rsqrt(lax.optimization_barrier(jnp.mean(mixed * mixed, -1, keepdims=True)) + norm_epsilon) * norm_gain).astype(jnp.bfloat16)
    gate_share = route_weight.astype(jnp.float32)

    def expert_step(total, inputs):
        expert_index, up_weight, down_weight = inputs
        pre_sum = jnp.dot(normed, up_weight, preferred_element_type=jnp.float32)
        activated = (jax.nn.silu(pre_sum[:, :FF]) * pre_sum[:, FF:]).astype(jnp.bfloat16)
        expert_out = jnp.dot(activated, down_weight, preferred_element_type=jnp.float32).astype(jnp.bfloat16)
        share = lax.optimization_barrier(jnp.sum(jnp.where(routes == expert_index, gate_share, 0.0), 1))
        return (total + share[:, None] * expert_out.astype(jnp.float32), None)
    expert_mix, _ = lax.scan(expert_step, jnp.zeros((REQUESTS, D), jnp.float32), (jnp.arange(EXPERTS, dtype=jnp.int32), gate_up, down))
    layer_out = (mixed + expert_mix).astype(jnp.bfloat16)
    return (layer_out, attn_out)
```

```python
import jax
import jax.numpy as jnp
from jax import lax
from jax.sharding import PartitionSpec as P

D = 1536
HEADS = 24
KV_HEADS = 8
HD = 64
FF = 512
TOP = 8


masked_score = -1e30
norm_epsilon = 1e-05


def from_partner(block, axis, apart):
    count = lax.axis_size(axis)
    route = []
    for low in range(count):
        high = low | 1 << apart
        if high != low and high < count:
            route += [(low, high), (high, low)]
    return lax.ppermute(block, axis, route)


def combined_all(part, axis, combine):
    gathered = jax.tree.map(lambda a: lax.all_gather(a, axis), part)

    def take(source):
        return jax.tree.map(lambda a: lax.dynamic_index_in_dim(a, source, 0, False), gathered)

    return lax.fori_loop(
        1, lax.axis_size(axis), lambda source, state: combine(state, take(source)), take(0)
    )


def merge_stack(parts):
    maxes, totals, accums = parts
    highest = jnp.max(maxes, 0)
    factors = jnp.exp(maxes - highest[None])
    return (
        highest,
        jnp.sum(totals * factors, 0),
        jnp.sum(accums * factors[..., None], 0),
    )


def merge_parts(earlier, later):
    max_one, total_one, accum_one = earlier
    max_two, total_two, accum_two = later
    highest = jnp.maximum(max_one, max_two)
    factor_one = jnp.exp(max_one - highest)
    factor_two = jnp.exp(max_two - highest)
    return (
        highest,
        total_one * factor_one + total_two * factor_two,
        accum_one * factor_one[..., None] + accum_two * factor_two[..., None],
    )


def per_device(
    hidden,
    query,
    new_kv,
    key_cache,
    value_cache,
    page_owner,
    page_fill,
    out_weight,
    norm_gain,
    gate_up,
    down,
    routes,
    route_weight,
):
    row_count = query.shape[0]
    group_count = lax.axis_size("grp")
    head_group = HEADS // KV_HEADS
    page_count = page_owner.shape[0]
    token_count = key_cache.shape[0]
    page_length = token_count // page_count
    both_rows = 2 * row_count
    scale = HD ** (-0.5)
    partner_query = from_partner(query, "grp", 0)
    all_queries = jnp.concatenate([query, partner_query], 0)
    query_heads = (
        all_queries.reshape(both_rows, KV_HEADS, head_group, HD)
        .transpose(1, 0, 2, 3)
        .reshape(KV_HEADS, both_rows * head_group, HD)
    )
    key_heads = key_cache.reshape(token_count, KV_HEADS, HD)
    value_heads = value_cache.reshape(token_count, KV_HEADS, HD)
    scores = (
        jnp.einsum("kqd,tkd->kqt", query_heads, key_heads, preferred_element_type=jnp.float32)
        * scale
    )
    scores = scores.reshape(KV_HEADS, both_rows, head_group, token_count)
    row_index = jnp.arange(both_rows, dtype=jnp.int32)
    in_page = jnp.arange(page_length, dtype=jnp.int32)
    usable = (page_owner[None, :, None] == row_index[:, None, None]) & (
        in_page[None, None, :] < page_fill[None, :, None]
    )
    usable = usable.reshape(both_rows, token_count)[None, :, None, :]
    local_top = jnp.max(jnp.where(usable, scores, masked_score), -1)
    weights = jnp.where(usable, jnp.exp(scores - local_top[..., None]), 0.0)
    local_total = jnp.sum(weights, -1)
    rounded = weights.astype(jnp.bfloat16).reshape(KV_HEADS, both_rows * head_group, token_count)
    local_accum = jnp.einsum(
        "kqt,tkd->kqd", rounded, value_heads, preferred_element_type=jnp.float32
    )
    part_max = local_top.transpose(1, 0, 2).reshape(both_rows, HEADS)
    part_total = local_total.transpose(1, 0, 2).reshape(both_rows, HEADS)
    part_accum = (
        local_accum.reshape(KV_HEADS, both_rows, head_group, HD)
        .transpose(1, 0, 2, 3)
        .reshape(both_rows, HEADS, HD)
    )
    gathered = lax.all_gather((part_max, part_total, part_accum), "ep")
    merged = merge_stack(gathered)
    returned = from_partner(
        (merged[0][row_count:], merged[1][row_count:], merged[2][row_count:]), "grp", 0
    )
    combined = merge_parts(
        (merged[0][:row_count], merged[1][:row_count], merged[2][:row_count]), returned
    )
    own_query = query.reshape(row_count, KV_HEADS, head_group, HD)
    fresh_key = new_kv[:, 0].reshape(row_count, KV_HEADS, HD)
    fresh_value = new_kv[:, 1].astype(jnp.float32).reshape(row_count, KV_HEADS, HD)
    own_score = (
        jnp.einsum(
            "rkgd,rkd->rkg", own_query, fresh_key, preferred_element_type=jnp.float32
        ).reshape(row_count, HEADS)
        * scale
    )
    cache_max, cache_total, cache_accum = combined
    highest = jnp.maximum(cache_max, own_score)
    cache_factor = jnp.exp(cache_max - highest)
    own_weight = jnp.exp(own_score - highest)
    value_rows = jnp.broadcast_to(
        fresh_value[:, :, None, :], (row_count, KV_HEADS, head_group, HD)
    ).reshape(row_count, HEADS, HD)
    numerator = cache_accum * cache_factor[..., None] + own_weight[..., None] * value_rows
    denominator = cache_total * cache_factor + own_weight
    attn_out = (
        (numerator / denominator[..., None]).reshape(row_count, HEADS * HD).astype(jnp.bfloat16)
    )
    weight_columns = lax.all_gather(out_weight, "grp", axis=0, tiled=True)
    projected = jnp.dot(attn_out, weight_columns, preferred_element_type=jnp.float32)
    feature_share = hidden.shape[1]
    mixed = hidden.astype(jnp.float32) + projected
    squares = lax.psum(jnp.sum(mixed * mixed, -1), "ep")
    normed = (mixed * lax.rsqrt(squares / D + norm_epsilon)[:, None] * norm_gain).astype(
        jnp.bfloat16
    )
    capacity = min(row_count, 2 * row_count * TOP // group_count)
    expert_ids = jnp.arange(group_count, dtype=jnp.int32)
    flat_routes = routes.reshape(-1)
    hits = (flat_routes[:, None] == expert_ids[None, :]).astype(jnp.int32)
    earlier_hits = jnp.cumsum(hits, 0) - hits
    position = jnp.sum(earlier_hits * hits, 1)
    slot_index = flat_routes * capacity + position
    slots_all = jnp.arange(group_count * capacity, dtype=jnp.int32)
    picker = jnp.any(
        slot_index.reshape(row_count, TOP)[None, :, :] == slots_all[:, None, None], 2
    ).astype(jnp.bfloat16)
    sender = (
        jnp.dot(picker, normed, preferred_element_type=jnp.float32)
        .astype(jnp.bfloat16)
        .reshape(group_count, capacity, feature_share)
    )
    arrived = lax.all_to_all(sender, "grp", split_axis=0, concat_axis=0, tiled=True)
    whole_rows = lax.all_to_all(
        arrived.reshape(group_count * capacity, feature_share),
        "ep",
        split_axis=0,
        concat_axis=1,
        tiled=True,
    )
    pre_sum = jnp.dot(whole_rows, gate_up[0], preferred_element_type=jnp.float32)
    activated = (jax.nn.silu(pre_sum[:, :FF]) * pre_sum[:, FF:]).astype(jnp.bfloat16)
    result = jnp.dot(activated, down[0], preferred_element_type=jnp.float32).astype(jnp.bfloat16)
    served = lax.all_to_all(result, "ep", split_axis=1, concat_axis=0, tiled=True).reshape(
        group_count, capacity, feature_share
    )
    returned_rows = lax.all_to_all(served, "grp", split_axis=0, concat_axis=0, tiled=True)
    gathered_rows = returned_rows.reshape(group_count * capacity, feature_share)[
        slot_index
    ].reshape(row_count, TOP, feature_share)
    expert_mix = jnp.sum(
        route_weight.astype(jnp.float32)[:, :, None] * gathered_rows.astype(jnp.float32), 1
    )
    layer_out = (mixed + expert_mix).astype(jnp.bfloat16)
    return (layer_out, attn_out)


def solution(mesh):
    placed = (
        P("grp", "ep"),
        P("grp", None),
        P("grp", None, None),
        P(("grp", "ep"), None),
        P(("grp", "ep"), None),
        P(("grp", "ep")),
        P(("grp", "ep")),
        P("grp", "ep"),
        P("ep"),
        P("grp", None, None),
        P("grp", None, None),
        P("grp", None),
        P("grp", None),
    )
    return jax.shard_map(
        per_device,
        mesh=mesh,
        in_specs=placed,
        out_specs=(P("grp", "ep"), P("grp", None)),
        check_vma=False,
    )
```

```python
import jax
import jax.numpy as jnp
from jax import lax
from jax.experimental import pallas as pl
from jax.experimental.pallas import tpu as pltpu
from jax.sharding import PartitionSpec as P
import functools

D = 1536
HEADS = 24
KV_HEADS = 8
HD = 64
FF = 512
TOP = 8


masked_score = -1e30

MESH = pl.DeviceIdType.MESH


def merge_kernel(rows, n_ep, part_ref, own_ref, out_ref, got, final, s1, r1, s2, r2):
    g = lax.axis_index("grp")
    e = lax.axis_index("ep")
    mate = g + 1 - 2 * (g % 2)
    barrier = pltpu.get_barrier_semaphore()
    for peer in range(n_ep):
        @pl.when(e != peer)
        def _():
            pl.semaphore_signal(barrier, inc=1, device_id=(g, peer), device_id_type=MESH)
        pl.semaphore_signal(barrier, inc=1, device_id=(mate, peer), device_id_type=MESH)
    pl.semaphore_wait(barrier, 2 * n_ep - 1)

    def first(row):
        if row < rows:
            target = (g, row)
            slot = e
        else:
            target = (mate, row - rows)
            slot = n_ep + e
        return pltpu.make_async_remote_copy(
            src_ref=part_ref.at[row], dst_ref=got.at[slot], send_sem=s1.at[row],
            recv_sem=r1.at[slot], device_id=target, device_id_type=MESH)

    for row in range(2 * rows):
        if row < rows:
            @pl.when(e != row)
            def _():
                first(row).start()

            @pl.when(e == row)
            def _():
                got[e] = part_ref[row]
        else:
            first(row).start()

    def incoming(slot):
        return pltpu.make_async_remote_copy(
            src_ref=part_ref.at[0], dst_ref=got.at[slot], send_sem=s1.at[0],
            recv_sem=r1.at[slot], device_id=(g, 0), device_id_type=MESH)

    def second(target):
        return pltpu.make_async_remote_copy(
            src_ref=final.at[e], dst_ref=final.at[e], send_sem=s2.at[target],
            recv_sem=r2.at[e], device_id=(g, target), device_id_type=MESH)

    @pl.when(e < rows)
    def _():
        for slot in range(2 * n_ep):
            if slot < n_ep:
                @pl.when(e != slot)
                def _():
                    incoming(slot).wait_recv()
            else:
                incoming(slot).wait_recv()
        stack = got[...]
        own = own_ref[e]
        maxes = jnp.maximum(jnp.max(stack[:, :, HD:HD + 1], 0), own[:, HD:HD + 1])
        factors = jnp.exp(stack[:, :, HD:HD + 1] - maxes[None])
        own_factor = jnp.exp(own[:, HD:HD + 1] - maxes)
        total = jnp.sum(stack[:, :, HD + 1:HD + 2] * factors, 0) + own_factor
        accum = jnp.sum(stack[:, :, :HD] * factors, 0) + own[:, :HD] * own_factor
        final[e] = (accum / total).astype(final.dtype)
        for target in range(n_ep):
            @pl.when(e != target)
            def _():
                second(target).start()

    for row in range(2 * rows):
        if row < rows:
            @pl.when(e != row)
            def _():
                first(row).wait_send()
        else:
            first(row).wait_send()

    def arriving(row):
        return pltpu.make_async_remote_copy(
            src_ref=final.at[row], dst_ref=final.at[row], send_sem=s2.at[0],
            recv_sem=r2.at[row], device_id=(g, row), device_id_type=MESH)

    for row in range(rows):
        @pl.when(e != row)
        def _():
            arriving(row).wait_recv()

    @pl.when(e < rows)
    def _():
        for target in range(n_ep):
            @pl.when(e != target)
            def _():
                second(target).wait_send()

    out_ref[...] = final[...]


def merge_call(part, own):
    rows = own.shape[0]
    heads = own.shape[1]
    n_ep = lax.axis_size("ep")
    return pl.pallas_call(
        functools.partial(merge_kernel, rows, n_ep),
        out_shape=jax.ShapeDtypeStruct((rows, heads, HD), jnp.bfloat16),
        in_specs=[pl.BlockSpec(memory_space=pltpu.VMEM)] * 2,
        out_specs=pl.BlockSpec(memory_space=pltpu.VMEM),
        scratch_shapes=[
            pltpu.VMEM((2 * n_ep, heads, 128), jnp.float32),
            pltpu.VMEM((rows, heads, HD), jnp.bfloat16),
            pltpu.SemaphoreType.DMA((2 * rows,)),
            pltpu.SemaphoreType.DMA((2 * n_ep,)),
            pltpu.SemaphoreType.DMA((n_ep,)),
            pltpu.SemaphoreType.DMA((rows,)),
        ],
        compiler_params=pltpu.CompilerParams(collective_id=0, has_side_effects=True),
    )(part, own)

norm_epsilon = 1e-05


def from_partner(block, axis, apart):
    count = lax.axis_size(axis)
    route = []
    for low in range(count):
        high = low | 1 << apart
        if high != low and high < count:
            route += [(low, high), (high, low)]
    return lax.ppermute(block, axis, route)


def per_device(
    hidden,
    query,
    new_kv,
    key_cache,
    value_cache,
    page_owner,
    page_fill,
    out_weight,
    norm_gain,
    gate_up,
    down,
    routes,
    route_weight,
):
    row_count = query.shape[0]
    group_count = lax.axis_size("grp")
    head_group = HEADS // KV_HEADS
    page_count = page_owner.shape[0]
    token_count = key_cache.shape[0]
    page_length = token_count // page_count
    both_rows = 2 * row_count
    scale = HD ** (-0.5)
    partner_query = from_partner(query, "grp", 0)
    all_queries = jnp.concatenate([query, partner_query], 0)
    query_heads = (
        all_queries.reshape(both_rows, KV_HEADS, head_group, HD)
        .transpose(1, 0, 2, 3)
        .reshape(KV_HEADS, both_rows * head_group, HD)
    )
    key_heads = key_cache.reshape(token_count, KV_HEADS, HD)
    value_heads = value_cache.reshape(token_count, KV_HEADS, HD)
    scores = (
        jnp.einsum("kqd,tkd->kqt", query_heads, key_heads, preferred_element_type=jnp.float32)
        * scale
    )
    scores = scores.reshape(KV_HEADS, both_rows, head_group, token_count)
    row_index = jnp.arange(both_rows, dtype=jnp.int32)
    in_page = jnp.arange(page_length, dtype=jnp.int32)
    usable = (page_owner[None, :, None] == row_index[:, None, None]) & (
        in_page[None, None, :] < page_fill[None, :, None]
    )
    usable = usable.reshape(both_rows, token_count)[None, :, None, :]
    local_top = jnp.max(jnp.where(usable, scores, masked_score), -1)
    weights = jnp.where(usable, jnp.exp(scores - local_top[..., None]), 0.0)
    local_total = jnp.sum(weights, -1)
    rounded = weights.astype(jnp.bfloat16).reshape(KV_HEADS, both_rows * head_group, token_count)
    local_accum = jnp.einsum(
        "kqt,tkd->kqd", rounded, value_heads, preferred_element_type=jnp.float32
    )
    part_max = local_top.transpose(1, 0, 2).reshape(both_rows, HEADS)
    part_total = local_total.transpose(1, 0, 2).reshape(both_rows, HEADS)
    part_accum = (
        local_accum.reshape(KV_HEADS, both_rows, head_group, HD)
        .transpose(1, 0, 2, 3)
        .reshape(both_rows, HEADS, HD)
    )
    own_query = query.reshape(row_count, KV_HEADS, head_group, HD)
    fresh_key = new_kv[:, 0].reshape(row_count, KV_HEADS, HD)
    fresh_value = new_kv[:, 1].astype(jnp.float32).reshape(row_count, KV_HEADS, HD)
    own_score = (
        jnp.einsum(
            "rkgd,rkd->rkg", own_query, fresh_key, preferred_element_type=jnp.float32
        ).reshape(row_count, HEADS)
        * scale
    )
    value_rows = jnp.broadcast_to(
        fresh_value[:, :, None, :], (row_count, KV_HEADS, head_group, HD)
    ).reshape(row_count, HEADS, HD)
    pad = jnp.zeros((both_rows, HEADS, 128 - HD - 2), jnp.float32)
    packed = jnp.concatenate(
        [part_accum, part_max[..., None], part_total[..., None], pad], -1
    )
    own_packed = jnp.concatenate(
        [value_rows, own_score[..., None], jnp.ones_like(own_score)[..., None], pad[:row_count]], -1
    )
    attn_out = merge_call(packed, own_packed).reshape(row_count, HEADS * HD)
    weight_columns = lax.all_gather(out_weight, "grp", axis=0, tiled=True)
    projected = jnp.dot(attn_out, weight_columns, preferred_element_type=jnp.float32)
    feature_share = hidden.shape[1]
    mixed = hidden.astype(jnp.float32) + projected
    squares = lax.psum(jnp.sum(mixed * mixed, -1), "ep")
    normed = (mixed * lax.rsqrt(squares / D + norm_epsilon)[:, None] * norm_gain).astype(
        jnp.bfloat16
    )
    capacity = min(row_count, 2 * row_count * TOP // group_count)
    expert_ids = jnp.arange(group_count, dtype=jnp.int32)
    flat_routes = routes.reshape(-1)
    hits = (flat_routes[:, None] == expert_ids[None, :]).astype(jnp.int32)
    earlier_hits = jnp.cumsum(hits, 0) - hits
    position = jnp.sum(earlier_hits * hits, 1)
    slot_index = flat_routes * capacity + position
    slots_all = jnp.arange(group_count * capacity, dtype=jnp.int32)
    picker = jnp.any(
        slot_index.reshape(row_count, TOP)[None, :, :] == slots_all[:, None, None], 2
    ).astype(jnp.bfloat16)
    sender = (
        jnp.dot(picker, normed, preferred_element_type=jnp.float32)
        .astype(jnp.bfloat16)
        .reshape(group_count, capacity, feature_share)
    )
    arrived = lax.all_to_all(sender, "grp", split_axis=0, concat_axis=0, tiled=True)
    whole_rows = lax.all_to_all(
        arrived.reshape(group_count * capacity, feature_share),
        "ep",
        split_axis=0,
        concat_axis=1,
        tiled=True,
    )
    pre_sum = jnp.dot(whole_rows, gate_up[0], preferred_element_type=jnp.float32)
    activated = (jax.nn.silu(pre_sum[:, :FF]) * pre_sum[:, FF:]).astype(jnp.bfloat16)
    result = jnp.dot(activated, down[0], preferred_element_type=jnp.float32).astype(jnp.bfloat16)
    served = lax.all_to_all(result, "ep", split_axis=1, concat_axis=0, tiled=True).reshape(
        group_count, capacity, feature_share
    )
    returned_rows = lax.all_to_all(served, "grp", split_axis=0, concat_axis=0, tiled=True)
    gathered_rows = returned_rows.reshape(group_count * capacity, feature_share)[
        slot_index
    ].reshape(row_count, TOP, feature_share)
    expert_mix = jnp.sum(
        route_weight.astype(jnp.float32)[:, :, None] * gathered_rows.astype(jnp.float32), 1
    )
    layer_out = (mixed + expert_mix).astype(jnp.bfloat16)
    return (layer_out, attn_out)


def solution(mesh):
    placed = (
        P("grp", "ep"),
        P("grp", None),
        P("grp", None, None),
        P(("grp", "ep"), None),
        P(("grp", "ep"), None),
        P(("grp", "ep")),
        P(("grp", "ep")),
        P("grp", "ep"),
        P("ep"),
        P("grp", None, None),
        P("grp", None, None),
        P("grp", None),
        P("grp", None),
    )
    return jax.shard_map(
        per_device,
        mesh=mesh,
        in_specs=placed,
        out_specs=(P("grp", "ep"), P("grp", None)),
        check_vma=False,
    )
```

```python
import jax
import jax.numpy as jnp
from jax import lax
from jax.experimental import pallas as pl
from jax.experimental.pallas import tpu as pltpu
from jax.sharding import PartitionSpec as P
import functools

D = 1536
HEADS = 24
KV_HEADS = 8
HD = 64
FF = 512
TOP = 8


masked_score = -1e30

MESH = pl.DeviceIdType.MESH


def merge_kernel(
    rows, n_ep, n_grp, part_ref, own_ref, block_ref, out_ref, columns_ref,
    got, final, blocks, s1, r1, s2, r2, s3, r3,
):
    g = lax.axis_index("grp")
    e = lax.axis_index("ep")
    mate = g + 1 - 2 * (g % 2)
    barrier = pltpu.get_barrier_semaphore()
    for peer in range(n_ep):
        @pl.when(e != peer)
        def _():
            pl.semaphore_signal(barrier, inc=1, device_id=(g, peer), device_id_type=MESH)
        pl.semaphore_signal(barrier, inc=1, device_id=(mate, peer), device_id_type=MESH)
    for step in range(1, n_grp):
        pl.semaphore_signal(
            barrier, inc=1, device_id=(lax.rem(g + step, n_grp), e), device_id_type=MESH
        )
    pl.semaphore_wait(barrier, 2 * n_ep - 1 + n_grp - 1)

    def first(row):
        if row < rows:
            target = (g, row)
            slot = e
        else:
            target = (mate, row - rows)
            slot = n_ep + e
        return pltpu.make_async_remote_copy(
            src_ref=part_ref.at[row], dst_ref=got.at[slot], send_sem=s1.at[row],
            recv_sem=r1.at[slot], device_id=target, device_id_type=MESH)

    for row in range(2 * rows):
        if row < rows:
            @pl.when(e != row)
            def _():
                first(row).start()

            @pl.when(e == row)
            def _():
                got[e] = part_ref[row]
        else:
            first(row).start()

    def spread(step):
        return pltpu.make_async_remote_copy(
            src_ref=block_ref, dst_ref=blocks.at[g], send_sem=s3.at[step],
            recv_sem=r3.at[g], device_id=(lax.rem(g + step, n_grp), e), device_id_type=MESH)

    def gathered(step):
        source = lax.rem(g + n_grp - step, n_grp)
        return pltpu.make_async_remote_copy(
            src_ref=block_ref, dst_ref=blocks.at[source], send_sem=s3.at[step],
            recv_sem=r3.at[source], device_id=(source, e), device_id_type=MESH)

    for step in range(1, n_grp):
        spread(step).start()
    blocks[g] = block_ref[...]

    def incoming(slot):
        return pltpu.make_async_remote_copy(
            src_ref=part_ref.at[0], dst_ref=got.at[slot], send_sem=s1.at[0],
            recv_sem=r1.at[slot], device_id=(g, 0), device_id_type=MESH)

    def second(target):
        return pltpu.make_async_remote_copy(
            src_ref=final.at[e], dst_ref=final.at[e], send_sem=s2.at[target],
            recv_sem=r2.at[e], device_id=(g, target), device_id_type=MESH)

    @pl.when(e < rows)
    def _():
        for slot in range(2 * n_ep):
            if slot < n_ep:
                @pl.when(e != slot)
                def _():
                    incoming(slot).wait_recv()
            else:
                incoming(slot).wait_recv()
        stack = got[...]
        own = own_ref[e]
        maxes = jnp.maximum(jnp.max(stack[:, :, HD:HD + 1], 0), own[:, HD:HD + 1])
        factors = jnp.exp(stack[:, :, HD:HD + 1] - maxes[None])
        own_factor = jnp.exp(own[:, HD:HD + 1] - maxes)
        total = jnp.sum(stack[:, :, HD + 1:HD + 2] * factors, 0) + own_factor
        accum = jnp.sum(stack[:, :, :HD] * factors, 0) + own[:, :HD] * own_factor
        final[e] = (accum / total).astype(final.dtype)
        for target in range(n_ep):
            @pl.when(e != target)
            def _():
                second(target).start()

    for row in range(2 * rows):
        if row < rows:
            @pl.when(e != row)
            def _():
                first(row).wait_send()
        else:
            first(row).wait_send()

    def arriving(row):
        return pltpu.make_async_remote_copy(
            src_ref=final.at[row], dst_ref=final.at[row], send_sem=s2.at[0],
            recv_sem=r2.at[row], device_id=(g, row), device_id_type=MESH)

    for row in range(rows):
        @pl.when(e != row)
        def _():
            arriving(row).wait_recv()

    @pl.when(e < rows)
    def _():
        for target in range(n_ep):
            @pl.when(e != target)
            def _():
                second(target).wait_send()

    for step in range(1, n_grp):
        spread(step).wait_send()
        gathered(step).wait_recv()
    out_ref[...] = final[...]
    columns_ref[...] = blocks[...]


def merge_call(part, own, block):
    rows = own.shape[0]
    heads = own.shape[1]
    n_ep = lax.axis_size("ep")
    n_grp = lax.axis_size("grp")
    gathered_shape = (n_grp,) + block.shape
    return pl.pallas_call(
        functools.partial(merge_kernel, rows, n_ep, n_grp),
        out_shape=(
            jax.ShapeDtypeStruct((rows, heads, HD), jnp.bfloat16),
            jax.ShapeDtypeStruct(gathered_shape, block.dtype),
        ),
        in_specs=[pl.BlockSpec(memory_space=pltpu.VMEM)] * 3,
        out_specs=(pl.BlockSpec(memory_space=pltpu.VMEM),) * 2,
        scratch_shapes=[
            pltpu.VMEM((2 * n_ep, heads, 128), jnp.float32),
            pltpu.VMEM((rows, heads, HD), jnp.bfloat16),
            pltpu.VMEM(gathered_shape, block.dtype),
            pltpu.SemaphoreType.DMA((2 * rows,)),
            pltpu.SemaphoreType.DMA((2 * n_ep,)),
            pltpu.SemaphoreType.DMA((n_ep,)),
            pltpu.SemaphoreType.DMA((rows,)),
            pltpu.SemaphoreType.DMA((n_grp,)),
            pltpu.SemaphoreType.DMA((n_grp,)),
        ],
        compiler_params=pltpu.CompilerParams(collective_id=0, has_side_effects=True),
    )(part, own, block)

norm_epsilon = 1e-05


def from_partner(block, axis, apart):
    count = lax.axis_size(axis)
    route = []
    for low in range(count):
        high = low | 1 << apart
        if high != low and high < count:
            route += [(low, high), (high, low)]
    return lax.ppermute(block, axis, route)


def per_device(
    hidden,
    query,
    new_kv,
    key_cache,
    value_cache,
    page_owner,
    page_fill,
    out_weight,
    norm_gain,
    gate_up,
    down,
    routes,
    route_weight,
):
    row_count = query.shape[0]
    group_count = lax.axis_size("grp")
    head_group = HEADS // KV_HEADS
    page_count = page_owner.shape[0]
    token_count = key_cache.shape[0]
    page_length = token_count // page_count
    both_rows = 2 * row_count
    scale = HD ** (-0.5)
    partner_query = from_partner(query, "grp", 0)
    all_queries = jnp.concatenate([query, partner_query], 0)
    query_heads = (
        all_queries.reshape(both_rows, KV_HEADS, head_group, HD)
        .transpose(1, 0, 2, 3)
        .reshape(KV_HEADS, both_rows * head_group, HD)
    )
    key_heads = key_cache.reshape(token_count, KV_HEADS, HD)
    value_heads = value_cache.reshape(token_count, KV_HEADS, HD)
    scores = (
        jnp.einsum("kqd,tkd->kqt", query_heads, key_heads, preferred_element_type=jnp.float32)
        * scale
    )
    scores = scores.reshape(KV_HEADS, both_rows, head_group, token_count)
    row_index = jnp.arange(both_rows, dtype=jnp.int32)
    in_page = jnp.arange(page_length, dtype=jnp.int32)
    usable = (page_owner[None, :, None] == row_index[:, None, None]) & (
        in_page[None, None, :] < page_fill[None, :, None]
    )
    usable = usable.reshape(both_rows, token_count)[None, :, None, :]
    local_top = jnp.max(jnp.where(usable, scores, masked_score), -1)
    weights = jnp.where(usable, jnp.exp(scores - local_top[..., None]), 0.0)
    local_total = jnp.sum(weights, -1)
    rounded = weights.astype(jnp.bfloat16).reshape(KV_HEADS, both_rows * head_group, token_count)
    local_accum = jnp.einsum(
        "kqt,tkd->kqd", rounded, value_heads, preferred_element_type=jnp.float32
    )
    part_max = local_top.transpose(1, 0, 2).reshape(both_rows, HEADS)
    part_total = local_total.transpose(1, 0, 2).reshape(both_rows, HEADS)
    part_accum = (
        local_accum.reshape(KV_HEADS, both_rows, head_group, HD)
        .transpose(1, 0, 2, 3)
        .reshape(both_rows, HEADS, HD)
    )
    own_query = query.reshape(row_count, KV_HEADS, head_group, HD)
    fresh_key = new_kv[:, 0].reshape(row_count, KV_HEADS, HD)
    fresh_value = new_kv[:, 1].astype(jnp.float32).reshape(row_count, KV_HEADS, HD)
    own_score = (
        jnp.einsum(
            "rkgd,rkd->rkg", own_query, fresh_key, preferred_element_type=jnp.float32
        ).reshape(row_count, HEADS)
        * scale
    )
    value_rows = jnp.broadcast_to(
        fresh_value[:, :, None, :], (row_count, KV_HEADS, head_group, HD)
    ).reshape(row_count, HEADS, HD)
    pad = jnp.zeros((both_rows, HEADS, 128 - HD - 2), jnp.float32)
    packed = jnp.concatenate(
        [part_accum, part_max[..., None], part_total[..., None], pad], -1
    )
    own_packed = jnp.concatenate(
        [value_rows, own_score[..., None], jnp.ones_like(own_score)[..., None], pad[:row_count]], -1
    )
    merged, weight_blocks = merge_call(packed, own_packed, out_weight)
    attn_out = merged.reshape(row_count, HEADS * HD)
    weight_columns = weight_blocks.reshape(-1, out_weight.shape[1])
    projected = jnp.dot(attn_out, weight_columns, preferred_element_type=jnp.float32)
    feature_share = hidden.shape[1]
    mixed = hidden.astype(jnp.float32) + projected
    squares = lax.psum(jnp.sum(mixed * mixed, -1), "ep")
    normed = (mixed * lax.rsqrt(squares / D + norm_epsilon)[:, None] * norm_gain).astype(
        jnp.bfloat16
    )
    capacity = min(row_count, 2 * row_count * TOP // group_count)
    expert_ids = jnp.arange(group_count, dtype=jnp.int32)
    flat_routes = routes.reshape(-1)
    hits = (flat_routes[:, None] == expert_ids[None, :]).astype(jnp.int32)
    earlier_hits = jnp.cumsum(hits, 0) - hits
    position = jnp.sum(earlier_hits * hits, 1)
    slot_index = flat_routes * capacity + position
    slots_all = jnp.arange(group_count * capacity, dtype=jnp.int32)
    picker = jnp.any(
        slot_index.reshape(row_count, TOP)[None, :, :] == slots_all[:, None, None], 2
    ).astype(jnp.bfloat16)
    sender = (
        jnp.dot(picker, normed, preferred_element_type=jnp.float32)
        .astype(jnp.bfloat16)
        .reshape(group_count, capacity, feature_share)
    )
    arrived = lax.all_to_all(sender, "grp", split_axis=0, concat_axis=0, tiled=True)
    whole_rows = lax.all_to_all(
        arrived.reshape(group_count * capacity, feature_share),
        "ep",
        split_axis=0,
        concat_axis=1,
        tiled=True,
    )
    pre_sum = jnp.dot(whole_rows, gate_up[0], preferred_element_type=jnp.float32)
    activated = (jax.nn.silu(pre_sum[:, :FF]) * pre_sum[:, FF:]).astype(jnp.bfloat16)
    result = jnp.dot(activated, down[0], preferred_element_type=jnp.float32).astype(jnp.bfloat16)
    served = lax.all_to_all(result, "ep", split_axis=1, concat_axis=0, tiled=True).reshape(
        group_count, capacity, feature_share
    )
    returned_rows = lax.all_to_all(served, "grp", split_axis=0, concat_axis=0, tiled=True)
    gathered_rows = returned_rows.reshape(group_count * capacity, feature_share)[
        slot_index
    ].reshape(row_count, TOP, feature_share)
    expert_mix = jnp.sum(
        route_weight.astype(jnp.float32)[:, :, None] * gathered_rows.astype(jnp.float32), 1
    )
    layer_out = (mixed + expert_mix).astype(jnp.bfloat16)
    return (layer_out, attn_out)


def solution(mesh):
    placed = (
        P("grp", "ep"),
        P("grp", None),
        P("grp", None, None),
        P(("grp", "ep"), None),
        P(("grp", "ep"), None),
        P(("grp", "ep")),
        P(("grp", "ep")),
        P("grp", "ep"),
        P("ep"),
        P("grp", None, None),
        P("grp", None, None),
        P("grp", None),
        P("grp", None),
    )
    return jax.shard_map(
        per_device,
        mesh=mesh,
        in_specs=placed,
        out_specs=(P("grp", "ep"), P("grp", None)),
        check_vma=False,
    )
```

```python
import jax
import jax.numpy as jnp
from jax import lax
from jax.experimental import pallas as pl
from jax.experimental.pallas import tpu as pltpu
from jax.sharding import PartitionSpec as P
import functools

D = 1536
HEADS = 24
KV_HEADS = 8
HD = 64
FF = 512
TOP = 8


masked_score = -1e30

MESH = pl.DeviceIdType.MESH


def merge_kernel(
    rows, n_ep, n_grp, part_ref, own_ref, block_ref, out_ref, columns_ref,
    got, final, blocks, s1, r1, s2, r2, s3, r3,
):
    g = lax.axis_index("grp")
    e = lax.axis_index("ep")
    mate = g + 1 - 2 * (g % 2)
    barrier = pltpu.get_barrier_semaphore()
    for peer in range(n_ep):
        @pl.when(e != peer)
        def _():
            pl.semaphore_signal(barrier, inc=1, device_id=(g, peer), device_id_type=MESH)
        pl.semaphore_signal(barrier, inc=1, device_id=(mate, peer), device_id_type=MESH)
    for step in range(1, n_grp):
        pl.semaphore_signal(
            barrier, inc=1, device_id=(lax.rem(g + step, n_grp), e), device_id_type=MESH
        )
    pl.semaphore_wait(barrier, 2 * n_ep - 1 + n_grp - 1)

    def first(row):
        if row < rows:
            target = (g, row)
            slot = e
        else:
            target = (mate, row - rows)
            slot = n_ep + e
        return pltpu.make_async_remote_copy(
            src_ref=part_ref.at[row], dst_ref=got.at[slot], send_sem=s1.at[row],
            recv_sem=r1.at[slot], device_id=target, device_id_type=MESH)

    for row in range(2 * rows):
        if row < rows:
            @pl.when(e != row)
            def _():
                first(row).start()

            @pl.when(e == row)
            def _():
                got[e] = part_ref[row]
        else:
            first(row).start()

    def spread(step):
        return pltpu.make_async_remote_copy(
            src_ref=block_ref, dst_ref=blocks.at[g], send_sem=s3.at[step],
            recv_sem=r3.at[g], device_id=(lax.rem(g + step, n_grp), e), device_id_type=MESH)

    def gathered(step):
        source = lax.rem(g + n_grp - step, n_grp)
        return pltpu.make_async_remote_copy(
            src_ref=block_ref, dst_ref=blocks.at[source], send_sem=s3.at[step],
            recv_sem=r3.at[source], device_id=(source, e), device_id_type=MESH)

    for step in range(1, n_grp):
        spread(step).start()
    blocks[g] = block_ref[...]

    def incoming(slot):
        return pltpu.make_async_remote_copy(
            src_ref=part_ref.at[0], dst_ref=got.at[slot], send_sem=s1.at[0],
            recv_sem=r1.at[slot], device_id=(g, 0), device_id_type=MESH)

    def second(target):
        return pltpu.make_async_remote_copy(
            src_ref=final.at[e], dst_ref=final.at[e], send_sem=s2.at[target],
            recv_sem=r2.at[e], device_id=(g, target), device_id_type=MESH)

    @pl.when(e < rows)
    def _():
        for slot in range(2 * n_ep):
            if slot < n_ep:
                @pl.when(e != slot)
                def _():
                    incoming(slot).wait_recv()
            else:
                incoming(slot).wait_recv()
        stack = got[...]
        own = own_ref[e]
        maxes = jnp.maximum(jnp.max(stack[:, :, HD:HD + 1], 0), own[:, HD:HD + 1])
        factors = jnp.exp(stack[:, :, HD:HD + 1] - maxes[None])
        own_factor = jnp.exp(own[:, HD:HD + 1] - maxes)
        total = jnp.sum(stack[:, :, HD + 1:HD + 2] * factors, 0) + own_factor
        accum = jnp.sum(stack[:, :, :HD] * factors, 0) + own[:, :HD] * own_factor
        final[e] = (accum / total).astype(final.dtype)
        for target in range(n_ep):
            @pl.when(e != target)
            def _():
                second(target).start()

    for row in range(2 * rows):
        if row < rows:
            @pl.when(e != row)
            def _():
                first(row).wait_send()
        else:
            first(row).wait_send()

    def arriving(row):
        return pltpu.make_async_remote_copy(
            src_ref=final.at[row], dst_ref=final.at[row], send_sem=s2.at[0],
            recv_sem=r2.at[row], device_id=(g, row), device_id_type=MESH)

    for row in range(rows):
        @pl.when(e != row)
        def _():
            arriving(row).wait_recv()

    @pl.when(e < rows)
    def _():
        for target in range(n_ep):
            @pl.when(e != target)
            def _():
                second(target).wait_send()

    for step in range(1, n_grp):
        spread(step).wait_send()
        gathered(step).wait_recv()
    out_ref[...] = final[...]
    columns_ref[...] = blocks[...]


def merge_call(part, own, block):
    rows = own.shape[0]
    heads = own.shape[1]
    n_ep = lax.axis_size("ep")
    n_grp = lax.axis_size("grp")
    gathered_shape = (n_grp,) + block.shape
    return pl.pallas_call(
        functools.partial(merge_kernel, rows, n_ep, n_grp),
        out_shape=(
            jax.ShapeDtypeStruct((rows, heads, HD), jnp.bfloat16),
            jax.ShapeDtypeStruct(gathered_shape, block.dtype),
        ),
        in_specs=[pl.BlockSpec(memory_space=pltpu.VMEM)] * 3,
        out_specs=(pl.BlockSpec(memory_space=pltpu.VMEM),) * 2,
        scratch_shapes=[
            pltpu.VMEM((2 * n_ep, heads, 128), jnp.float32),
            pltpu.VMEM((rows, heads, HD), jnp.bfloat16),
            pltpu.VMEM(gathered_shape, block.dtype),
            pltpu.SemaphoreType.DMA((2 * rows,)),
            pltpu.SemaphoreType.DMA((2 * n_ep,)),
            pltpu.SemaphoreType.DMA((n_ep,)),
            pltpu.SemaphoreType.DMA((rows,)),
            pltpu.SemaphoreType.DMA((n_grp,)),
            pltpu.SemaphoreType.DMA((n_grp,)),
        ],
        compiler_params=pltpu.CompilerParams(collective_id=0, has_side_effects=True),
    )(part, own, block)

norm_epsilon = 1e-05


def from_partner(block, axis, apart):
    count = lax.axis_size(axis)
    route = []
    for low in range(count):
        high = low | 1 << apart
        if high != low and high < count:
            route += [(low, high), (high, low)]
    return lax.ppermute(block, axis, route)


def expert_kernel(
    n_ep, n_grp, width, mixed_ref, gain_ref, picker_ref, combine_ref, up_ref, down_ref,
    out_ref, squares, outgoing, incoming, results, returned,
    s_sq, r_sq, s_out, r_in, s_res, r_ret,
):
    g = lax.axis_index("grp")
    e = lax.axis_index("ep")
    home = g // 2
    serving = home == e
    barrier = pltpu.get_barrier_semaphore()
    for peer in range(n_ep):
        @pl.when(e != peer)
        def _():
            pl.semaphore_signal(barrier, inc=1, device_id=(g, peer), device_id_type=MESH)
    for expert in range(n_grp):
        @pl.when(jnp.logical_not(serving & (g == expert)))
        def _():
            pl.semaphore_signal(barrier, inc=1, device_id=(expert, home), device_id_type=MESH)
    for half in range(2):
        for peer in range(n_ep):
            @pl.when(jnp.logical_not(serving & (g == 2 * e + half) & (e == peer)))
            def _():
                pl.semaphore_signal(
                    barrier, inc=1, device_id=(2 * e + half, peer), device_id_type=MESH
                )

    @pl.when(serving)
    def _():
        pl.semaphore_wait(barrier, n_ep - 1 + 2 * (2 * n_ep - 1))

    @pl.when(jnp.logical_not(serving))
    def _():
        pl.semaphore_wait(barrier, n_ep - 1 + 2 * 2 * n_ep)

    mixed = mixed_ref[...]
    own_sum = jnp.sum(mixed * mixed, axis=1, keepdims=True)
    squares[e] = jnp.broadcast_to(own_sum, squares.shape[1:])

    def sq_copy(peer):
        return pltpu.make_async_remote_copy(
            src_ref=squares.at[e], dst_ref=squares.at[e], send_sem=s_sq.at[peer],
            recv_sem=r_sq.at[e], device_id=(g, peer), device_id_type=MESH)

    def sq_arrival(peer):
        return pltpu.make_async_remote_copy(
            src_ref=squares.at[peer], dst_ref=squares.at[peer], send_sem=s_sq.at[peer],
            recv_sem=r_sq.at[peer], device_id=(g, peer), device_id_type=MESH)

    for peer in range(n_ep):
        @pl.when(e != peer)
        def _():
            sq_copy(peer).start()
    for peer in range(n_ep):
        @pl.when(e != peer)
        def _():
            sq_arrival(peer).wait_recv()
    total = jnp.sum(squares[...][:, :, 0:1], axis=0)
    normed = (mixed * lax.rsqrt(total / width + norm_epsilon) * gain_ref[...]).astype(jnp.bfloat16)
    slots = outgoing.shape[1]
    picked = jnp.dot(picker_ref[...], normed, preferred_element_type=jnp.float32)
    outgoing[...] = picked.reshape(outgoing.shape)

    def dispatch(expert):
        return pltpu.make_async_remote_copy(
            src_ref=outgoing.at[expert], dst_ref=incoming.at[e, g % 2], send_sem=s_out.at[expert],
            recv_sem=r_in.at[g % 2, e], device_id=(expert, home), device_id_type=MESH)

    for expert in range(n_grp):
        @pl.when(jnp.logical_not(serving & (g == expert)))
        def _():
            dispatch(expert).start()

    @pl.when(serving)
    def _():
        incoming[e, g % 2] = outgoing[g]

    def gathered(half, peer):
        return pltpu.make_async_remote_copy(
            src_ref=outgoing.at[0], dst_ref=incoming.at[peer, half], send_sem=s_out.at[0],
            recv_sem=r_in.at[half, peer], device_id=(2 * e + half, peer), device_id_type=MESH)

    for half in range(2):
        for peer in range(n_ep):
            @pl.when(jnp.logical_not(serving & (g == 2 * e + half) & (e == peer)))
            def _():
                gathered(half, peer).wait_recv()

    pre = jnp.zeros((2 * slots, up_ref.shape[1]), jnp.float32)
    for peer in range(n_ep):
        lhs = incoming[peer].reshape(2 * slots, width // n_ep).astype(jnp.bfloat16)
        pre = pre + jnp.dot(
            lhs, up_ref[peer * (width // n_ep):(peer + 1) * (width // n_ep), :],
            preferred_element_type=jnp.float32)
    hidden_units = up_ref.shape[1] // 2
    gate = pre[:, :hidden_units]
    act = (gate / (1.0 + jnp.exp(-gate)) * pre[:, hidden_units:]).astype(jnp.bfloat16)
    for peer in range(n_ep):
        piece = jnp.dot(act, down_ref[peer], preferred_element_type=jnp.float32)
        results[peer] = piece.astype(jnp.bfloat16).astype(jnp.float32).reshape(results.shape[1:])

    def give_back(half, peer):
        return pltpu.make_async_remote_copy(
            src_ref=results.at[peer, half], dst_ref=returned.at[g], send_sem=s_res.at[half, peer],
            recv_sem=r_ret.at[g], device_id=(2 * e + half, peer), device_id_type=MESH)

    for half in range(2):
        for peer in range(n_ep):
            @pl.when(jnp.logical_not(serving & (g == 2 * e + half) & (e == peer)))
            def _():
                give_back(half, peer).start()

    @pl.when(serving)
    def _():
        returned[g] = results[e, g % 2]

    def coming_back(expert):
        return pltpu.make_async_remote_copy(
            src_ref=results.at[0, 0], dst_ref=returned.at[expert], send_sem=s_res.at[0, 0],
            recv_sem=r_ret.at[expert], device_id=(expert, home), device_id_type=MESH)

    for expert in range(n_grp):
        @pl.when(jnp.logical_not(serving & (g == expert)))
        def _():
            coming_back(expert).wait_recv()

    back = returned[...].reshape(n_grp * slots, width // n_ep).astype(jnp.bfloat16)
    mix = jnp.dot(combine_ref[...], back, preferred_element_type=jnp.float32)
    out_ref[...] = (mixed + mix).astype(out_ref.dtype)

    for peer in range(n_ep):
        @pl.when(e != peer)
        def _():
            sq_copy(peer).wait_send()
    for expert in range(n_grp):
        @pl.when(jnp.logical_not(serving & (g == expert)))
        def _():
            dispatch(expert).wait_send()
    for half in range(2):
        for peer in range(n_ep):
            @pl.when(jnp.logical_not(serving & (g == 2 * e + half) & (e == peer)))
            def _():
                give_back(half, peer).wait_send()


def expert_call(mixed, gain, picker, combine, up, down_parts):
    n_ep = lax.axis_size("ep")
    n_grp = lax.axis_size("grp")
    rows, share = mixed.shape
    slots = picker.shape[0] // n_grp
    width = share * n_ep
    return pl.pallas_call(
        functools.partial(expert_kernel, n_ep, n_grp, width),
        out_shape=jax.ShapeDtypeStruct((rows, share), jnp.bfloat16),
        in_specs=[pl.BlockSpec(memory_space=pltpu.VMEM)] * 6,
        out_specs=pl.BlockSpec(memory_space=pltpu.VMEM),
        scratch_shapes=[
            pltpu.VMEM((n_ep, rows, 128), jnp.float32),
            pltpu.VMEM((n_grp, slots, share), jnp.float32),
            pltpu.VMEM((n_ep, 2, slots, share), jnp.float32),
            pltpu.VMEM((n_ep, 2, slots, share), jnp.float32),
            pltpu.VMEM((n_grp, slots, share), jnp.float32),
            pltpu.SemaphoreType.DMA((n_ep,)),
            pltpu.SemaphoreType.DMA((n_ep,)),
            pltpu.SemaphoreType.DMA((n_grp,)),
            pltpu.SemaphoreType.DMA((2, n_ep)),
            pltpu.SemaphoreType.DMA((2, n_ep)),
            pltpu.SemaphoreType.DMA((n_grp,)),
        ],
        compiler_params=pltpu.CompilerParams(collective_id=1, has_side_effects=True),
    )(mixed, gain, picker, combine, up, down_parts)


def per_device(
    hidden,
    query,
    new_kv,
    key_cache,
    value_cache,
    page_owner,
    page_fill,
    out_weight,
    norm_gain,
    gate_up,
    down,
    routes,
    route_weight,
):
    row_count = query.shape[0]
    group_count = lax.axis_size("grp")
    head_group = HEADS // KV_HEADS
    page_count = page_owner.shape[0]
    token_count = key_cache.shape[0]
    page_length = token_count // page_count
    both_rows = 2 * row_count
    scale = HD ** (-0.5)
    partner_query = from_partner(query, "grp", 0)
    all_queries = jnp.concatenate([query, partner_query], 0)
    query_heads = (
        all_queries.reshape(both_rows, KV_HEADS, head_group, HD)
        .transpose(1, 0, 2, 3)
        .reshape(KV_HEADS, both_rows * head_group, HD)
    )
    key_heads = key_cache.reshape(token_count, KV_HEADS, HD)
    value_heads = value_cache.reshape(token_count, KV_HEADS, HD)
    scores = (
        jnp.einsum("kqd,tkd->kqt", query_heads, key_heads, preferred_element_type=jnp.float32)
        * scale
    )
    scores = scores.reshape(KV_HEADS, both_rows, head_group, token_count)
    row_index = jnp.arange(both_rows, dtype=jnp.int32)
    in_page = jnp.arange(page_length, dtype=jnp.int32)
    usable = (page_owner[None, :, None] == row_index[:, None, None]) & (
        in_page[None, None, :] < page_fill[None, :, None]
    )
    usable = usable.reshape(both_rows, token_count)[None, :, None, :]
    local_top = jnp.max(jnp.where(usable, scores, masked_score), -1)
    weights = jnp.where(usable, jnp.exp(scores - local_top[..., None]), 0.0)
    local_total = jnp.sum(weights, -1)
    rounded = weights.astype(jnp.bfloat16).reshape(KV_HEADS, both_rows * head_group, token_count)
    local_accum = jnp.einsum(
        "kqt,tkd->kqd", rounded, value_heads, preferred_element_type=jnp.float32
    )
    part_max = local_top.transpose(1, 0, 2).reshape(both_rows, HEADS)
    part_total = local_total.transpose(1, 0, 2).reshape(both_rows, HEADS)
    part_accum = (
        local_accum.reshape(KV_HEADS, both_rows, head_group, HD)
        .transpose(1, 0, 2, 3)
        .reshape(both_rows, HEADS, HD)
    )
    own_query = query.reshape(row_count, KV_HEADS, head_group, HD)
    fresh_key = new_kv[:, 0].reshape(row_count, KV_HEADS, HD)
    fresh_value = new_kv[:, 1].astype(jnp.float32).reshape(row_count, KV_HEADS, HD)
    own_score = (
        jnp.einsum(
            "rkgd,rkd->rkg", own_query, fresh_key, preferred_element_type=jnp.float32
        ).reshape(row_count, HEADS)
        * scale
    )
    value_rows = jnp.broadcast_to(
        fresh_value[:, :, None, :], (row_count, KV_HEADS, head_group, HD)
    ).reshape(row_count, HEADS, HD)
    pad = jnp.zeros((both_rows, HEADS, 128 - HD - 2), jnp.float32)
    packed = jnp.concatenate(
        [part_accum, part_max[..., None], part_total[..., None], pad], -1
    )
    own_packed = jnp.concatenate(
        [value_rows, own_score[..., None], jnp.ones_like(own_score)[..., None], pad[:row_count]], -1
    )
    merged, weight_blocks = merge_call(packed, own_packed, out_weight)
    attn_out = merged.reshape(row_count, HEADS * HD)
    weight_columns = weight_blocks.reshape(-1, out_weight.shape[1])
    projected = jnp.dot(attn_out, weight_columns, preferred_element_type=jnp.float32)
    feature_share = hidden.shape[1]
    mixed = hidden.astype(jnp.float32) + projected
    expert_ids = jnp.arange(group_count, dtype=jnp.int32)
    named = routes[:, :, None] == expert_ids[None, None, :]
    chosen = jnp.any(named, 1).astype(jnp.int32)
    weight_at = jnp.sum(
        jnp.where(named, route_weight.astype(jnp.float32)[:, :, None], 0.0), 1
    )
    position = jnp.cumsum(chosen, 0) - chosen
    slot_ids = jnp.arange(row_count, dtype=jnp.int32)
    placed = (chosen[:, :, None] == 1) & (position[:, :, None] == slot_ids[None, None, :])
    picker = (
        placed.transpose(1, 2, 0).reshape(group_count * row_count, row_count).astype(jnp.bfloat16)
    )
    combine = (
        jnp.where(placed, weight_at[:, :, None], 0.0)
        .reshape(row_count, group_count * row_count)
        .astype(jnp.bfloat16)
    )
    down_parts = (
        down[0].reshape(FF, lax.axis_size("ep"), feature_share).transpose(1, 0, 2)
    )
    layer_out = expert_call(
        mixed, norm_gain.reshape(1, feature_share), picker, combine, gate_up[0], down_parts
    )
    return (layer_out, attn_out)


def solution(mesh):
    placed = (
        P("grp", "ep"),
        P("grp", None),
        P("grp", None, None),
        P(("grp", "ep"), None),
        P(("grp", "ep"), None),
        P(("grp", "ep")),
        P(("grp", "ep")),
        P("grp", "ep"),
        P("ep"),
        P("grp", None, None),
        P("grp", None, None),
        P("grp", None),
        P("grp", None),
    )
    return jax.shard_map(
        per_device,
        mesh=mesh,
        in_specs=placed,
        out_specs=(P("grp", "ep"), P("grp", None)),
        check_vma=False,
    )
```

```python
import jax
import jax.numpy as jnp
from jax import lax
from jax.experimental import pallas as pl
from jax.experimental.pallas import tpu as pltpu
from jax.sharding import PartitionSpec as P
import functools

D = 1536
HEADS = 24
KV_HEADS = 8
HD = 64
FF = 512
TOP = 8


masked_score = -1e30
norm_epsilon = 1e-05

MESH = pl.DeviceIdType.MESH


def layer_kernel(
    rows, n_ep, n_grp, width,
    part_ref, own_ref, block_ref, hidden_ref, gain_ref, picker_ref, combine_ref, up_ref, down_ref,
    out_ref, attn_ref,
    got, final, blocks, squares, outgoing, incoming, results, returned,
    s1, r1, s2, r2, s3, r3, s_sq, r_sq, s_out, r_in, s_res, r_ret,
):
    g = lax.axis_index("grp")
    e = lax.axis_index("ep")
    mate = g + 1 - 2 * (g % 2)
    home = g // 2
    serving = home == e
    share = width // n_ep
    barrier = pltpu.get_barrier_semaphore()
    for peer in range(n_ep):
        @pl.when(e != peer)
        def _():
            pl.semaphore_signal(barrier, inc=1, device_id=(g, peer), device_id_type=MESH)
            pl.semaphore_signal(barrier, inc=1, device_id=(g, peer), device_id_type=MESH)
        pl.semaphore_signal(barrier, inc=1, device_id=(mate, peer), device_id_type=MESH)
    for step in range(1, n_grp):
        pl.semaphore_signal(
            barrier, inc=1, device_id=(lax.rem(g + step, n_grp), e), device_id_type=MESH
        )
    for expert in range(n_grp):
        @pl.when(jnp.logical_not(serving & (g == expert)))
        def _():
            pl.semaphore_signal(barrier, inc=1, device_id=(expert, home), device_id_type=MESH)
    for half in range(2):
        for peer in range(n_ep):
            @pl.when(jnp.logical_not(serving & (g == 2 * e + half) & (e == peer)))
            def _():
                pl.semaphore_signal(
                    barrier, inc=1, device_id=(2 * e + half, peer), device_id_type=MESH
                )
    common = 2 * (n_ep - 1) + n_ep + n_grp - 1

    @pl.when(serving)
    def _():
        pl.semaphore_wait(barrier, common + n_grp - 1 + 2 * n_ep - 1)

    @pl.when(jnp.logical_not(serving))
    def _():
        pl.semaphore_wait(barrier, common + n_grp + 2 * n_ep)

    def first(row):
        if row < rows:
            target = (g, row)
            slot = e
        else:
            target = (mate, row - rows)
            slot = n_ep + e
        return pltpu.make_async_remote_copy(
            src_ref=part_ref.at[row], dst_ref=got.at[slot], send_sem=s1.at[row],
            recv_sem=r1.at[slot], device_id=target, device_id_type=MESH)

    for row in range(2 * rows):
        if row < rows:
            @pl.when(e != row)
            def _():
                first(row).start()

            @pl.when(e == row)
            def _():
                got[e] = part_ref[row]
        else:
            first(row).start()

    def spread(step):
        return pltpu.make_async_remote_copy(
            src_ref=block_ref, dst_ref=blocks.at[g], send_sem=s3.at[step],
            recv_sem=r3.at[g], device_id=(lax.rem(g + step, n_grp), e), device_id_type=MESH)

    def gathered_block(step):
        source = lax.rem(g + n_grp - step, n_grp)
        return pltpu.make_async_remote_copy(
            src_ref=block_ref, dst_ref=blocks.at[source], send_sem=s3.at[step],
            recv_sem=r3.at[source], device_id=(source, e), device_id_type=MESH)

    for step in range(1, n_grp):
        spread(step).start()
    blocks[g] = block_ref[...]

    def incoming_part(slot):
        return pltpu.make_async_remote_copy(
            src_ref=part_ref.at[0], dst_ref=got.at[slot], send_sem=s1.at[0],
            recv_sem=r1.at[slot], device_id=(g, 0), device_id_type=MESH)

    def second(target):
        return pltpu.make_async_remote_copy(
            src_ref=final.at[e], dst_ref=final.at[e], send_sem=s2.at[target],
            recv_sem=r2.at[e], device_id=(g, target), device_id_type=MESH)

    @pl.when(e < rows)
    def _():
        for slot in range(2 * n_ep):
            if slot < n_ep:
                @pl.when(e != slot)
                def _():
                    incoming_part(slot).wait_recv()
            else:
                incoming_part(slot).wait_recv()
        stack = got[...]
        own = own_ref[e]
        maxes = jnp.maximum(jnp.max(stack[:, 1:2, :], 0), own[1:2, :])
        factors = jnp.exp(stack[:, 1:2, :] - maxes[None])
        own_factor = jnp.exp(own[1:2, :] - maxes)
        total = jnp.sum(stack[:, 2:3, :] * factors, 0) + own_factor
        accum = jnp.sum(stack[:, 0:1, :] * factors, 0) + own[0:1, :] * own_factor
        final[e] = (accum / total).astype(jnp.bfloat16).astype(jnp.float32)
        for target in range(n_ep):
            @pl.when(e != target)
            def _():
                second(target).start()

    def arriving(row):
        return pltpu.make_async_remote_copy(
            src_ref=final.at[row], dst_ref=final.at[row], send_sem=s2.at[0],
            recv_sem=r2.at[row], device_id=(g, row), device_id_type=MESH)

    for row in range(rows):
        @pl.when(e != row)
        def _():
            arriving(row).wait_recv()

    row_ids = lax.broadcasted_iota(jnp.int32, (rows, width), 0)
    attn = jnp.zeros((rows, width), jnp.float32)
    for row in range(rows):
        attn = jnp.where(row_ids == row, jnp.broadcast_to(final[row], (rows, width)), attn)
    attn = attn.astype(jnp.bfloat16)
    attn_ref[...] = attn

    for step in range(1, n_grp):
        gathered_block(step).wait_recv()
    columns = blocks[...].reshape(n_grp * blocks.shape[1], share)
    projected = jnp.dot(attn, columns, preferred_element_type=jnp.float32)
    mixed = hidden_ref[...].astype(jnp.float32) + projected

    own_sum = jnp.sum(mixed * mixed, axis=1, keepdims=True)
    squares[e] = jnp.broadcast_to(own_sum, squares.shape[1:])

    def sq_copy(peer):
        return pltpu.make_async_remote_copy(
            src_ref=squares.at[e], dst_ref=squares.at[e], send_sem=s_sq.at[peer],
            recv_sem=r_sq.at[e], device_id=(g, peer), device_id_type=MESH)

    def sq_arrival(peer):
        return pltpu.make_async_remote_copy(
            src_ref=squares.at[peer], dst_ref=squares.at[peer], send_sem=s_sq.at[peer],
            recv_sem=r_sq.at[peer], device_id=(g, peer), device_id_type=MESH)

    for peer in range(n_ep):
        @pl.when(e != peer)
        def _():
            sq_copy(peer).start()
    for peer in range(n_ep):
        @pl.when(e != peer)
        def _():
            sq_arrival(peer).wait_recv()
    total_sq = jnp.sum(squares[...][:, :, 0:1], axis=0)
    normed = (mixed * lax.rsqrt(total_sq / width + norm_epsilon) * gain_ref[...]).astype(jnp.bfloat16)
    slots = outgoing.shape[1]
    picked = jnp.dot(picker_ref[...], normed, preferred_element_type=jnp.float32)
    outgoing[...] = picked.reshape(outgoing.shape)

    def dispatch(expert):
        return pltpu.make_async_remote_copy(
            src_ref=outgoing.at[expert], dst_ref=incoming.at[e, g % 2], send_sem=s_out.at[expert],
            recv_sem=r_in.at[g % 2, e], device_id=(expert, home), device_id_type=MESH)

    for expert in range(n_grp):
        @pl.when(jnp.logical_not(serving & (g == expert)))
        def _():
            dispatch(expert).start()

    @pl.when(serving)
    def _():
        incoming[e, g % 2] = outgoing[g]

    def gathered(half, peer):
        return pltpu.make_async_remote_copy(
            src_ref=outgoing.at[0], dst_ref=incoming.at[peer, half], send_sem=s_out.at[0],
            recv_sem=r_in.at[half, peer], device_id=(2 * e + half, peer), device_id_type=MESH)

    for half in range(2):
        for peer in range(n_ep):
            @pl.when(jnp.logical_not(serving & (g == 2 * e + half) & (e == peer)))
            def _():
                gathered(half, peer).wait_recv()

    pre = jnp.zeros((2 * slots, up_ref.shape[1]), jnp.float32)
    for peer in range(n_ep):
        lhs = incoming[peer].reshape(2 * slots, share).astype(jnp.bfloat16)
        pre = pre + jnp.dot(
            lhs, up_ref[peer * share:(peer + 1) * share, :], preferred_element_type=jnp.float32)
    hidden_units = up_ref.shape[1] // 2
    gate = pre[:, :hidden_units]
    act = (gate / (1.0 + jnp.exp(-gate)) * pre[:, hidden_units:]).astype(jnp.bfloat16)
    for peer in range(n_ep):
        piece = jnp.dot(act, down_ref[peer], preferred_element_type=jnp.float32)
        results[peer] = piece.astype(jnp.bfloat16).astype(jnp.float32).reshape(results.shape[1:])

    def give_back(half, peer):
        return pltpu.make_async_remote_copy(
            src_ref=results.at[peer, half], dst_ref=returned.at[g], send_sem=s_res.at[half, peer],
            recv_sem=r_ret.at[g], device_id=(2 * e + half, peer), device_id_type=MESH)

    for half in range(2):
        for peer in range(n_ep):
            @pl.when(jnp.logical_not(serving & (g == 2 * e + half) & (e == peer)))
            def _():
                give_back(half, peer).start()

    @pl.when(serving)
    def _():
        returned[g] = results[e, g % 2]

    def coming_back(expert):
        return pltpu.make_async_remote_copy(
            src_ref=results.at[0, 0], dst_ref=returned.at[expert], send_sem=s_res.at[0, 0],
            recv_sem=r_ret.at[expert], device_id=(expert, home), device_id_type=MESH)

    for expert in range(n_grp):
        @pl.when(jnp.logical_not(serving & (g == expert)))
        def _():
            coming_back(expert).wait_recv()

    back = returned[...].reshape(n_grp * slots, share).astype(jnp.bfloat16)
    mix = jnp.dot(combine_ref[...], back, preferred_element_type=jnp.float32)
    out_ref[...] = (mixed + mix).astype(out_ref.dtype)

    for row in range(2 * rows):
        if row < rows:
            @pl.when(e != row)
            def _():
                first(row).wait_send()
        else:
            first(row).wait_send()

    @pl.when(e < rows)
    def _():
        for target in range(n_ep):
            @pl.when(e != target)
            def _():
                second(target).wait_send()

    for step in range(1, n_grp):
        spread(step).wait_send()
    for peer in range(n_ep):
        @pl.when(e != peer)
        def _():
            sq_copy(peer).wait_send()
    for expert in range(n_grp):
        @pl.when(jnp.logical_not(serving & (g == expert)))
        def _():
            dispatch(expert).wait_send()
    for half in range(2):
        for peer in range(n_ep):
            @pl.when(jnp.logical_not(serving & (g == 2 * e + half) & (e == peer)))
            def _():
                give_back(half, peer).wait_send()


def layer_call(part, own, block, hidden, gain, picker, combine, up, down_parts):
    n_ep = lax.axis_size("ep")
    n_grp = lax.axis_size("grp")
    rows, share = hidden.shape
    width = share * n_ep
    slots = picker.shape[0] // n_grp
    return pl.pallas_call(
        functools.partial(layer_kernel, rows, n_ep, n_grp, width),
        out_shape=(
            jax.ShapeDtypeStruct((rows, share), jnp.bfloat16),
            jax.ShapeDtypeStruct((rows, width), jnp.bfloat16),
        ),
        in_specs=[pl.BlockSpec(memory_space=pltpu.VMEM)] * 9,
        out_specs=(pl.BlockSpec(memory_space=pltpu.VMEM),) * 2,
        scratch_shapes=[
            pltpu.VMEM((2 * n_ep,) + part.shape[1:], jnp.float32),
            pltpu.VMEM((rows, 1, width), jnp.float32),
            pltpu.VMEM((n_grp,) + block.shape, block.dtype),
            pltpu.VMEM((n_ep, rows, 128), jnp.float32),
            pltpu.VMEM((n_grp, slots, share), jnp.float32),
            pltpu.VMEM((n_ep, 2, slots, share), jnp.float32),
            pltpu.VMEM((n_ep, 2, slots, share), jnp.float32),
            pltpu.VMEM((n_grp, slots, share), jnp.float32),
            pltpu.SemaphoreType.DMA((2 * rows,)),
            pltpu.SemaphoreType.DMA((2 * n_ep,)),
            pltpu.SemaphoreType.DMA((n_ep,)),
            pltpu.SemaphoreType.DMA((rows,)),
            pltpu.SemaphoreType.DMA((n_grp,)),
            pltpu.SemaphoreType.DMA((n_grp,)),
            pltpu.SemaphoreType.DMA((n_ep,)),
            pltpu.SemaphoreType.DMA((n_ep,)),
            pltpu.SemaphoreType.DMA((n_grp,)),
            pltpu.SemaphoreType.DMA((2, n_ep)),
            pltpu.SemaphoreType.DMA((2, n_ep)),
            pltpu.SemaphoreType.DMA((n_grp,)),
        ],
        compiler_params=pltpu.CompilerParams(collective_id=0, has_side_effects=True),
    )(part, own, block, hidden, gain, picker, combine, up, down_parts)


def from_partner(block, axis, apart):
    count = lax.axis_size(axis)
    route = []
    for low in range(count):
        high = low | 1 << apart
        if high != low and high < count:
            route += [(low, high), (high, low)]
    return lax.ppermute(block, axis, route)


def per_device(
    hidden,
    query,
    new_kv,
    key_cache,
    value_cache,
    page_owner,
    page_fill,
    out_weight,
    norm_gain,
    gate_up,
    down,
    routes,
    route_weight,
):
    row_count = query.shape[0]
    group_count = lax.axis_size("grp")
    head_group = HEADS // KV_HEADS
    page_count = page_owner.shape[0]
    token_count = key_cache.shape[0]
    page_length = token_count // page_count
    both_rows = 2 * row_count
    scale = HD ** (-0.5)
    partner_query = from_partner(query, "grp", 0)
    all_queries = jnp.concatenate([query, partner_query], 0)
    query_heads = (
        all_queries.reshape(both_rows, KV_HEADS, head_group, HD)
        .transpose(1, 0, 2, 3)
        .reshape(KV_HEADS, both_rows * head_group, HD)
    )
    key_heads = key_cache.reshape(token_count, KV_HEADS, HD)
    value_heads = value_cache.reshape(token_count, KV_HEADS, HD)
    scores = (
        jnp.einsum("kqd,tkd->kqt", query_heads, key_heads, preferred_element_type=jnp.float32)
        * scale
    )
    scores = scores.reshape(KV_HEADS, both_rows, head_group, token_count)
    row_index = jnp.arange(both_rows, dtype=jnp.int32)
    in_page = jnp.arange(page_length, dtype=jnp.int32)
    usable = (page_owner[None, :, None] == row_index[:, None, None]) & (
        in_page[None, None, :] < page_fill[None, :, None]
    )
    usable = usable.reshape(both_rows, token_count)[None, :, None, :]
    local_top = jnp.max(jnp.where(usable, scores, masked_score), -1)
    weights = jnp.where(usable, jnp.exp(scores - local_top[..., None]), 0.0)
    local_total = jnp.sum(weights, -1)
    rounded = weights.astype(jnp.bfloat16).reshape(KV_HEADS, both_rows * head_group, token_count)
    local_accum = jnp.einsum(
        "kqt,tkd->kqd", rounded, value_heads, preferred_element_type=jnp.float32
    )
    part_max = local_top.transpose(1, 0, 2).reshape(both_rows, HEADS)
    part_total = local_total.transpose(1, 0, 2).reshape(both_rows, HEADS)
    part_accum = (
        local_accum.reshape(KV_HEADS, both_rows, head_group, HD)
        .transpose(1, 0, 2, 3)
        .reshape(both_rows, HEADS, HD)
    )
    own_query = query.reshape(row_count, KV_HEADS, head_group, HD)
    fresh_key = new_kv[:, 0].reshape(row_count, KV_HEADS, HD)
    fresh_value = new_kv[:, 1].astype(jnp.float32).reshape(row_count, KV_HEADS, HD)
    own_score = (
        jnp.einsum(
            "rkgd,rkd->rkg", own_query, fresh_key, preferred_element_type=jnp.float32
        ).reshape(row_count, HEADS)
        * scale
    )
    value_rows = jnp.broadcast_to(
        fresh_value[:, :, None, :], (row_count, KV_HEADS, head_group, HD)
    ).reshape(row_count, HEADS, HD)
    width = HEADS * HD
    packed = jnp.stack(
        [
            part_accum.reshape(both_rows, width),
            jnp.broadcast_to(part_max[..., None], part_accum.shape).reshape(both_rows, width),
            jnp.broadcast_to(part_total[..., None], part_accum.shape).reshape(both_rows, width),
        ],
        1,
    )
    own_packed = jnp.stack(
        [
            value_rows.reshape(row_count, width),
            jnp.broadcast_to(own_score[..., None], value_rows.shape).reshape(row_count, width),
            jnp.ones((row_count, width), jnp.float32),
        ],
        1,
    )
    feature_share = hidden.shape[1]
    expert_ids = jnp.arange(group_count, dtype=jnp.int32)
    named = routes[:, :, None] == expert_ids[None, None, :]
    chosen = jnp.any(named, 1).astype(jnp.int32)
    weight_at = jnp.sum(
        jnp.where(named, route_weight.astype(jnp.float32)[:, :, None], 0.0), 1
    )
    position = jnp.cumsum(chosen, 0) - chosen
    slot_ids = jnp.arange(row_count, dtype=jnp.int32)
    placed = (chosen[:, :, None] == 1) & (position[:, :, None] == slot_ids[None, None, :])
    picker = (
        placed.transpose(1, 2, 0).reshape(group_count * row_count, row_count).astype(jnp.bfloat16)
    )
    combine = (
        jnp.where(placed, weight_at[:, :, None], 0.0)
        .reshape(row_count, group_count * row_count)
        .astype(jnp.bfloat16)
    )
    down_parts = (
        down[0].reshape(FF, lax.axis_size("ep"), feature_share).transpose(1, 0, 2)
    )
    layer_out, attn_out = layer_call(
        packed, own_packed, out_weight, hidden, norm_gain.reshape(1, feature_share),
        picker, combine, gate_up[0], down_parts,
    )
    return (layer_out, attn_out)


def solution(mesh):
    placed = (
        P("grp", "ep"),
        P("grp", None),
        P("grp", None, None),
        P(("grp", "ep"), None),
        P(("grp", "ep"), None),
        P(("grp", "ep")),
        P(("grp", "ep")),
        P("grp", "ep"),
        P("ep"),
        P("grp", None, None),
        P("grp", None, None),
        P("grp", None),
        P("grp", None),
    )
    return jax.shard_map(
        per_device,
        mesh=mesh,
        in_specs=placed,
        out_specs=(P("grp", "ep"), P("grp", None)),
        check_vma=False,
    )
```

```python
import jax
import jax.numpy as jnp
from jax import lax
from jax.experimental import pallas as pl
from jax.experimental.pallas import tpu as pltpu
from jax.sharding import PartitionSpec as P
import functools

D = 1536
HEADS = 24
KV_HEADS = 8
HD = 64
FF = 512
TOP = 8


masked_score = -1e30
norm_epsilon = 1e-05

MESH = pl.DeviceIdType.MESH


def layer_kernel(
    rows, n_ep, n_grp, width,
    query_ref, mate_query_ref, key_ref, value_ref, owner_ref, fill_ref,
    own_ref, block_ref, hidden_ref, gain_ref, picker_ref, combine_ref, up_ref, down_ref,
    out_ref, attn_ref,
    part_ref, got, final, blocks, squares, outgoing, incoming, results, returned,
    s1, r1, s2, r2, s3, r3, s_sq, r_sq, s_out, r_in, s_res, r_ret,
):
    g = lax.axis_index("grp")
    e = lax.axis_index("ep")
    mate = g + 1 - 2 * (g % 2)
    home = g // 2
    serving = home == e
    share = width // n_ep
    barrier = pltpu.get_barrier_semaphore()
    for peer in range(n_ep):
        @pl.when(e != peer)
        def _():
            pl.semaphore_signal(barrier, inc=1, device_id=(g, peer), device_id_type=MESH)
            pl.semaphore_signal(barrier, inc=1, device_id=(g, peer), device_id_type=MESH)
        pl.semaphore_signal(barrier, inc=1, device_id=(mate, peer), device_id_type=MESH)
    for step in range(1, n_grp):
        pl.semaphore_signal(
            barrier, inc=1, device_id=(lax.rem(g + step, n_grp), e), device_id_type=MESH
        )
    for expert in range(n_grp):
        @pl.when(jnp.logical_not(serving & (g == expert)))
        def _():
            pl.semaphore_signal(barrier, inc=1, device_id=(expert, home), device_id_type=MESH)
    for half in range(2):
        for peer in range(n_ep):
            @pl.when(jnp.logical_not(serving & (g == 2 * e + half) & (e == peer)))
            def _():
                pl.semaphore_signal(
                    barrier, inc=1, device_id=(2 * e + half, peer), device_id_type=MESH
                )
    common = 2 * (n_ep - 1) + n_ep + n_grp - 1

    heads = width // HD
    both = 2 * rows
    pages = owner_ref.shape[1]
    tokens = key_ref.shape[0]
    page_length = tokens // pages
    queries = jnp.concatenate([query_ref[...], mate_query_ref[...]], 0)
    lane_head = lax.broadcasted_iota(jnp.int32, (both, width), 1) // HD
    stacked = jnp.concatenate(
        [jnp.where(lane_head == h, queries, jnp.zeros_like(queries)) for h in range(heads)], 0
    )
    row_of = lax.broadcasted_iota(jnp.int32, (both, pages), 0)
    owns = (owner_ref[...] == row_of).astype(jnp.float32)
    token_of = lax.broadcasted_iota(jnp.int32, (tokens, pages), 0)
    page_of = lax.broadcasted_iota(jnp.int32, (tokens, pages), 1)
    filled = (
        (token_of // page_length == page_of) & (token_of % page_length < fill_ref[...])
    ).astype(jnp.float32)
    usable = lax.dot_general(
        owns, filled, (((1,), (1,)), ((), ())), preferred_element_type=jnp.float32
    ) > 0.5
    usable = jnp.concatenate([usable] * heads, 0)
    scores = lax.dot_general(
        stacked, key_ref[...], (((1,), (1,)), ((), ())), preferred_element_type=jnp.float32
    ) * (HD ** -0.5)
    local_top = jnp.max(jnp.where(usable, scores, masked_score), 1, keepdims=True)
    weights = jnp.where(usable, jnp.exp(scores - local_top), 0.0)
    local_total = jnp.sum(weights, 1, keepdims=True)
    local_accum = jnp.dot(
        weights.astype(jnp.bfloat16), value_ref[...], preferred_element_type=jnp.float32
    )
    accum_rows = jnp.zeros((both, width), jnp.float32)
    top_rows = jnp.zeros((both, width), jnp.float32)
    total_rows = jnp.zeros((both, width), jnp.float32)
    for h in range(heads):
        mine = lane_head == h
        block = slice(h * both, (h + 1) * both)
        accum_rows = jnp.where(mine, local_accum[block], accum_rows)
        top_rows = jnp.where(mine, jnp.broadcast_to(local_top[block], (both, width)), top_rows)
        total_rows = jnp.where(mine, jnp.broadcast_to(local_total[block], (both, width)), total_rows)
    for row in range(both):
        part_ref[row, 0:1, :] = accum_rows[row:row + 1]
        part_ref[row, 1:2, :] = top_rows[row:row + 1]
        part_ref[row, 2:3, :] = total_rows[row:row + 1]

    @pl.when(serving)
    def _():
        pl.semaphore_wait(barrier, common + n_grp - 1 + 2 * n_ep - 1)

    @pl.when(jnp.logical_not(serving))
    def _():
        pl.semaphore_wait(barrier, common + n_grp + 2 * n_ep)

    def first(row):
        if row < rows:
            target = (g, row)
            slot = e
        else:
            target = (mate, row - rows)
            slot = n_ep + e
        return pltpu.make_async_remote_copy(
            src_ref=part_ref.at[row], dst_ref=got.at[slot], send_sem=s1.at[row],
            recv_sem=r1.at[slot], device_id=target, device_id_type=MESH)

    for row in range(2 * rows):
        if row < rows:
            @pl.when(e != row)
            def _():
                first(row).start()

            @pl.when(e == row)
            def _():
                got[e] = part_ref[row]
        else:
            first(row).start()

    def spread(step):
        return pltpu.make_async_remote_copy(
            src_ref=block_ref, dst_ref=blocks.at[g], send_sem=s3.at[step],
            recv_sem=r3.at[g], device_id=(lax.rem(g + step, n_grp), e), device_id_type=MESH)

    def gathered_block(step):
        source = lax.rem(g + n_grp - step, n_grp)
        return pltpu.make_async_remote_copy(
            src_ref=block_ref, dst_ref=blocks.at[source], send_sem=s3.at[step],
            recv_sem=r3.at[source], device_id=(source, e), device_id_type=MESH)

    for step in range(1, n_grp):
        spread(step).start()
    blocks[g] = block_ref[...]

    def incoming_part(slot):
        return pltpu.make_async_remote_copy(
            src_ref=part_ref.at[0], dst_ref=got.at[slot], send_sem=s1.at[0],
            recv_sem=r1.at[slot], device_id=(g, 0), device_id_type=MESH)

    def second(target):
        return pltpu.make_async_remote_copy(
            src_ref=final.at[e], dst_ref=final.at[e], send_sem=s2.at[target],
            recv_sem=r2.at[e], device_id=(g, target), device_id_type=MESH)

    @pl.when(e < rows)
    def _():
        for slot in range(2 * n_ep):
            if slot < n_ep:
                @pl.when(e != slot)
                def _():
                    incoming_part(slot).wait_recv()
            else:
                incoming_part(slot).wait_recv()
        stack = got[...]
        own = own_ref[e]
        maxes = jnp.maximum(jnp.max(stack[:, 1:2, :], 0), own[1:2, :])
        factors = jnp.exp(stack[:, 1:2, :] - maxes[None])
        own_factor = jnp.exp(own[1:2, :] - maxes)
        total = jnp.sum(stack[:, 2:3, :] * factors, 0) + own_factor
        accum = jnp.sum(stack[:, 0:1, :] * factors, 0) + own[0:1, :] * own_factor
        final[e] = (accum / total).astype(jnp.bfloat16).astype(jnp.float32)
        for target in range(n_ep):
            @pl.when(e != target)
            def _():
                second(target).start()

    def arriving(row):
        return pltpu.make_async_remote_copy(
            src_ref=final.at[row], dst_ref=final.at[row], send_sem=s2.at[0],
            recv_sem=r2.at[row], device_id=(g, row), device_id_type=MESH)

    for row in range(rows):
        @pl.when(e != row)
        def _():
            arriving(row).wait_recv()

    row_ids = lax.broadcasted_iota(jnp.int32, (rows, width), 0)
    attn = jnp.zeros((rows, width), jnp.float32)
    for row in range(rows):
        attn = jnp.where(row_ids == row, jnp.broadcast_to(final[row], (rows, width)), attn)
    attn = attn.astype(jnp.bfloat16)
    attn_ref[...] = attn

    for step in range(1, n_grp):
        gathered_block(step).wait_recv()
    columns = blocks[...].reshape(n_grp * blocks.shape[1], share)
    projected = jnp.dot(attn, columns, preferred_element_type=jnp.float32)
    mixed = hidden_ref[...].astype(jnp.float32) + projected

    own_sum = jnp.sum(mixed * mixed, axis=1, keepdims=True)
    squares[e] = jnp.broadcast_to(own_sum, squares.shape[1:])

    def sq_copy(peer):
        return pltpu.make_async_remote_copy(
            src_ref=squares.at[e], dst_ref=squares.at[e], send_sem=s_sq.at[peer],
            recv_sem=r_sq.at[e], device_id=(g, peer), device_id_type=MESH)

    def sq_arrival(peer):
        return pltpu.make_async_remote_copy(
            src_ref=squares.at[peer], dst_ref=squares.at[peer], send_sem=s_sq.at[peer],
            recv_sem=r_sq.at[peer], device_id=(g, peer), device_id_type=MESH)

    for peer in range(n_ep):
        @pl.when(e != peer)
        def _():
            sq_copy(peer).start()
    for peer in range(n_ep):
        @pl.when(e != peer)
        def _():
            sq_arrival(peer).wait_recv()
    total_sq = jnp.sum(squares[...][:, :, 0:1], axis=0)
    normed = (mixed * lax.rsqrt(total_sq / width + norm_epsilon) * gain_ref[...]).astype(jnp.bfloat16)
    slots = outgoing.shape[1]
    picked = jnp.dot(picker_ref[...], normed, preferred_element_type=jnp.float32)
    outgoing[...] = picked.reshape(outgoing.shape)

    def dispatch(expert):
        return pltpu.make_async_remote_copy(
            src_ref=outgoing.at[expert], dst_ref=incoming.at[e, g % 2], send_sem=s_out.at[expert],
            recv_sem=r_in.at[g % 2, e], device_id=(expert, home), device_id_type=MESH)

    for expert in range(n_grp):
        @pl.when(jnp.logical_not(serving & (g == expert)))
        def _():
            dispatch(expert).start()

    @pl.when(serving)
    def _():
        incoming[e, g % 2] = outgoing[g]

    def gathered(half, peer):
        return pltpu.make_async_remote_copy(
            src_ref=outgoing.at[0], dst_ref=incoming.at[peer, half], send_sem=s_out.at[0],
            recv_sem=r_in.at[half, peer], device_id=(2 * e + half, peer), device_id_type=MESH)

    for half in range(2):
        for peer in range(n_ep):
            @pl.when(jnp.logical_not(serving & (g == 2 * e + half) & (e == peer)))
            def _():
                gathered(half, peer).wait_recv()

    pre = jnp.zeros((2 * slots, up_ref.shape[1]), jnp.float32)
    for peer in range(n_ep):
        lhs = incoming[peer].reshape(2 * slots, share).astype(jnp.bfloat16)
        pre = pre + jnp.dot(
            lhs, up_ref[peer * share:(peer + 1) * share, :], preferred_element_type=jnp.float32)
    hidden_units = up_ref.shape[1] // 2
    gate = pre[:, :hidden_units]
    act = (gate / (1.0 + jnp.exp(-gate)) * pre[:, hidden_units:]).astype(jnp.bfloat16)
    for peer in range(n_ep):
        piece = jnp.dot(act, down_ref[peer], preferred_element_type=jnp.float32)
        results[peer] = piece.astype(jnp.bfloat16).astype(jnp.float32).reshape(results.shape[1:])

    def give_back(half, peer):
        return pltpu.make_async_remote_copy(
            src_ref=results.at[peer, half], dst_ref=returned.at[g], send_sem=s_res.at[half, peer],
            recv_sem=r_ret.at[g], device_id=(2 * e + half, peer), device_id_type=MESH)

    for half in range(2):
        for peer in range(n_ep):
            @pl.when(jnp.logical_not(serving & (g == 2 * e + half) & (e == peer)))
            def _():
                give_back(half, peer).start()

    @pl.when(serving)
    def _():
        returned[g] = results[e, g % 2]

    def coming_back(expert):
        return pltpu.make_async_remote_copy(
            src_ref=results.at[0, 0], dst_ref=returned.at[expert], send_sem=s_res.at[0, 0],
            recv_sem=r_ret.at[expert], device_id=(expert, home), device_id_type=MESH)

    for expert in range(n_grp):
        @pl.when(jnp.logical_not(serving & (g == expert)))
        def _():
            coming_back(expert).wait_recv()

    back = returned[...].reshape(n_grp * slots, share).astype(jnp.bfloat16)
    mix = jnp.dot(combine_ref[...], back, preferred_element_type=jnp.float32)
    out_ref[...] = (mixed + mix).astype(out_ref.dtype)

    for row in range(2 * rows):
        if row < rows:
            @pl.when(e != row)
            def _():
                first(row).wait_send()
        else:
            first(row).wait_send()

    @pl.when(e < rows)
    def _():
        for target in range(n_ep):
            @pl.when(e != target)
            def _():
                second(target).wait_send()

    for step in range(1, n_grp):
        spread(step).wait_send()
    for peer in range(n_ep):
        @pl.when(e != peer)
        def _():
            sq_copy(peer).wait_send()
    for expert in range(n_grp):
        @pl.when(jnp.logical_not(serving & (g == expert)))
        def _():
            dispatch(expert).wait_send()
    for half in range(2):
        for peer in range(n_ep):
            @pl.when(jnp.logical_not(serving & (g == 2 * e + half) & (e == peer)))
            def _():
                give_back(half, peer).wait_send()


def layer_call(query, mate_query, keys, values, owner, fill, own, block, hidden, gain, picker, combine, up, down_parts):
    n_ep = lax.axis_size("ep")
    n_grp = lax.axis_size("grp")
    rows, share = hidden.shape
    width = share * n_ep
    slots = picker.shape[0] // n_grp
    return pl.pallas_call(
        functools.partial(layer_kernel, rows, n_ep, n_grp, width),
        out_shape=(
            jax.ShapeDtypeStruct((rows, share), jnp.bfloat16),
            jax.ShapeDtypeStruct((rows, width), jnp.bfloat16),
        ),
        in_specs=[pl.BlockSpec(memory_space=pltpu.VMEM)] * 14,
        out_specs=(pl.BlockSpec(memory_space=pltpu.VMEM),) * 2,
        scratch_shapes=[
            pltpu.VMEM((2 * rows, 3, width), jnp.float32),
            pltpu.VMEM((2 * n_ep, 3, width), jnp.float32),
            pltpu.VMEM((rows, 1, width), jnp.float32),
            pltpu.VMEM((n_grp,) + block.shape, block.dtype),
            pltpu.VMEM((n_ep, rows, 128), jnp.float32),
            pltpu.VMEM((n_grp, slots, share), jnp.float32),
            pltpu.VMEM((n_ep, 2, slots, share), jnp.float32),
            pltpu.VMEM((n_ep, 2, slots, share), jnp.float32),
            pltpu.VMEM((n_grp, slots, share), jnp.float32),
            pltpu.SemaphoreType.DMA((2 * rows,)),
            pltpu.SemaphoreType.DMA((2 * n_ep,)),
            pltpu.SemaphoreType.DMA((n_ep,)),
            pltpu.SemaphoreType.DMA((rows,)),
            pltpu.SemaphoreType.DMA((n_grp,)),
            pltpu.SemaphoreType.DMA((n_grp,)),
            pltpu.SemaphoreType.DMA((n_ep,)),
            pltpu.SemaphoreType.DMA((n_ep,)),
            pltpu.SemaphoreType.DMA((n_grp,)),
            pltpu.SemaphoreType.DMA((2, n_ep)),
            pltpu.SemaphoreType.DMA((2, n_ep)),
            pltpu.SemaphoreType.DMA((n_grp,)),
        ],
        compiler_params=pltpu.CompilerParams(collective_id=0, has_side_effects=True),
    )(query, mate_query, keys, values, owner, fill, own, block, hidden, gain, picker, combine, up, down_parts)


def from_partner(block, axis, apart):
    count = lax.axis_size(axis)
    route = []
    for low in range(count):
        high = low | 1 << apart
        if high != low and high < count:
            route += [(low, high), (high, low)]
    return lax.ppermute(block, axis, route)


def per_device(
    hidden,
    query,
    new_kv,
    key_cache,
    value_cache,
    page_owner,
    page_fill,
    out_weight,
    norm_gain,
    gate_up,
    down,
    routes,
    route_weight,
):
    row_count = query.shape[0]
    group_count = lax.axis_size("grp")
    head_group = HEADS // KV_HEADS
    page_count = page_owner.shape[0]
    token_count = key_cache.shape[0]
    page_length = token_count // page_count
    both_rows = 2 * row_count
    scale = HD ** (-0.5)
    partner_query = from_partner(query, "grp", 0)
    expanded = (token_count, KV_HEADS, head_group, HD)
    keys = jnp.broadcast_to(
        key_cache.reshape(token_count, KV_HEADS, 1, HD), expanded
    ).reshape(token_count, HEADS * HD)
    values = jnp.broadcast_to(
        value_cache.reshape(token_count, KV_HEADS, 1, HD), expanded
    ).reshape(token_count, HEADS * HD)
    own_query = query.reshape(row_count, KV_HEADS, head_group, HD)
    fresh_key = new_kv[:, 0].reshape(row_count, KV_HEADS, HD)
    fresh_value = new_kv[:, 1].astype(jnp.float32).reshape(row_count, KV_HEADS, HD)
    own_score = (
        jnp.einsum(
            "rkgd,rkd->rkg", own_query, fresh_key, preferred_element_type=jnp.float32
        ).reshape(row_count, HEADS)
        * scale
    )
    value_rows = jnp.broadcast_to(
        fresh_value[:, :, None, :], (row_count, KV_HEADS, head_group, HD)
    ).reshape(row_count, HEADS, HD)
    width = HEADS * HD
    own_packed = jnp.stack(
        [
            value_rows.reshape(row_count, width),
            jnp.broadcast_to(own_score[..., None], value_rows.shape).reshape(row_count, width),
            jnp.ones((row_count, width), jnp.float32),
        ],
        1,
    )
    feature_share = hidden.shape[1]
    expert_ids = jnp.arange(group_count, dtype=jnp.int32)
    named = routes[:, :, None] == expert_ids[None, None, :]
    chosen = jnp.any(named, 1).astype(jnp.int32)
    weight_at = jnp.sum(
        jnp.where(named, route_weight.astype(jnp.float32)[:, :, None], 0.0), 1
    )
    position = jnp.cumsum(chosen, 0) - chosen
    slot_ids = jnp.arange(row_count, dtype=jnp.int32)
    placed = (chosen[:, :, None] == 1) & (position[:, :, None] == slot_ids[None, None, :])
    picker = (
        placed.transpose(1, 2, 0).reshape(group_count * row_count, row_count).astype(jnp.bfloat16)
    )
    combine = (
        jnp.where(placed, weight_at[:, :, None], 0.0)
        .reshape(row_count, group_count * row_count)
        .astype(jnp.bfloat16)
    )
    down_parts = (
        down[0].reshape(FF, lax.axis_size("ep"), feature_share).transpose(1, 0, 2)
    )
    layer_out, attn_out = layer_call(
        query, partner_query, keys, values, page_owner.reshape(1, -1), page_fill.reshape(1, -1),
        own_packed, out_weight, hidden, norm_gain.reshape(1, feature_share),
        picker, combine, gate_up[0], down_parts,
    )
    return (layer_out, attn_out)


def solution(mesh):
    placed = (
        P("grp", "ep"),
        P("grp", None),
        P("grp", None, None),
        P(("grp", "ep"), None),
        P(("grp", "ep"), None),
        P(("grp", "ep")),
        P(("grp", "ep")),
        P("grp", "ep"),
        P("ep"),
        P("grp", None, None),
        P("grp", None, None),
        P("grp", None),
        P("grp", None),
    )
    return jax.shard_map(
        per_device,
        mesh=mesh,
        in_specs=placed,
        out_specs=(P("grp", "ep"), P("grp", None)),
        check_vma=False,
    )
```

```python
import jax
import jax.numpy as jnp
from jax import lax
from jax.experimental import pallas as pl
from jax.experimental.pallas import tpu as pltpu
from jax.sharding import PartitionSpec as P
import functools

D = 1536
HEADS = 24
KV_HEADS = 8
HD = 64
FF = 512
TOP = 8


masked_score = -1e30
norm_epsilon = 1e-05

MESH = pl.DeviceIdType.MESH


def layer_kernel(
    rows, n_ep, n_grp, width,
    query_ref, mate_query_ref, key_ref, value_ref, owner_ref, fill_ref,
    own_ref, block_ref, hidden_ref, gain_ref, routes_ref, route_weight_ref, up_ref, down_ref,
    out_ref, attn_ref,
    part_ref, got, final, blocks, squares, outgoing, incoming, results, returned,
    s1, r1, s2, r2, s3, r3, s_sq, r_sq, s_out, r_in, s_res, r_ret,
):
    g = lax.axis_index("grp")
    e = lax.axis_index("ep")
    mate = g + 1 - 2 * (g % 2)
    home = g // 2
    serving = home == e
    share = width // n_ep
    barrier = pltpu.get_barrier_semaphore()
    for peer in range(n_ep):
        @pl.when(e != peer)
        def _():
            pl.semaphore_signal(barrier, inc=1, device_id=(g, peer), device_id_type=MESH)
            pl.semaphore_signal(barrier, inc=1, device_id=(g, peer), device_id_type=MESH)
        pl.semaphore_signal(barrier, inc=1, device_id=(mate, peer), device_id_type=MESH)
    for step in range(1, n_grp):
        pl.semaphore_signal(
            barrier, inc=1, device_id=(lax.rem(g + step, n_grp), e), device_id_type=MESH
        )
    for expert in range(n_grp):
        @pl.when(jnp.logical_not(serving & (g == expert)))
        def _():
            pl.semaphore_signal(barrier, inc=1, device_id=(expert, home), device_id_type=MESH)
    for half in range(2):
        for peer in range(n_ep):
            @pl.when(jnp.logical_not(serving & (g == 2 * e + half) & (e == peer)))
            def _():
                pl.semaphore_signal(
                    barrier, inc=1, device_id=(2 * e + half, peer), device_id_type=MESH
                )
    common = 2 * (n_ep - 1) + n_ep + n_grp - 1

    heads = width // HD
    both = 2 * rows
    pages = owner_ref.shape[1]
    tokens = key_ref.shape[0]
    page_length = tokens // pages
    queries = jnp.concatenate([query_ref[...], mate_query_ref[...]], 0)
    lane_head = lax.broadcasted_iota(jnp.int32, (both, width), 1) // HD
    stacked = jnp.concatenate(
        [jnp.where(lane_head == h, queries, jnp.zeros_like(queries)) for h in range(heads)], 0
    )
    row_of = lax.broadcasted_iota(jnp.int32, (both, pages), 0)
    owns = (owner_ref[...] == row_of).astype(jnp.float32)
    token_of = lax.broadcasted_iota(jnp.int32, (tokens, pages), 0)
    page_of = lax.broadcasted_iota(jnp.int32, (tokens, pages), 1)
    filled = (
        (token_of // page_length == page_of) & (token_of % page_length < fill_ref[...])
    ).astype(jnp.float32)
    usable = lax.dot_general(
        owns, filled, (((1,), (1,)), ((), ())), preferred_element_type=jnp.float32
    ) > 0.5
    usable = jnp.concatenate([usable] * heads, 0)
    scores = lax.dot_general(
        stacked, key_ref[...], (((1,), (1,)), ((), ())), preferred_element_type=jnp.float32
    ) * (HD ** -0.5)
    local_top = jnp.max(jnp.where(usable, scores, masked_score), 1, keepdims=True)
    weights = jnp.where(usable, jnp.exp(scores - local_top), 0.0)
    local_total = jnp.sum(weights, 1, keepdims=True)
    local_accum = jnp.dot(
        weights.astype(jnp.bfloat16), value_ref[...], preferred_element_type=jnp.float32
    )
    accum_rows = jnp.zeros((both, width), jnp.float32)
    top_rows = jnp.zeros((both, width), jnp.float32)
    total_rows = jnp.zeros((both, width), jnp.float32)
    for h in range(heads):
        mine = lane_head == h
        block = slice(h * both, (h + 1) * both)
        accum_rows = jnp.where(mine, local_accum[block], accum_rows)
        top_rows = jnp.where(mine, jnp.broadcast_to(local_top[block], (both, width)), top_rows)
        total_rows = jnp.where(mine, jnp.broadcast_to(local_total[block], (both, width)), total_rows)
    for row in range(both):
        part_ref[row, 0:1, :] = accum_rows[row:row + 1]
        part_ref[row, 1:2, :] = top_rows[row:row + 1]
        part_ref[row, 2:3, :] = total_rows[row:row + 1]

    choices = routes_ref.shape[1]
    expert_of = lax.broadcasted_iota(jnp.int32, (rows, n_grp), 1)
    chosen = jnp.zeros((rows, n_grp), jnp.float32)
    weight_at = jnp.zeros((rows, n_grp), jnp.float32)
    for choice in range(choices):
        hit = routes_ref[:, choice:choice + 1] == expert_of
        chosen = chosen + hit.astype(jnp.float32)
        weight_at = weight_at + jnp.where(
            hit, route_weight_ref[:, choice:choice + 1].astype(jnp.float32), 0.0)
    earlier = (
        lax.broadcasted_iota(jnp.int32, (rows, rows), 1)
        < lax.broadcasted_iota(jnp.int32, (rows, rows), 0)
    ).astype(jnp.float32)
    position = jnp.dot(earlier, chosen, preferred_element_type=jnp.float32)
    slot_count = rows * n_grp
    spread_out = (
        lax.broadcasted_iota(jnp.int32, (n_grp, slot_count), 1) // rows
        == lax.broadcasted_iota(jnp.int32, (n_grp, slot_count), 0)
    ).astype(jnp.bfloat16)
    chosen_wide = jnp.dot(chosen.astype(jnp.bfloat16), spread_out, preferred_element_type=jnp.float32)
    position_wide = jnp.dot(position.astype(jnp.bfloat16), spread_out, preferred_element_type=jnp.float32)
    weight_wide = jnp.dot(weight_at.astype(jnp.bfloat16), spread_out, preferred_element_type=jnp.float32)
    slot_of = (lax.broadcasted_iota(jnp.int32, (rows, slot_count), 1) % rows).astype(jnp.float32)
    placed = (chosen_wide > 0.5) & (position_wide == slot_of)
    combine = jnp.where(placed, weight_wide, 0.0).astype(jnp.bfloat16)
    picker = jnp.transpose(placed.astype(jnp.float32)).astype(jnp.bfloat16)

    @pl.when(serving)
    def _():
        pl.semaphore_wait(barrier, common + n_grp - 1 + 2 * n_ep - 1)

    @pl.when(jnp.logical_not(serving))
    def _():
        pl.semaphore_wait(barrier, common + n_grp + 2 * n_ep)

    def first(row):
        if row < rows:
            target = (g, row)
            slot = e
        else:
            target = (mate, row - rows)
            slot = n_ep + e
        return pltpu.make_async_remote_copy(
            src_ref=part_ref.at[row], dst_ref=got.at[slot], send_sem=s1.at[row],
            recv_sem=r1.at[slot], device_id=target, device_id_type=MESH)

    for row in range(2 * rows):
        if row < rows:
            @pl.when(e != row)
            def _():
                first(row).start()

            @pl.when(e == row)
            def _():
                got[e] = part_ref[row]
        else:
            first(row).start()

    def spread(step):
        return pltpu.make_async_remote_copy(
            src_ref=block_ref, dst_ref=blocks.at[g], send_sem=s3.at[step],
            recv_sem=r3.at[g], device_id=(lax.rem(g + step, n_grp), e), device_id_type=MESH)

    def gathered_block(step):
        source = lax.rem(g + n_grp - step, n_grp)
        return pltpu.make_async_remote_copy(
            src_ref=block_ref, dst_ref=blocks.at[source], send_sem=s3.at[step],
            recv_sem=r3.at[source], device_id=(source, e), device_id_type=MESH)

    for step in range(1, n_grp):
        spread(step).start()
    blocks[g] = block_ref[...]

    def incoming_part(slot):
        return pltpu.make_async_remote_copy(
            src_ref=part_ref.at[0], dst_ref=got.at[slot], send_sem=s1.at[0],
            recv_sem=r1.at[slot], device_id=(g, 0), device_id_type=MESH)

    def second(target):
        return pltpu.make_async_remote_copy(
            src_ref=final.at[e], dst_ref=final.at[e], send_sem=s2.at[target],
            recv_sem=r2.at[e], device_id=(g, target), device_id_type=MESH)

    @pl.when(e < rows)
    def _():
        for slot in range(2 * n_ep):
            if slot < n_ep:
                @pl.when(e != slot)
                def _():
                    incoming_part(slot).wait_recv()
            else:
                incoming_part(slot).wait_recv()
        stack = got[...]
        own = own_ref[e]
        maxes = jnp.maximum(jnp.max(stack[:, 1:2, :], 0), own[1:2, :])
        factors = jnp.exp(stack[:, 1:2, :] - maxes[None])
        own_factor = jnp.exp(own[1:2, :] - maxes)
        total = jnp.sum(stack[:, 2:3, :] * factors, 0) + own_factor
        accum = jnp.sum(stack[:, 0:1, :] * factors, 0) + own[0:1, :] * own_factor
        final[e] = (accum / total).astype(jnp.bfloat16).astype(jnp.float32)
        for target in range(n_ep):
            @pl.when(e != target)
            def _():
                second(target).start()

    def arriving(row):
        return pltpu.make_async_remote_copy(
            src_ref=final.at[row], dst_ref=final.at[row], send_sem=s2.at[0],
            recv_sem=r2.at[row], device_id=(g, row), device_id_type=MESH)

    for row in range(rows):
        @pl.when(e != row)
        def _():
            arriving(row).wait_recv()

    row_ids = lax.broadcasted_iota(jnp.int32, (rows, width), 0)
    attn = jnp.zeros((rows, width), jnp.float32)
    for row in range(rows):
        attn = jnp.where(row_ids == row, jnp.broadcast_to(final[row], (rows, width)), attn)
    attn = attn.astype(jnp.bfloat16)
    attn_ref[...] = attn

    for step in range(1, n_grp):
        gathered_block(step).wait_recv()
    columns = blocks[...].reshape(n_grp * blocks.shape[1], share)
    projected = jnp.dot(attn, columns, preferred_element_type=jnp.float32)
    mixed = hidden_ref[...].astype(jnp.float32) + projected

    own_sum = jnp.sum(mixed * mixed, axis=1, keepdims=True)
    squares[e] = jnp.broadcast_to(own_sum, squares.shape[1:])

    def sq_copy(peer):
        return pltpu.make_async_remote_copy(
            src_ref=squares.at[e], dst_ref=squares.at[e], send_sem=s_sq.at[peer],
            recv_sem=r_sq.at[e], device_id=(g, peer), device_id_type=MESH)

    def sq_arrival(peer):
        return pltpu.make_async_remote_copy(
            src_ref=squares.at[peer], dst_ref=squares.at[peer], send_sem=s_sq.at[peer],
            recv_sem=r_sq.at[peer], device_id=(g, peer), device_id_type=MESH)

    for peer in range(n_ep):
        @pl.when(e != peer)
        def _():
            sq_copy(peer).start()
    for peer in range(n_ep):
        @pl.when(e != peer)
        def _():
            sq_arrival(peer).wait_recv()
    total_sq = jnp.sum(squares[...][:, :, 0:1], axis=0)
    normed = (mixed * lax.rsqrt(total_sq / width + norm_epsilon) * gain_ref[...]).astype(jnp.bfloat16)
    slots = outgoing.shape[1]
    picked = jnp.dot(picker, normed, preferred_element_type=jnp.float32)
    outgoing[...] = picked.reshape(outgoing.shape)

    def dispatch(expert):
        return pltpu.make_async_remote_copy(
            src_ref=outgoing.at[expert], dst_ref=incoming.at[e, g % 2], send_sem=s_out.at[expert],
            recv_sem=r_in.at[g % 2, e], device_id=(expert, home), device_id_type=MESH)

    for expert in range(n_grp):
        @pl.when(jnp.logical_not(serving & (g == expert)))
        def _():
            dispatch(expert).start()

    @pl.when(serving)
    def _():
        incoming[e, g % 2] = outgoing[g]

    def gathered(half, peer):
        return pltpu.make_async_remote_copy(
            src_ref=outgoing.at[0], dst_ref=incoming.at[peer, half], send_sem=s_out.at[0],
            recv_sem=r_in.at[half, peer], device_id=(2 * e + half, peer), device_id_type=MESH)

    for half in range(2):
        for peer in range(n_ep):
            @pl.when(jnp.logical_not(serving & (g == 2 * e + half) & (e == peer)))
            def _():
                gathered(half, peer).wait_recv()

    pre = jnp.zeros((2 * slots, up_ref.shape[1]), jnp.float32)
    for peer in range(n_ep):
        lhs = incoming[peer].reshape(2 * slots, share).astype(jnp.bfloat16)
        pre = pre + jnp.dot(
            lhs, up_ref[peer * share:(peer + 1) * share, :], preferred_element_type=jnp.float32)
    hidden_units = up_ref.shape[1] // 2
    gate = pre[:, :hidden_units]
    act = (gate / (1.0 + jnp.exp(-gate)) * pre[:, hidden_units:]).astype(jnp.bfloat16)
    for peer in range(n_ep):
        piece = jnp.dot(
            act, down_ref[:, peer * share:(peer + 1) * share], preferred_element_type=jnp.float32)
        results[peer] = piece.astype(jnp.bfloat16).astype(jnp.float32).reshape(results.shape[1:])

    def give_back(half, peer):
        return pltpu.make_async_remote_copy(
            src_ref=results.at[peer, half], dst_ref=returned.at[g], send_sem=s_res.at[half, peer],
            recv_sem=r_ret.at[g], device_id=(2 * e + half, peer), device_id_type=MESH)

    for half in range(2):
        for peer in range(n_ep):
            @pl.when(jnp.logical_not(serving & (g == 2 * e + half) & (e == peer)))
            def _():
                give_back(half, peer).start()

    @pl.when(serving)
    def _():
        returned[g] = results[e, g % 2]

    def coming_back(expert):
        return pltpu.make_async_remote_copy(
            src_ref=results.at[0, 0], dst_ref=returned.at[expert], send_sem=s_res.at[0, 0],
            recv_sem=r_ret.at[expert], device_id=(expert, home), device_id_type=MESH)

    for expert in range(n_grp):
        @pl.when(jnp.logical_not(serving & (g == expert)))
        def _():
            coming_back(expert).wait_recv()

    back = returned[...].reshape(n_grp * slots, share).astype(jnp.bfloat16)
    mix = jnp.dot(combine, back, preferred_element_type=jnp.float32)
    out_ref[...] = (mixed + mix).astype(out_ref.dtype)

    for row in range(2 * rows):
        if row < rows:
            @pl.when(e != row)
            def _():
                first(row).wait_send()
        else:
            first(row).wait_send()

    @pl.when(e < rows)
    def _():
        for target in range(n_ep):
            @pl.when(e != target)
            def _():
                second(target).wait_send()

    for step in range(1, n_grp):
        spread(step).wait_send()
    for peer in range(n_ep):
        @pl.when(e != peer)
        def _():
            sq_copy(peer).wait_send()
    for expert in range(n_grp):
        @pl.when(jnp.logical_not(serving & (g == expert)))
        def _():
            dispatch(expert).wait_send()
    for half in range(2):
        for peer in range(n_ep):
            @pl.when(jnp.logical_not(serving & (g == 2 * e + half) & (e == peer)))
            def _():
                give_back(half, peer).wait_send()


def layer_call(query, mate_query, keys, values, owner, fill, own, block, hidden, gain, routes, route_weight, up, down):
    n_ep = lax.axis_size("ep")
    n_grp = lax.axis_size("grp")
    rows, share = hidden.shape
    width = share * n_ep
    slots = rows
    return pl.pallas_call(
        functools.partial(layer_kernel, rows, n_ep, n_grp, width),
        out_shape=(
            jax.ShapeDtypeStruct((rows, share), jnp.bfloat16),
            jax.ShapeDtypeStruct((rows, width), jnp.bfloat16),
        ),
        in_specs=[pl.BlockSpec(memory_space=pltpu.VMEM)] * 14,
        out_specs=(pl.BlockSpec(memory_space=pltpu.VMEM),) * 2,
        scratch_shapes=[
            pltpu.VMEM((2 * rows, 3, width), jnp.float32),
            pltpu.VMEM((2 * n_ep, 3, width), jnp.float32),
            pltpu.VMEM((rows, 1, width), jnp.float32),
            pltpu.VMEM((n_grp,) + block.shape, block.dtype),
            pltpu.VMEM((n_ep, rows, 128), jnp.float32),
            pltpu.VMEM((n_grp, slots, share), jnp.float32),
            pltpu.VMEM((n_ep, 2, slots, share), jnp.float32),
            pltpu.VMEM((n_ep, 2, slots, share), jnp.float32),
            pltpu.VMEM((n_grp, slots, share), jnp.float32),
            pltpu.SemaphoreType.DMA((2 * rows,)),
            pltpu.SemaphoreType.DMA((2 * n_ep,)),
            pltpu.SemaphoreType.DMA((n_ep,)),
            pltpu.SemaphoreType.DMA((rows,)),
            pltpu.SemaphoreType.DMA((n_grp,)),
            pltpu.SemaphoreType.DMA((n_grp,)),
            pltpu.SemaphoreType.DMA((n_ep,)),
            pltpu.SemaphoreType.DMA((n_ep,)),
            pltpu.SemaphoreType.DMA((n_grp,)),
            pltpu.SemaphoreType.DMA((2, n_ep)),
            pltpu.SemaphoreType.DMA((2, n_ep)),
            pltpu.SemaphoreType.DMA((n_grp,)),
        ],
        compiler_params=pltpu.CompilerParams(collective_id=0, has_side_effects=True),
    )(query, mate_query, keys, values, owner, fill, own, block, hidden, gain, routes, route_weight, up, down)


def from_partner(block, axis, apart):
    count = lax.axis_size(axis)
    route = []
    for low in range(count):
        high = low | 1 << apart
        if high != low and high < count:
            route += [(low, high), (high, low)]
    return lax.ppermute(block, axis, route)


def per_device(
    hidden,
    query,
    new_kv,
    key_cache,
    value_cache,
    page_owner,
    page_fill,
    out_weight,
    norm_gain,
    gate_up,
    down,
    routes,
    route_weight,
):
    row_count = query.shape[0]
    group_count = lax.axis_size("grp")
    head_group = HEADS // KV_HEADS
    page_count = page_owner.shape[0]
    token_count = key_cache.shape[0]
    page_length = token_count // page_count
    both_rows = 2 * row_count
    scale = HD ** (-0.5)
    partner_query = from_partner(query, "grp", 0)
    expanded = (token_count, KV_HEADS, head_group, HD)
    keys = jnp.broadcast_to(
        key_cache.reshape(token_count, KV_HEADS, 1, HD), expanded
    ).reshape(token_count, HEADS * HD)
    values = jnp.broadcast_to(
        value_cache.reshape(token_count, KV_HEADS, 1, HD), expanded
    ).reshape(token_count, HEADS * HD)
    own_query = query.reshape(row_count, KV_HEADS, head_group, HD)
    fresh_key = new_kv[:, 0].reshape(row_count, KV_HEADS, HD)
    fresh_value = new_kv[:, 1].astype(jnp.float32).reshape(row_count, KV_HEADS, HD)
    own_score = (
        jnp.einsum(
            "rkgd,rkd->rkg", own_query, fresh_key, preferred_element_type=jnp.float32
        ).reshape(row_count, HEADS)
        * scale
    )
    value_rows = jnp.broadcast_to(
        fresh_value[:, :, None, :], (row_count, KV_HEADS, head_group, HD)
    ).reshape(row_count, HEADS, HD)
    width = HEADS * HD
    own_packed = jnp.stack(
        [
            value_rows.reshape(row_count, width),
            jnp.broadcast_to(own_score[..., None], value_rows.shape).reshape(row_count, width),
            jnp.ones((row_count, width), jnp.float32),
        ],
        1,
    )
    feature_share = hidden.shape[1]
    layer_out, attn_out = layer_call(
        query, partner_query, keys, values, page_owner.reshape(1, -1), page_fill.reshape(1, -1),
        own_packed, out_weight, hidden, norm_gain.reshape(1, feature_share),
        routes, route_weight, gate_up[0], down[0],
    )
    return (layer_out, attn_out)


def solution(mesh):
    placed = (
        P("grp", "ep"),
        P("grp", None),
        P("grp", None, None),
        P(("grp", "ep"), None),
        P(("grp", "ep"), None),
        P(("grp", "ep")),
        P(("grp", "ep")),
        P("grp", "ep"),
        P("ep"),
        P("grp", None, None),
        P("grp", None, None),
        P("grp", None),
        P("grp", None),
    )
    return jax.shard_map(
        per_device,
        mesh=mesh,
        in_specs=placed,
        out_specs=(P("grp", "ep"), P("grp", None)),
        check_vma=False,
    )
```

```python
import jax
import jax.numpy as jnp
from jax import lax
from jax.experimental import pallas as pl
from jax.experimental.pallas import tpu as pltpu
from jax.sharding import PartitionSpec as P
import functools

D = 1536
HEADS = 24
KV_HEADS = 8
HD = 64
FF = 512
TOP = 8


masked_score = -1e30
norm_epsilon = 1e-05

MESH = pl.DeviceIdType.MESH


def layer_kernel(
    rows, n_ep, n_grp, width,
    query_ref, mate_query_ref, key_ref, value_ref, owner_ref, fill_ref,
    fresh_ref, block_ref, hidden_ref, gain_ref, routes_ref, route_weight_ref, up_ref, down_ref,
    out_ref, attn_ref,
    part_ref, own_ref, got, final, blocks, squares, outgoing, incoming, results, returned,
    s1, r1, s2, r2, s3, r3, s_sq, r_sq, s_out, r_in, s_res, r_ret,
):
    g = lax.axis_index("grp")
    e = lax.axis_index("ep")
    mate = g + 1 - 2 * (g % 2)
    home = g // 2
    serving = home == e
    share = width // n_ep
    barrier = pltpu.get_barrier_semaphore()
    for peer in range(n_ep):
        @pl.when(e != peer)
        def _():
            pl.semaphore_signal(barrier, inc=1, device_id=(g, peer), device_id_type=MESH)
            pl.semaphore_signal(barrier, inc=1, device_id=(g, peer), device_id_type=MESH)
        pl.semaphore_signal(barrier, inc=1, device_id=(mate, peer), device_id_type=MESH)
    for step in range(1, n_grp):
        pl.semaphore_signal(
            barrier, inc=1, device_id=(lax.rem(g + step, n_grp), e), device_id_type=MESH
        )
    for expert in range(n_grp):
        @pl.when(jnp.logical_not(serving & (g == expert)))
        def _():
            pl.semaphore_signal(barrier, inc=1, device_id=(expert, home), device_id_type=MESH)
    for half in range(2):
        for peer in range(n_ep):
            @pl.when(jnp.logical_not(serving & (g == 2 * e + half) & (e == peer)))
            def _():
                pl.semaphore_signal(
                    barrier, inc=1, device_id=(2 * e + half, peer), device_id_type=MESH
                )
    common = 2 * (n_ep - 1) + n_ep + n_grp - 1

    heads = width // HD
    both = 2 * rows
    pages = owner_ref.shape[1]
    tokens = key_ref.shape[0]
    kv_width = key_ref.shape[1]
    group_size = heads // (kv_width // HD)
    kv_lane = lax.broadcasted_iota(jnp.int32, (kv_width, width), 0)
    head_lane = lax.broadcasted_iota(jnp.int32, (kv_width, width), 1)
    widen = (
        (kv_lane % HD == head_lane % HD) & (kv_lane // HD == head_lane // (HD * group_size))
    ).astype(jnp.bfloat16)
    wide_keys = jnp.dot(key_ref[...], widen, preferred_element_type=jnp.float32).astype(jnp.bfloat16)
    wide_values = jnp.dot(value_ref[...], widen, preferred_element_type=jnp.float32).astype(jnp.bfloat16)
    fresh_keys = jnp.dot(
        fresh_ref[:, :kv_width], widen, preferred_element_type=jnp.float32).astype(jnp.bfloat16)
    fresh_values = jnp.dot(fresh_ref[:, kv_width:], widen, preferred_element_type=jnp.float32)
    page_length = tokens // pages
    queries = jnp.concatenate([query_ref[...], mate_query_ref[...]], 0)
    lane_head = lax.broadcasted_iota(jnp.int32, (both, width), 1) // HD
    stacked = jnp.concatenate(
        [jnp.where(lane_head == h, queries, jnp.zeros_like(queries)) for h in range(heads)], 0
    )
    row_of = lax.broadcasted_iota(jnp.int32, (both, pages), 0)
    owns = (owner_ref[...] == row_of).astype(jnp.float32)
    token_of = lax.broadcasted_iota(jnp.int32, (tokens, pages), 0)
    page_of = lax.broadcasted_iota(jnp.int32, (tokens, pages), 1)
    filled = (
        (token_of // page_length == page_of) & (token_of % page_length < fill_ref[...])
    ).astype(jnp.float32)
    usable = lax.dot_general(
        owns, filled, (((1,), (1,)), ((), ())), preferred_element_type=jnp.float32
    ) > 0.5
    usable = jnp.concatenate([usable] * heads, 0)
    scores = lax.dot_general(
        stacked, wide_keys, (((1,), (1,)), ((), ())), preferred_element_type=jnp.float32
    ) * (HD ** -0.5)
    own_scores = lax.dot_general(
        stacked, fresh_keys, (((1,), (1,)), ((), ())), preferred_element_type=jnp.float32
    ) * (HD ** -0.5)
    own_column = lax.broadcasted_iota(jnp.int32, own_scores.shape, 1)
    own_row = lax.broadcasted_iota(jnp.int32, own_scores.shape, 0) % both
    own_top = jnp.sum(jnp.where(own_column == own_row, own_scores, 0.0), 1, keepdims=True)
    local_top = jnp.max(jnp.where(usable, scores, masked_score), 1, keepdims=True)
    weights = jnp.where(usable, jnp.exp(scores - local_top), 0.0)
    local_total = jnp.sum(weights, 1, keepdims=True)
    local_accum = jnp.dot(
        weights.astype(jnp.bfloat16), wide_values, preferred_element_type=jnp.float32
    )
    accum_rows = jnp.zeros((both, width), jnp.float32)
    top_rows = jnp.zeros((both, width), jnp.float32)
    total_rows = jnp.zeros((both, width), jnp.float32)
    own_rows = jnp.zeros((both, width), jnp.float32)
    for h in range(heads):
        mine = lane_head == h
        block = slice(h * both, (h + 1) * both)
        accum_rows = jnp.where(mine, local_accum[block], accum_rows)
        top_rows = jnp.where(mine, jnp.broadcast_to(local_top[block], (both, width)), top_rows)
        total_rows = jnp.where(mine, jnp.broadcast_to(local_total[block], (both, width)), total_rows)
        own_rows = jnp.where(mine, jnp.broadcast_to(own_top[block], (both, width)), own_rows)
    for row in range(both):
        part_ref[row, 0:1, :] = accum_rows[row:row + 1]
        part_ref[row, 1:2, :] = top_rows[row:row + 1]
        part_ref[row, 2:3, :] = total_rows[row:row + 1]
    for row in range(rows):
        own_ref[row, 0:1, :] = fresh_values[row:row + 1]
        own_ref[row, 1:2, :] = own_rows[row:row + 1]
        own_ref[row, 2:3, :] = jnp.ones((1, width), jnp.float32)

    choices = routes_ref.shape[1]
    expert_of = lax.broadcasted_iota(jnp.int32, (rows, n_grp), 1)
    chosen = jnp.zeros((rows, n_grp), jnp.float32)
    weight_at = jnp.zeros((rows, n_grp), jnp.float32)
    for choice in range(choices):
        hit = routes_ref[:, choice:choice + 1] == expert_of
        chosen = chosen + hit.astype(jnp.float32)
        weight_at = weight_at + jnp.where(
            hit, route_weight_ref[:, choice:choice + 1].astype(jnp.float32), 0.0)
    earlier = (
        lax.broadcasted_iota(jnp.int32, (rows, rows), 1)
        < lax.broadcasted_iota(jnp.int32, (rows, rows), 0)
    ).astype(jnp.float32)
    position = jnp.dot(earlier, chosen, preferred_element_type=jnp.float32)
    slot_count = rows * n_grp
    spread_out = (
        lax.broadcasted_iota(jnp.int32, (n_grp, slot_count), 1) // rows
        == lax.broadcasted_iota(jnp.int32, (n_grp, slot_count), 0)
    ).astype(jnp.bfloat16)
    chosen_wide = jnp.dot(chosen.astype(jnp.bfloat16), spread_out, preferred_element_type=jnp.float32)
    position_wide = jnp.dot(position.astype(jnp.bfloat16), spread_out, preferred_element_type=jnp.float32)
    weight_wide = jnp.dot(weight_at.astype(jnp.bfloat16), spread_out, preferred_element_type=jnp.float32)
    slot_of = (lax.broadcasted_iota(jnp.int32, (rows, slot_count), 1) % rows).astype(jnp.float32)
    placed = (chosen_wide > 0.5) & (position_wide == slot_of)
    combine = jnp.where(placed, weight_wide, 0.0).astype(jnp.bfloat16)
    picker = jnp.transpose(placed.astype(jnp.float32)).astype(jnp.bfloat16)

    @pl.when(serving)
    def _():
        pl.semaphore_wait(barrier, common + n_grp - 1 + 2 * n_ep - 1)

    @pl.when(jnp.logical_not(serving))
    def _():
        pl.semaphore_wait(barrier, common + n_grp + 2 * n_ep)

    def first(row):
        if row < rows:
            target = (g, row)
            slot = e
        else:
            target = (mate, row - rows)
            slot = n_ep + e
        return pltpu.make_async_remote_copy(
            src_ref=part_ref.at[row], dst_ref=got.at[slot], send_sem=s1.at[row],
            recv_sem=r1.at[slot], device_id=target, device_id_type=MESH)

    for row in range(2 * rows):
        if row < rows:
            @pl.when(e != row)
            def _():
                first(row).start()

            @pl.when(e == row)
            def _():
                got[e] = part_ref[row]
        else:
            first(row).start()

    def spread(step):
        return pltpu.make_async_remote_copy(
            src_ref=block_ref, dst_ref=blocks.at[g], send_sem=s3.at[step],
            recv_sem=r3.at[g], device_id=(lax.rem(g + step, n_grp), e), device_id_type=MESH)

    def gathered_block(step):
        source = lax.rem(g + n_grp - step, n_grp)
        return pltpu.make_async_remote_copy(
            src_ref=block_ref, dst_ref=blocks.at[source], send_sem=s3.at[step],
            recv_sem=r3.at[source], device_id=(source, e), device_id_type=MESH)

    for step in range(1, n_grp):
        spread(step).start()
    blocks[g] = block_ref[...]

    def incoming_part(slot):
        return pltpu.make_async_remote_copy(
            src_ref=part_ref.at[0], dst_ref=got.at[slot], send_sem=s1.at[0],
            recv_sem=r1.at[slot], device_id=(g, 0), device_id_type=MESH)

    def second(target):
        return pltpu.make_async_remote_copy(
            src_ref=final.at[e], dst_ref=final.at[e], send_sem=s2.at[target],
            recv_sem=r2.at[e], device_id=(g, target), device_id_type=MESH)

    @pl.when(e < rows)
    def _():
        for slot in range(2 * n_ep):
            if slot < n_ep:
                @pl.when(e != slot)
                def _():
                    incoming_part(slot).wait_recv()
            else:
                incoming_part(slot).wait_recv()
        stack = got[...]
        own = own_ref[e]
        maxes = jnp.maximum(jnp.max(stack[:, 1:2, :], 0), own[1:2, :])
        factors = jnp.exp(stack[:, 1:2, :] - maxes[None])
        own_factor = jnp.exp(own[1:2, :] - maxes)
        total = jnp.sum(stack[:, 2:3, :] * factors, 0) + own_factor
        accum = jnp.sum(stack[:, 0:1, :] * factors, 0) + own[0:1, :] * own_factor
        final[e] = (accum / total).astype(jnp.bfloat16).astype(jnp.float32)
        for target in range(n_ep):
            @pl.when(e != target)
            def _():
                second(target).start()

    def arriving(row):
        return pltpu.make_async_remote_copy(
            src_ref=final.at[row], dst_ref=final.at[row], send_sem=s2.at[0],
            recv_sem=r2.at[row], device_id=(g, row), device_id_type=MESH)

    for row in range(rows):
        @pl.when(e != row)
        def _():
            arriving(row).wait_recv()

    row_ids = lax.broadcasted_iota(jnp.int32, (rows, width), 0)
    attn = jnp.zeros((rows, width), jnp.float32)
    for row in range(rows):
        attn = jnp.where(row_ids == row, jnp.broadcast_to(final[row], (rows, width)), attn)
    attn = attn.astype(jnp.bfloat16)
    attn_ref[...] = attn

    for step in range(1, n_grp):
        gathered_block(step).wait_recv()
    columns = blocks[...].reshape(n_grp * blocks.shape[1], share)
    projected = jnp.dot(attn, columns, preferred_element_type=jnp.float32)
    mixed = hidden_ref[...].astype(jnp.float32) + projected

    own_sum = jnp.sum(mixed * mixed, axis=1, keepdims=True)
    squares[e] = jnp.broadcast_to(own_sum, squares.shape[1:])

    def sq_copy(peer):
        return pltpu.make_async_remote_copy(
            src_ref=squares.at[e], dst_ref=squares.at[e], send_sem=s_sq.at[peer],
            recv_sem=r_sq.at[e], device_id=(g, peer), device_id_type=MESH)

    def sq_arrival(peer):
        return pltpu.make_async_remote_copy(
            src_ref=squares.at[peer], dst_ref=squares.at[peer], send_sem=s_sq.at[peer],
            recv_sem=r_sq.at[peer], device_id=(g, peer), device_id_type=MESH)

    for peer in range(n_ep):
        @pl.when(e != peer)
        def _():
            sq_copy(peer).start()
    for peer in range(n_ep):
        @pl.when(e != peer)
        def _():
            sq_arrival(peer).wait_recv()
    total_sq = jnp.sum(squares[...][:, :, 0:1], axis=0)
    normed = (mixed * lax.rsqrt(total_sq / width + norm_epsilon) * gain_ref[...]).astype(jnp.bfloat16)
    slots = outgoing.shape[1]
    picked = jnp.dot(picker, normed, preferred_element_type=jnp.float32)
    outgoing[...] = picked.reshape(outgoing.shape)

    def dispatch(expert):
        return pltpu.make_async_remote_copy(
            src_ref=outgoing.at[expert], dst_ref=incoming.at[e, g % 2], send_sem=s_out.at[expert],
            recv_sem=r_in.at[g % 2, e], device_id=(expert, home), device_id_type=MESH)

    for expert in range(n_grp):
        @pl.when(jnp.logical_not(serving & (g == expert)))
        def _():
            dispatch(expert).start()

    @pl.when(serving)
    def _():
        incoming[e, g % 2] = outgoing[g]

    def gathered(half, peer):
        return pltpu.make_async_remote_copy(
            src_ref=outgoing.at[0], dst_ref=incoming.at[peer, half], send_sem=s_out.at[0],
            recv_sem=r_in.at[half, peer], device_id=(2 * e + half, peer), device_id_type=MESH)

    for half in range(2):
        for peer in range(n_ep):
            @pl.when(jnp.logical_not(serving & (g == 2 * e + half) & (e == peer)))
            def _():
                gathered(half, peer).wait_recv()

    pre = jnp.zeros((2 * slots, up_ref.shape[1]), jnp.float32)
    for peer in range(n_ep):
        lhs = incoming[peer].reshape(2 * slots, share).astype(jnp.bfloat16)
        pre = pre + jnp.dot(
            lhs, up_ref[peer * share:(peer + 1) * share, :], preferred_element_type=jnp.float32)
    hidden_units = up_ref.shape[1] // 2
    gate = pre[:, :hidden_units]
    act = (gate / (1.0 + jnp.exp(-gate)) * pre[:, hidden_units:]).astype(jnp.bfloat16)
    for peer in range(n_ep):
        piece = jnp.dot(
            act, down_ref[:, peer * share:(peer + 1) * share], preferred_element_type=jnp.float32)
        results[peer] = piece.astype(jnp.bfloat16).astype(jnp.float32).reshape(results.shape[1:])

    def give_back(half, peer):
        return pltpu.make_async_remote_copy(
            src_ref=results.at[peer, half], dst_ref=returned.at[g], send_sem=s_res.at[half, peer],
            recv_sem=r_ret.at[g], device_id=(2 * e + half, peer), device_id_type=MESH)

    for half in range(2):
        for peer in range(n_ep):
            @pl.when(jnp.logical_not(serving & (g == 2 * e + half) & (e == peer)))
            def _():
                give_back(half, peer).start()

    @pl.when(serving)
    def _():
        returned[g] = results[e, g % 2]

    def coming_back(expert):
        return pltpu.make_async_remote_copy(
            src_ref=results.at[0, 0], dst_ref=returned.at[expert], send_sem=s_res.at[0, 0],
            recv_sem=r_ret.at[expert], device_id=(expert, home), device_id_type=MESH)

    for expert in range(n_grp):
        @pl.when(jnp.logical_not(serving & (g == expert)))
        def _():
            coming_back(expert).wait_recv()

    back = returned[...].reshape(n_grp * slots, share).astype(jnp.bfloat16)
    mix = jnp.dot(combine, back, preferred_element_type=jnp.float32)
    out_ref[...] = (mixed + mix).astype(out_ref.dtype)

    for row in range(2 * rows):
        if row < rows:
            @pl.when(e != row)
            def _():
                first(row).wait_send()
        else:
            first(row).wait_send()

    @pl.when(e < rows)
    def _():
        for target in range(n_ep):
            @pl.when(e != target)
            def _():
                second(target).wait_send()

    for step in range(1, n_grp):
        spread(step).wait_send()
    for peer in range(n_ep):
        @pl.when(e != peer)
        def _():
            sq_copy(peer).wait_send()
    for expert in range(n_grp):
        @pl.when(jnp.logical_not(serving & (g == expert)))
        def _():
            dispatch(expert).wait_send()
    for half in range(2):
        for peer in range(n_ep):
            @pl.when(jnp.logical_not(serving & (g == 2 * e + half) & (e == peer)))
            def _():
                give_back(half, peer).wait_send()


def layer_call(query, mate_query, keys, values, owner, fill, fresh, block, hidden, gain, routes, route_weight, up, down):
    n_ep = lax.axis_size("ep")
    n_grp = lax.axis_size("grp")
    rows, share = hidden.shape
    width = share * n_ep
    slots = rows
    return pl.pallas_call(
        functools.partial(layer_kernel, rows, n_ep, n_grp, width),
        out_shape=(
            jax.ShapeDtypeStruct((rows, share), jnp.bfloat16),
            jax.ShapeDtypeStruct((rows, width), jnp.bfloat16),
        ),
        in_specs=[pl.BlockSpec(memory_space=pltpu.VMEM)] * 14,
        out_specs=(pl.BlockSpec(memory_space=pltpu.VMEM),) * 2,
        scratch_shapes=[
            pltpu.VMEM((2 * rows, 3, width), jnp.float32),
            pltpu.VMEM((rows, 3, width), jnp.float32),
            pltpu.VMEM((2 * n_ep, 3, width), jnp.float32),
            pltpu.VMEM((rows, 1, width), jnp.float32),
            pltpu.VMEM((n_grp,) + block.shape, block.dtype),
            pltpu.VMEM((n_ep, rows, 128), jnp.float32),
            pltpu.VMEM((n_grp, slots, share), jnp.float32),
            pltpu.VMEM((n_ep, 2, slots, share), jnp.float32),
            pltpu.VMEM((n_ep, 2, slots, share), jnp.float32),
            pltpu.VMEM((n_grp, slots, share), jnp.float32),
            pltpu.SemaphoreType.DMA((2 * rows,)),
            pltpu.SemaphoreType.DMA((2 * n_ep,)),
            pltpu.SemaphoreType.DMA((n_ep,)),
            pltpu.SemaphoreType.DMA((rows,)),
            pltpu.SemaphoreType.DMA((n_grp,)),
            pltpu.SemaphoreType.DMA((n_grp,)),
            pltpu.SemaphoreType.DMA((n_ep,)),
            pltpu.SemaphoreType.DMA((n_ep,)),
            pltpu.SemaphoreType.DMA((n_grp,)),
            pltpu.SemaphoreType.DMA((2, n_ep)),
            pltpu.SemaphoreType.DMA((2, n_ep)),
            pltpu.SemaphoreType.DMA((n_grp,)),
        ],
        compiler_params=pltpu.CompilerParams(collective_id=0, has_side_effects=True),
    )(query, mate_query, keys, values, owner, fill, fresh, block, hidden, gain, routes, route_weight, up, down)


def from_partner(block, axis, apart):
    count = lax.axis_size(axis)
    route = []
    for low in range(count):
        high = low | 1 << apart
        if high != low and high < count:
            route += [(low, high), (high, low)]
    return lax.ppermute(block, axis, route)


def per_device(
    hidden,
    query,
    new_kv,
    key_cache,
    value_cache,
    page_owner,
    page_fill,
    out_weight,
    norm_gain,
    gate_up,
    down,
    routes,
    route_weight,
):
    row_count = query.shape[0]
    group_count = lax.axis_size("grp")
    head_group = HEADS // KV_HEADS
    page_count = page_owner.shape[0]
    token_count = key_cache.shape[0]
    page_length = token_count // page_count
    both_rows = 2 * row_count
    scale = HD ** (-0.5)
    partner_query = from_partner(query, "grp", 0)
    feature_share = hidden.shape[1]
    layer_out, attn_out = layer_call(
        query, partner_query, key_cache, value_cache, page_owner.reshape(1, -1),
        page_fill.reshape(1, -1), new_kv.reshape(row_count, -1), out_weight, hidden, norm_gain.reshape(1, feature_share),
        routes, route_weight, gate_up[0], down[0],
    )
    return (layer_out, attn_out)


def solution(mesh):
    placed = (
        P("grp", "ep"),
        P("grp", None),
        P("grp", None, None),
        P(("grp", "ep"), None),
        P(("grp", "ep"), None),
        P(("grp", "ep")),
        P(("grp", "ep")),
        P("grp", "ep"),
        P("ep"),
        P("grp", None, None),
        P("grp", None, None),
        P("grp", None),
        P("grp", None),
    )
    return jax.shard_map(
        per_device,
        mesh=mesh,
        in_specs=placed,
        out_specs=(P("grp", "ep"), P("grp", None)),
        check_vma=False,
    )
```

```python
import jax
import jax.numpy as jnp
from jax import lax
from jax.experimental import pallas as pl
from jax.experimental.pallas import tpu as pltpu
from jax.sharding import PartitionSpec as P
import functools

D = 1536
HEADS = 24
KV_HEADS = 8
HD = 64
FF = 512
TOP = 8


masked_score = -1e30
norm_epsilon = 1e-05

MESH = pl.DeviceIdType.MESH


def layer_kernel(
    rows, n_ep, n_grp, width,
    query_ref, mate_query_ref, key_ref, value_ref, owner_ref, fill_ref,
    fresh_ref, block_ref, hidden_ref, gain_ref, routes_ref, route_weight_ref, up_ref, down_ref,
    out_ref, attn_ref,
    part_ref, own_ref, got, final, blocks, squares, outgoing, incoming, results, returned,
    s1, r1, s2, r2, s3, r3, s_sq, r_sq, s_out, r_in, s_res, r_ret,
):
    g = lax.axis_index("grp")
    e = lax.axis_index("ep")
    mate = g + 1 - 2 * (g % 2)
    home = g // 2
    serving = home == e
    share = width // n_ep
    barrier = pltpu.get_barrier_semaphore()
    for peer in range(n_ep):
        @pl.when(e != peer)
        def _():
            pl.semaphore_signal(barrier, inc=1, device_id=(g, peer), device_id_type=MESH)
            pl.semaphore_signal(barrier, inc=1, device_id=(g, peer), device_id_type=MESH)
        pl.semaphore_signal(barrier, inc=1, device_id=(mate, peer), device_id_type=MESH)
    for step in range(1, n_grp):
        pl.semaphore_signal(
            barrier, inc=1, device_id=(lax.rem(g + step, n_grp), e), device_id_type=MESH
        )
    for expert in range(n_grp):
        @pl.when(jnp.logical_not(serving & (g == expert)))
        def _():
            pl.semaphore_signal(barrier, inc=1, device_id=(expert, home), device_id_type=MESH)
    for half in range(2):
        for peer in range(n_ep):
            @pl.when(jnp.logical_not(serving & (g == 2 * e + half) & (e == peer)))
            def _():
                pl.semaphore_signal(
                    barrier, inc=1, device_id=(2 * e + half, peer), device_id_type=MESH
                )
    common = 2 * (n_ep - 1) + n_ep + n_grp - 1

    heads = width // HD
    both = 2 * rows
    pages = owner_ref.shape[1]
    tokens = key_ref.shape[0]
    kv_width = key_ref.shape[1]
    group_size = heads // (kv_width // HD)
    kv_lane = lax.broadcasted_iota(jnp.int32, (kv_width, width), 0)
    head_lane = lax.broadcasted_iota(jnp.int32, (kv_width, width), 1)
    widen = (
        (kv_lane % HD == head_lane % HD) & (kv_lane // HD == head_lane // (HD * group_size))
    ).astype(jnp.bfloat16)
    wide_keys = jnp.dot(key_ref[...], widen, preferred_element_type=jnp.float32).astype(jnp.bfloat16)
    wide_values = jnp.dot(value_ref[...], widen, preferred_element_type=jnp.float32).astype(jnp.bfloat16)
    fresh_keys = jnp.dot(
        fresh_ref[:, :kv_width], widen, preferred_element_type=jnp.float32).astype(jnp.bfloat16)
    fresh_values = jnp.dot(fresh_ref[:, kv_width:], widen, preferred_element_type=jnp.float32)
    page_length = tokens // pages
    queries = jnp.concatenate([query_ref[...], mate_query_ref[...]], 0)
    lane_head = lax.broadcasted_iota(jnp.int32, (both, width), 1) // HD
    stacked = jnp.concatenate(
        [jnp.where(lane_head == h, queries, jnp.zeros_like(queries)) for h in range(heads)], 0
    )
    row_of = lax.broadcasted_iota(jnp.int32, (both, pages), 0)
    owns = (owner_ref[...] == row_of).astype(jnp.float32)
    token_of = lax.broadcasted_iota(jnp.int32, (tokens, pages), 0)
    page_of = lax.broadcasted_iota(jnp.int32, (tokens, pages), 1)
    filled = (
        (token_of // page_length == page_of) & (token_of % page_length < fill_ref[...])
    ).astype(jnp.float32)
    usable = lax.dot_general(
        owns, filled, (((1,), (1,)), ((), ())), preferred_element_type=jnp.float32
    ) > 0.5
    usable = jnp.concatenate([usable] * heads, 0)
    scores = lax.dot_general(
        stacked, wide_keys, (((1,), (1,)), ((), ())), preferred_element_type=jnp.float32
    ) * (HD ** -0.5)
    own_scores = lax.dot_general(
        stacked, fresh_keys, (((1,), (1,)), ((), ())), preferred_element_type=jnp.float32
    ) * (HD ** -0.5)
    own_column = lax.broadcasted_iota(jnp.int32, own_scores.shape, 1)
    own_row = lax.broadcasted_iota(jnp.int32, own_scores.shape, 0) % both
    own_top = jnp.sum(jnp.where(own_column == own_row, own_scores, 0.0), 1, keepdims=True)
    local_top = jnp.max(jnp.where(usable, scores, masked_score), 1, keepdims=True)
    weights = jnp.where(usable, jnp.exp(scores - local_top), 0.0)
    local_total = jnp.sum(weights, 1, keepdims=True)
    local_accum = jnp.dot(
        weights.astype(jnp.bfloat16), wide_values, preferred_element_type=jnp.float32
    )
    accum_rows = jnp.zeros((both, width), jnp.float32)
    top_rows = jnp.zeros((both, width), jnp.float32)
    total_rows = jnp.zeros((both, width), jnp.float32)
    own_rows = jnp.zeros((both, width), jnp.float32)
    for h in range(heads):
        mine = lane_head == h
        block = slice(h * both, (h + 1) * both)
        accum_rows = jnp.where(mine, local_accum[block], accum_rows)
        top_rows = jnp.where(mine, jnp.broadcast_to(local_top[block], (both, width)), top_rows)
        total_rows = jnp.where(mine, jnp.broadcast_to(local_total[block], (both, width)), total_rows)
        own_rows = jnp.where(mine, jnp.broadcast_to(own_top[block], (both, width)), own_rows)
    for row in range(both):
        part_ref[row, 0:1, :] = accum_rows[row:row + 1]
        part_ref[row, 1:2, :] = top_rows[row:row + 1]
        part_ref[row, 2:3, :] = total_rows[row:row + 1]
    for row in range(rows):
        own_ref[row, 0:1, :] = fresh_values[row:row + 1]
        own_ref[row, 1:2, :] = own_rows[row:row + 1]
        own_ref[row, 2:3, :] = jnp.ones((1, width), jnp.float32)

    choices = routes_ref.shape[1]
    expert_of = lax.broadcasted_iota(jnp.int32, (rows, n_grp), 1)
    chosen = jnp.zeros((rows, n_grp), jnp.float32)
    weight_at = jnp.zeros((rows, n_grp), jnp.float32)
    for choice in range(choices):
        hit = routes_ref[:, choice:choice + 1] == expert_of
        chosen = chosen + hit.astype(jnp.float32)
        weight_at = weight_at + jnp.where(
            hit, route_weight_ref[:, choice:choice + 1].astype(jnp.float32), 0.0)
    earlier = (
        lax.broadcasted_iota(jnp.int32, (rows, rows), 1)
        < lax.broadcasted_iota(jnp.int32, (rows, rows), 0)
    ).astype(jnp.float32)
    position = jnp.dot(earlier, chosen, preferred_element_type=jnp.float32)
    slot_count = rows * n_grp
    spread_out = (
        lax.broadcasted_iota(jnp.int32, (n_grp, slot_count), 1) // rows
        == lax.broadcasted_iota(jnp.int32, (n_grp, slot_count), 0)
    ).astype(jnp.bfloat16)
    chosen_wide = jnp.dot(chosen.astype(jnp.bfloat16), spread_out, preferred_element_type=jnp.float32)
    position_wide = jnp.dot(position.astype(jnp.bfloat16), spread_out, preferred_element_type=jnp.float32)
    weight_wide = jnp.dot(weight_at.astype(jnp.bfloat16), spread_out, preferred_element_type=jnp.float32)
    slot_of = (lax.broadcasted_iota(jnp.int32, (rows, slot_count), 1) % rows).astype(jnp.float32)
    placed = (chosen_wide > 0.5) & (position_wide == slot_of)
    combine = jnp.where(placed, weight_wide, 0.0).astype(jnp.bfloat16)
    picker = jnp.transpose(placed.astype(jnp.float32)).astype(jnp.bfloat16)

    @pl.when(serving)
    def _():
        pl.semaphore_wait(barrier, common + n_grp - 1 + 2 * n_ep - 1)

    @pl.when(jnp.logical_not(serving))
    def _():
        pl.semaphore_wait(barrier, common + n_grp + 2 * n_ep)

    def first(row):
        if row < rows:
            target = (g, row)
            slot = e
        else:
            target = (mate, row - rows)
            slot = n_ep + e
        return pltpu.make_async_remote_copy(
            src_ref=part_ref.at[row], dst_ref=got.at[slot], send_sem=s1.at[row],
            recv_sem=r1.at[slot], device_id=target, device_id_type=MESH)

    for row in range(2 * rows):
        if row < rows:
            @pl.when(e != row)
            def _():
                first(row).start()

            @pl.when(e == row)
            def _():
                got[e] = part_ref[row]
        else:
            first(row).start()

    def spread(step):
        return pltpu.make_async_remote_copy(
            src_ref=block_ref, dst_ref=blocks.at[g], send_sem=s3.at[step],
            recv_sem=r3.at[g], device_id=(lax.rem(g + step, n_grp), e), device_id_type=MESH)

    def gathered_block(step):
        source = lax.rem(g + n_grp - step, n_grp)
        return pltpu.make_async_remote_copy(
            src_ref=block_ref, dst_ref=blocks.at[source], send_sem=s3.at[step],
            recv_sem=r3.at[source], device_id=(source, e), device_id_type=MESH)

    for step in range(1, n_grp):
        spread(step).start()
    blocks[g] = block_ref[...]

    def incoming_part(slot):
        return pltpu.make_async_remote_copy(
            src_ref=part_ref.at[0], dst_ref=got.at[slot], send_sem=s1.at[0],
            recv_sem=r1.at[slot], device_id=(g, 0), device_id_type=MESH)

    def second(target):
        return pltpu.make_async_remote_copy(
            src_ref=final.at[e], dst_ref=final.at[e], send_sem=s2.at[target],
            recv_sem=r2.at[e], device_id=(g, target), device_id_type=MESH)

    @pl.when(e < rows)
    def _():
        for slot in range(2 * n_ep):
            if slot < n_ep:
                @pl.when(e != slot)
                def _():
                    incoming_part(slot).wait_recv()
            else:
                incoming_part(slot).wait_recv()
        stack = got[...]
        own = own_ref[e]
        maxes = jnp.maximum(jnp.max(stack[:, 1:2, :], 0), own[1:2, :])
        factors = jnp.exp(stack[:, 1:2, :] - maxes[None])
        own_factor = jnp.exp(own[1:2, :] - maxes)
        total = jnp.sum(stack[:, 2:3, :] * factors, 0) + own_factor
        accum = jnp.sum(stack[:, 0:1, :] * factors, 0) + own[0:1, :] * own_factor
        final[e] = (accum / total).astype(jnp.bfloat16).astype(jnp.float32)
        for target in range(n_ep):
            @pl.when(e != target)
            def _():
                second(target).start()

    def arriving(row):
        return pltpu.make_async_remote_copy(
            src_ref=final.at[row], dst_ref=final.at[row], send_sem=s2.at[0],
            recv_sem=r2.at[row], device_id=(g, row), device_id_type=MESH)

    for row in range(rows):
        @pl.when(e != row)
        def _():
            arriving(row).wait_recv()

    row_ids = lax.broadcasted_iota(jnp.int32, (rows, width), 0)
    attn = jnp.zeros((rows, width), jnp.float32)
    for row in range(rows):
        attn = jnp.where(row_ids == row, jnp.broadcast_to(final[row], (rows, width)), attn)
    attn = attn.astype(jnp.bfloat16)
    attn_ref[...] = attn

    for step in range(1, n_grp):
        gathered_block(step).wait_recv()
    columns = blocks[...].reshape(n_grp * blocks.shape[1], share)
    projected = jnp.dot(attn, columns, preferred_element_type=jnp.float32)
    mixed = hidden_ref[...].astype(jnp.float32) + projected

    scaled = mixed * gain_ref[...]
    lanes = outgoing.shape[2]
    place = (
        lax.broadcasted_iota(jnp.int32, (share, lanes), 0)
        == lax.broadcasted_iota(jnp.int32, (share, lanes), 1)
    ).astype(jnp.float32)
    lane_of = lax.broadcasted_iota(jnp.int32, (rows, lanes), 1)
    carried = jnp.dot(
        scaled, place, precision=lax.Precision.HIGHEST, preferred_element_type=jnp.float32
    ) + jnp.where(lane_of == share, jnp.sum(mixed * mixed, axis=1, keepdims=True), 0.0)
    slots = outgoing.shape[1]
    picked = jnp.dot(
        picker.astype(jnp.float32), carried, precision=lax.Precision.HIGHEST,
        preferred_element_type=jnp.float32)
    outgoing[...] = picked.reshape(outgoing.shape)

    def dispatch(expert):
        return pltpu.make_async_remote_copy(
            src_ref=outgoing.at[expert], dst_ref=incoming.at[e, g % 2], send_sem=s_out.at[expert],
            recv_sem=r_in.at[g % 2, e], device_id=(expert, home), device_id_type=MESH)

    for expert in range(n_grp):
        @pl.when(jnp.logical_not(serving & (g == expert)))
        def _():
            dispatch(expert).start()

    @pl.when(serving)
    def _():
        incoming[e, g % 2] = outgoing[g]

    def gathered(half, peer):
        return pltpu.make_async_remote_copy(
            src_ref=outgoing.at[0], dst_ref=incoming.at[peer, half], send_sem=s_out.at[0],
            recv_sem=r_in.at[half, peer], device_id=(2 * e + half, peer), device_id_type=MESH)

    for half in range(2):
        for peer in range(n_ep):
            @pl.when(jnp.logical_not(serving & (g == 2 * e + half) & (e == peer)))
            def _():
                gathered(half, peer).wait_recv()

    arrived = incoming[...]
    row_total = jnp.sum(arrived[:, :, :, share:share + 1], 0)
    factor = lax.rsqrt(row_total / width + norm_epsilon)
    pre = jnp.zeros((2 * slots, up_ref.shape[1]), jnp.float32)
    for peer in range(n_ep):
        lhs = (arrived[peer][:, :, :share] * factor).astype(jnp.bfloat16).reshape(2 * slots, share)
        pre = pre + jnp.dot(
            lhs, up_ref[peer * share:(peer + 1) * share, :], preferred_element_type=jnp.float32)
    hidden_units = up_ref.shape[1] // 2
    gate = pre[:, :hidden_units]
    act = (gate / (1.0 + jnp.exp(-gate)) * pre[:, hidden_units:]).astype(jnp.bfloat16)
    for peer in range(n_ep):
        piece = jnp.dot(
            act, down_ref[:, peer * share:(peer + 1) * share], preferred_element_type=jnp.float32)
        results[peer] = piece.astype(jnp.bfloat16).astype(jnp.float32).reshape(results.shape[1:])

    def give_back(half, peer):
        return pltpu.make_async_remote_copy(
            src_ref=results.at[peer, half], dst_ref=returned.at[g], send_sem=s_res.at[half, peer],
            recv_sem=r_ret.at[g], device_id=(2 * e + half, peer), device_id_type=MESH)

    for half in range(2):
        for peer in range(n_ep):
            @pl.when(jnp.logical_not(serving & (g == 2 * e + half) & (e == peer)))
            def _():
                give_back(half, peer).start()

    @pl.when(serving)
    def _():
        returned[g] = results[e, g % 2]

    def coming_back(expert):
        return pltpu.make_async_remote_copy(
            src_ref=results.at[0, 0], dst_ref=returned.at[expert], send_sem=s_res.at[0, 0],
            recv_sem=r_ret.at[expert], device_id=(expert, home), device_id_type=MESH)

    for expert in range(n_grp):
        @pl.when(jnp.logical_not(serving & (g == expert)))
        def _():
            coming_back(expert).wait_recv()

    back = returned[...].reshape(n_grp * slots, share).astype(jnp.bfloat16)
    mix = jnp.dot(combine, back, preferred_element_type=jnp.float32)
    out_ref[...] = (mixed + mix).astype(out_ref.dtype)

    for row in range(2 * rows):
        if row < rows:
            @pl.when(e != row)
            def _():
                first(row).wait_send()
        else:
            first(row).wait_send()

    @pl.when(e < rows)
    def _():
        for target in range(n_ep):
            @pl.when(e != target)
            def _():
                second(target).wait_send()

    for step in range(1, n_grp):
        spread(step).wait_send()
    for expert in range(n_grp):
        @pl.when(jnp.logical_not(serving & (g == expert)))
        def _():
            dispatch(expert).wait_send()
    for half in range(2):
        for peer in range(n_ep):
            @pl.when(jnp.logical_not(serving & (g == 2 * e + half) & (e == peer)))
            def _():
                give_back(half, peer).wait_send()


def layer_call(query, mate_query, keys, values, owner, fill, fresh, block, hidden, gain, routes, route_weight, up, down):
    n_ep = lax.axis_size("ep")
    n_grp = lax.axis_size("grp")
    rows, share = hidden.shape
    width = share * n_ep
    slots = rows
    return pl.pallas_call(
        functools.partial(layer_kernel, rows, n_ep, n_grp, width),
        out_shape=(
            jax.ShapeDtypeStruct((rows, share), jnp.bfloat16),
            jax.ShapeDtypeStruct((rows, width), jnp.bfloat16),
        ),
        in_specs=[pl.BlockSpec(memory_space=pltpu.VMEM)] * 14,
        out_specs=(pl.BlockSpec(memory_space=pltpu.VMEM),) * 2,
        scratch_shapes=[
            pltpu.VMEM((2 * rows, 3, width), jnp.float32),
            pltpu.VMEM((rows, 3, width), jnp.float32),
            pltpu.VMEM((2 * n_ep, 3, width), jnp.float32),
            pltpu.VMEM((rows, 1, width), jnp.float32),
            pltpu.VMEM((n_grp,) + block.shape, block.dtype),
            pltpu.VMEM((n_ep, rows, 128), jnp.float32),
            pltpu.VMEM((n_grp, slots, 128), jnp.float32),
            pltpu.VMEM((n_ep, 2, slots, 128), jnp.float32),
            pltpu.VMEM((n_ep, 2, slots, share), jnp.float32),
            pltpu.VMEM((n_grp, slots, share), jnp.float32),
            pltpu.SemaphoreType.DMA((2 * rows,)),
            pltpu.SemaphoreType.DMA((2 * n_ep,)),
            pltpu.SemaphoreType.DMA((n_ep,)),
            pltpu.SemaphoreType.DMA((rows,)),
            pltpu.SemaphoreType.DMA((n_grp,)),
            pltpu.SemaphoreType.DMA((n_grp,)),
            pltpu.SemaphoreType.DMA((n_ep,)),
            pltpu.SemaphoreType.DMA((n_ep,)),
            pltpu.SemaphoreType.DMA((n_grp,)),
            pltpu.SemaphoreType.DMA((2, n_ep)),
            pltpu.SemaphoreType.DMA((2, n_ep)),
            pltpu.SemaphoreType.DMA((n_grp,)),
        ],
        compiler_params=pltpu.CompilerParams(collective_id=0, has_side_effects=True),
    )(query, mate_query, keys, values, owner, fill, fresh, block, hidden, gain, routes, route_weight, up, down)


def from_partner(block, axis, apart):
    count = lax.axis_size(axis)
    route = []
    for low in range(count):
        high = low | 1 << apart
        if high != low and high < count:
            route += [(low, high), (high, low)]
    return lax.ppermute(block, axis, route)


def per_device(
    hidden,
    query,
    new_kv,
    key_cache,
    value_cache,
    page_owner,
    page_fill,
    out_weight,
    norm_gain,
    gate_up,
    down,
    routes,
    route_weight,
):
    row_count = query.shape[0]
    group_count = lax.axis_size("grp")
    head_group = HEADS // KV_HEADS
    page_count = page_owner.shape[0]
    token_count = key_cache.shape[0]
    page_length = token_count // page_count
    both_rows = 2 * row_count
    scale = HD ** (-0.5)
    partner_query = from_partner(query, "grp", 0)
    feature_share = hidden.shape[1]
    layer_out, attn_out = layer_call(
        query, partner_query, key_cache, value_cache, page_owner.reshape(1, -1),
        page_fill.reshape(1, -1), new_kv.reshape(row_count, -1), out_weight, hidden, norm_gain.reshape(1, feature_share),
        routes, route_weight, gate_up[0], down[0],
    )
    return (layer_out, attn_out)


def solution(mesh):
    placed = (
        P("grp", "ep"),
        P("grp", None),
        P("grp", None, None),
        P(("grp", "ep"), None),
        P(("grp", "ep"), None),
        P(("grp", "ep")),
        P(("grp", "ep")),
        P("grp", "ep"),
        P("ep"),
        P("grp", None, None),
        P("grp", None, None),
        P("grp", None),
        P("grp", None),
    )
    return jax.shard_map(
        per_device,
        mesh=mesh,
        in_specs=placed,
        out_specs=(P("grp", "ep"), P("grp", None)),
        check_vma=False,
    )
```

```python
import jax
import jax.numpy as jnp
from jax import lax
from jax.experimental import pallas as pl
from jax.experimental.pallas import tpu as pltpu
from jax.sharding import PartitionSpec as P
import functools

D = 1536
HEADS = 24
KV_HEADS = 8
HD = 64
FF = 512
TOP = 8


masked_score = -1e30
norm_epsilon = 1e-05

MESH = pl.DeviceIdType.MESH


def layer_kernel(
    rows, n_ep, n_grp, width,
    query_ref, mate_query_ref, key_ref, value_ref, owner_ref, fill_ref,
    fresh_ref, block_ref, hidden_ref, gain_ref, routes_ref, route_weight_ref, up_ref, down_ref,
    out_ref, attn_ref,
    part_ref, own_ref, got, final, blocks, squares, outgoing, incoming, results, returned,
    s1, r1, s2, r2, s3, r3, s_sq, r_sq, s_out, r_in, s_res, r_ret,
):
    g = lax.axis_index("grp")
    e = lax.axis_index("ep")
    mate = g + 1 - 2 * (g % 2)
    home = g // 2
    serving = home == e
    share = width // n_ep
    barrier = pltpu.get_barrier_semaphore()
    for peer in range(n_ep):
        @pl.when(e != peer)
        def _():
            pl.semaphore_signal(barrier, inc=1, device_id=(g, peer), device_id_type=MESH)
            pl.semaphore_signal(barrier, inc=1, device_id=(g, peer), device_id_type=MESH)
        pl.semaphore_signal(barrier, inc=1, device_id=(mate, peer), device_id_type=MESH)
    for step in range(1, n_grp):
        pl.semaphore_signal(
            barrier, inc=1, device_id=(lax.rem(g + step, n_grp), e), device_id_type=MESH
        )
    for expert in range(n_grp):
        @pl.when(jnp.logical_not(serving & (g == expert)))
        def _():
            pl.semaphore_signal(barrier, inc=1, device_id=(expert, home), device_id_type=MESH)
    for half in range(2):
        for peer in range(n_ep):
            @pl.when(jnp.logical_not(serving & (g == 2 * e + half) & (e == peer)))
            def _():
                pl.semaphore_signal(
                    barrier, inc=1, device_id=(2 * e + half, peer), device_id_type=MESH
                )
    common = 2 * (n_ep - 1) + n_ep + n_grp - 1

    heads = width // HD
    both = 2 * rows
    pages = owner_ref.shape[1]
    tokens = key_ref.shape[0]
    kv_width = key_ref.shape[1]
    group_size = heads // (kv_width // HD)
    kv_lane = lax.broadcasted_iota(jnp.int32, (kv_width, width), 0)
    head_lane = lax.broadcasted_iota(jnp.int32, (kv_width, width), 1)
    widen = (
        (kv_lane % HD == head_lane % HD) & (kv_lane // HD == head_lane // (HD * group_size))
    ).astype(jnp.bfloat16)
    wide_keys = jnp.dot(key_ref[...], widen, preferred_element_type=jnp.float32).astype(jnp.bfloat16)
    wide_values = jnp.dot(value_ref[...], widen, preferred_element_type=jnp.float32).astype(jnp.bfloat16)
    fresh_keys = jnp.dot(
        fresh_ref[:, :kv_width], widen, preferred_element_type=jnp.float32).astype(jnp.bfloat16)
    fresh_values = jnp.dot(fresh_ref[:, kv_width:], widen, preferred_element_type=jnp.float32)
    page_length = tokens // pages
    queries = jnp.concatenate([query_ref[...], mate_query_ref[...]], 0)
    lane_head = lax.broadcasted_iota(jnp.int32, (both, width), 1) // HD
    stacked = jnp.concatenate(
        [jnp.where(lane_head == h, queries, jnp.zeros_like(queries)) for h in range(heads)], 0
    )
    row_of = lax.broadcasted_iota(jnp.int32, (both, pages), 0)
    owns = (owner_ref[...] == row_of).astype(jnp.float32)
    token_of = lax.broadcasted_iota(jnp.int32, (tokens, pages), 0)
    page_of = lax.broadcasted_iota(jnp.int32, (tokens, pages), 1)
    filled = (
        (token_of // page_length == page_of) & (token_of % page_length < fill_ref[...])
    ).astype(jnp.float32)
    usable = lax.dot_general(
        owns, filled, (((1,), (1,)), ((), ())), preferred_element_type=jnp.float32
    ) > 0.5
    usable = jnp.concatenate([usable] * heads, 0)
    scores = lax.dot_general(
        stacked, wide_keys, (((1,), (1,)), ((), ())), preferred_element_type=jnp.float32
    ) * (HD ** -0.5)
    own_scores = lax.dot_general(
        stacked, fresh_keys, (((1,), (1,)), ((), ())), preferred_element_type=jnp.float32
    ) * (HD ** -0.5)
    own_column = lax.broadcasted_iota(jnp.int32, own_scores.shape, 1)
    own_row = lax.broadcasted_iota(jnp.int32, own_scores.shape, 0) % both
    own_top = jnp.sum(jnp.where(own_column == own_row, own_scores, 0.0), 1, keepdims=True)
    local_top = jnp.max(jnp.where(usable, scores, masked_score), 1, keepdims=True)
    weights = jnp.where(usable, jnp.exp(scores - local_top), 0.0)
    local_total = jnp.sum(weights, 1, keepdims=True)
    local_accum = jnp.dot(
        weights.astype(jnp.bfloat16), wide_values, preferred_element_type=jnp.float32
    )
    accum_rows = jnp.zeros((both, width), jnp.float32)
    top_rows = jnp.zeros((both, width), jnp.float32)
    total_rows = jnp.zeros((both, width), jnp.float32)
    own_rows = jnp.zeros((both, width), jnp.float32)
    for h in range(heads):
        mine = lane_head == h
        block = slice(h * both, (h + 1) * both)
        accum_rows = jnp.where(mine, local_accum[block], accum_rows)
        top_rows = jnp.where(mine, jnp.broadcast_to(local_top[block], (both, width)), top_rows)
        total_rows = jnp.where(mine, jnp.broadcast_to(local_total[block], (both, width)), total_rows)
        own_rows = jnp.where(mine, jnp.broadcast_to(own_top[block], (both, width)), own_rows)
    for row in range(both):
        part_ref[row, 0:1, :] = accum_rows[row:row + 1]
        part_ref[row, 1:2, :] = top_rows[row:row + 1]
        part_ref[row, 2:3, :] = total_rows[row:row + 1]
    for row in range(rows):
        own_ref[row, 0:1, :] = fresh_values[row:row + 1]
        own_ref[row, 1:2, :] = own_rows[row:row + 1]
        own_ref[row, 2:3, :] = jnp.ones((1, width), jnp.float32)

    choices = routes_ref.shape[1]
    expert_of = lax.broadcasted_iota(jnp.int32, (rows, n_grp), 1)
    chosen = jnp.zeros((rows, n_grp), jnp.float32)
    weight_at = jnp.zeros((rows, n_grp), jnp.float32)
    for choice in range(choices):
        hit = routes_ref[:, choice:choice + 1] == expert_of
        chosen = chosen + hit.astype(jnp.float32)
        weight_at = weight_at + jnp.where(
            hit, route_weight_ref[:, choice:choice + 1].astype(jnp.float32), 0.0)
    earlier = (
        lax.broadcasted_iota(jnp.int32, (rows, rows), 1)
        < lax.broadcasted_iota(jnp.int32, (rows, rows), 0)
    ).astype(jnp.float32)
    position = jnp.dot(earlier, chosen, preferred_element_type=jnp.float32)
    slot_count = rows * n_grp
    spread_out = (
        lax.broadcasted_iota(jnp.int32, (n_grp, slot_count), 1) // rows
        == lax.broadcasted_iota(jnp.int32, (n_grp, slot_count), 0)
    ).astype(jnp.bfloat16)
    chosen_wide = jnp.dot(chosen.astype(jnp.bfloat16), spread_out, preferred_element_type=jnp.float32)
    position_wide = jnp.dot(position.astype(jnp.bfloat16), spread_out, preferred_element_type=jnp.float32)
    weight_wide = jnp.dot(weight_at.astype(jnp.bfloat16), spread_out, preferred_element_type=jnp.float32)
    slot_of = (lax.broadcasted_iota(jnp.int32, (rows, slot_count), 1) % rows).astype(jnp.float32)
    placed = (chosen_wide > 0.5) & (position_wide == slot_of)
    combine = jnp.where(placed, weight_wide, 0.0).astype(jnp.bfloat16)
    picker = jnp.transpose(placed.astype(jnp.float32)).astype(jnp.bfloat16)

    @pl.when(serving)
    def _():
        pl.semaphore_wait(barrier, common + n_grp - 1 + 2 * n_ep - 1)

    @pl.when(jnp.logical_not(serving))
    def _():
        pl.semaphore_wait(barrier, common + n_grp + 2 * n_ep)

    def first(row):
        if row < rows:
            target = (g, row)
            slot = e
        else:
            target = (mate, row - rows)
            slot = n_ep + e
        return pltpu.make_async_remote_copy(
            src_ref=part_ref.at[row], dst_ref=got.at[slot], send_sem=s1.at[row],
            recv_sem=r1.at[slot], device_id=target, device_id_type=MESH)

    for row in range(2 * rows):
        if row < rows:
            @pl.when(e != row)
            def _():
                first(row).start()

            @pl.when(e == row)
            def _():
                got[e] = part_ref[row]
        else:
            first(row).start()

    def spread(step):
        return pltpu.make_async_remote_copy(
            src_ref=block_ref, dst_ref=blocks.at[g], send_sem=s3.at[step],
            recv_sem=r3.at[g], device_id=(lax.rem(g + step, n_grp), e), device_id_type=MESH)

    def gathered_block(step):
        source = lax.rem(g + n_grp - step, n_grp)
        return pltpu.make_async_remote_copy(
            src_ref=block_ref, dst_ref=blocks.at[source], send_sem=s3.at[step],
            recv_sem=r3.at[source], device_id=(source, e), device_id_type=MESH)

    for step in range(1, n_grp):
        spread(step).start()
    blocks[g] = block_ref[...]

    def incoming_part(slot):
        return pltpu.make_async_remote_copy(
            src_ref=part_ref.at[0], dst_ref=got.at[slot], send_sem=s1.at[0],
            recv_sem=r1.at[slot], device_id=(g, 0), device_id_type=MESH)

    def second(target):
        return pltpu.make_async_remote_copy(
            src_ref=final.at[e], dst_ref=final.at[e], send_sem=s2.at[target],
            recv_sem=r2.at[e], device_id=(g, target), device_id_type=MESH)

    @pl.when(e < rows)
    def _():
        for slot in range(2 * n_ep):
            if slot < n_ep:
                @pl.when(e != slot)
                def _():
                    incoming_part(slot).wait_recv()
            else:
                incoming_part(slot).wait_recv()
        stack = got[...]
        own = own_ref[e]
        maxes = jnp.maximum(jnp.max(stack[:, 1:2, :], 0), own[1:2, :])
        factors = jnp.exp(stack[:, 1:2, :] - maxes[None])
        own_factor = jnp.exp(own[1:2, :] - maxes)
        total = jnp.sum(stack[:, 2:3, :] * factors, 0) + own_factor
        accum = jnp.sum(stack[:, 0:1, :] * factors, 0) + own[0:1, :] * own_factor
        final[e] = (accum / total).astype(jnp.bfloat16).astype(jnp.float32)
        for target in range(n_ep):
            @pl.when(e != target)
            def _():
                second(target).start()

    def arriving(row):
        return pltpu.make_async_remote_copy(
            src_ref=final.at[row], dst_ref=final.at[row], send_sem=s2.at[0],
            recv_sem=r2.at[row], device_id=(g, row), device_id_type=MESH)

    for row in range(rows):
        @pl.when(e != row)
        def _():
            arriving(row).wait_recv()

    row_ids = lax.broadcasted_iota(jnp.int32, (rows, width), 0)
    attn = jnp.zeros((rows, width), jnp.float32)
    for row in range(rows):
        attn = jnp.where(row_ids == row, jnp.broadcast_to(final[row], (rows, width)), attn)
    attn = attn.astype(jnp.bfloat16)
    attn_ref[...] = attn

    for step in range(1, n_grp):
        gathered_block(step).wait_recv()
    columns = blocks[...].reshape(n_grp * blocks.shape[1], share)
    projected = jnp.dot(attn, columns, preferred_element_type=jnp.float32)
    mixed = hidden_ref[...].astype(jnp.float32) + projected

    scaled = mixed * gain_ref[...]
    lanes = outgoing.shape[2]
    place = (
        lax.broadcasted_iota(jnp.int32, (share, lanes), 0)
        == lax.broadcasted_iota(jnp.int32, (share, lanes), 1)
    ).astype(jnp.float32)
    lane_of = lax.broadcasted_iota(jnp.int32, (rows, lanes), 1)
    carried = jnp.dot(
        scaled, place, precision=lax.Precision.HIGHEST, preferred_element_type=jnp.float32
    ) + jnp.where(lane_of == share, jnp.sum(mixed * mixed, axis=1, keepdims=True), 0.0)
    slots = outgoing.shape[1]
    picked = jnp.dot(
        picker.astype(jnp.float32), carried, precision=lax.Precision.HIGHEST,
        preferred_element_type=jnp.float32)
    outgoing[...] = picked.reshape(outgoing.shape)

    def dispatch(expert):
        return pltpu.make_async_remote_copy(
            src_ref=outgoing.at[expert], dst_ref=incoming.at[e, g % 2], send_sem=s_out.at[expert],
            recv_sem=r_in.at[g % 2, e], device_id=(expert, home), device_id_type=MESH)

    for expert in range(n_grp):
        @pl.when(jnp.logical_not(serving & (g == expert)))
        def _():
            dispatch(expert).start()

    @pl.when(serving)
    def _():
        incoming[e, g % 2] = outgoing[g]

    def gathered(half, peer):
        return pltpu.make_async_remote_copy(
            src_ref=outgoing.at[0], dst_ref=incoming.at[peer, half], send_sem=s_out.at[0],
            recv_sem=r_in.at[half, peer], device_id=(2 * e + half, peer), device_id_type=MESH)

    for half in range(2):
        for peer in range(n_ep):
            @pl.when(jnp.logical_not(serving & (g == 2 * e + half) & (e == peer)))
            def _():
                gathered(half, peer).wait_recv()

    arrived = incoming[...]
    row_total = jnp.sum(arrived[:, :, :, share:share + 1], 0)
    factor = lax.rsqrt(row_total / width + norm_epsilon)
    pre = jnp.zeros((2 * slots, up_ref.shape[1]), jnp.float32)
    for peer in range(n_ep):
        lhs = (arrived[peer][:, :, :share] * factor).astype(jnp.bfloat16).reshape(2 * slots, share)
        pre = pre + jnp.dot(
            lhs, up_ref[peer * share:(peer + 1) * share, :], preferred_element_type=jnp.float32)
    hidden_units = up_ref.shape[1] // 2
    gate = pre[:, :hidden_units]
    act = (gate / (1.0 + jnp.exp(-gate)) * pre[:, hidden_units:]).astype(jnp.bfloat16)
    for peer in range(n_ep):
        piece = jnp.dot(
            act, down_ref[:, peer * share:(peer + 1) * share], preferred_element_type=jnp.float32)
        results[peer] = piece.astype(jnp.bfloat16).astype(jnp.float32).reshape(results.shape[1:])

    def give_back(half, peer):
        return pltpu.make_async_remote_copy(
            src_ref=results.at[peer, half], dst_ref=returned.at[g], send_sem=s_res.at[half, peer],
            recv_sem=r_ret.at[g], device_id=(2 * e + half, peer), device_id_type=MESH)

    for half in range(2):
        for peer in range(n_ep):
            @pl.when(jnp.logical_not(serving & (g == 2 * e + half) & (e == peer)))
            def _():
                give_back(half, peer).start()

    @pl.when(serving)
    def _():
        returned[g] = results[e, g % 2]

    def coming_back(expert):
        return pltpu.make_async_remote_copy(
            src_ref=results.at[0, 0], dst_ref=returned.at[expert], send_sem=s_res.at[0, 0],
            recv_sem=r_ret.at[expert], device_id=(expert, home), device_id_type=MESH)

    for expert in range(n_grp):
        @pl.when(jnp.logical_not(serving & (g == expert)))
        def _():
            coming_back(expert).wait_recv()

    back = returned[...].reshape(n_grp * slots, share).astype(jnp.bfloat16)
    mix = jnp.dot(combine, back, preferred_element_type=jnp.float32)
    out_ref[...] = (mixed + mix).astype(out_ref.dtype)

    for row in range(2 * rows):
        if row < rows:
            @pl.when(e != row)
            def _():
                first(row).wait_send()
        else:
            first(row).wait_send()

    @pl.when(e < rows)
    def _():
        for target in range(n_ep):
            @pl.when(e != target)
            def _():
                second(target).wait_send()

    for step in range(1, n_grp):
        spread(step).wait_send()
    for expert in range(n_grp):
        @pl.when(jnp.logical_not(serving & (g == expert)))
        def _():
            dispatch(expert).wait_send()
    for half in range(2):
        for peer in range(n_ep):
            @pl.when(jnp.logical_not(serving & (g == 2 * e + half) & (e == peer)))
            def _():
                give_back(half, peer).wait_send()


def layer_call(query, mate_query, keys, values, owner, fill, fresh, block, hidden, gain, routes, route_weight, up, down):
    n_ep = lax.axis_size("ep")
    n_grp = lax.axis_size("grp")
    rows, share = hidden.shape
    width = share * n_ep
    slots = rows
    return pl.pallas_call(
        functools.partial(layer_kernel, rows, n_ep, n_grp, width),
        out_shape=(
            jax.ShapeDtypeStruct((rows, share), jnp.bfloat16),
            jax.ShapeDtypeStruct((rows, width), jnp.bfloat16),
        ),
        in_specs=[pl.BlockSpec(memory_space=pltpu.VMEM)] * 14,
        out_specs=(pl.BlockSpec(memory_space=pltpu.VMEM),) * 2,
        scratch_shapes=[
            pltpu.VMEM((2 * rows, 3, width), jnp.float32),
            pltpu.VMEM((rows, 3, width), jnp.float32),
            pltpu.VMEM((2 * n_ep, 3, width), jnp.float32),
            pltpu.VMEM((rows, 1, width), jnp.float32),
            pltpu.VMEM((n_grp,) + block.shape, block.dtype),
            pltpu.VMEM((n_ep, rows, 128), jnp.float32),
            pltpu.VMEM((n_grp, slots, 128), jnp.float32),
            pltpu.VMEM((n_ep, 2, slots, 128), jnp.float32),
            pltpu.VMEM((n_ep, 2, slots, share), jnp.float32),
            pltpu.VMEM((n_grp, slots, share), jnp.float32),
            pltpu.SemaphoreType.DMA((2 * rows,)),
            pltpu.SemaphoreType.DMA((2 * n_ep,)),
            pltpu.SemaphoreType.DMA((n_ep,)),
            pltpu.SemaphoreType.DMA((rows,)),
            pltpu.SemaphoreType.DMA((n_grp,)),
            pltpu.SemaphoreType.DMA((n_grp,)),
            pltpu.SemaphoreType.DMA((n_ep,)),
            pltpu.SemaphoreType.DMA((n_ep,)),
            pltpu.SemaphoreType.DMA((n_grp,)),
            pltpu.SemaphoreType.DMA((2, n_ep)),
            pltpu.SemaphoreType.DMA((2, n_ep)),
            pltpu.SemaphoreType.DMA((n_grp,)),
        ],
        compiler_params=pltpu.CompilerParams(collective_id=0, has_side_effects=True),
    )(query, mate_query, keys, values, owner, fill, fresh, block, hidden, gain, routes, route_weight, up, down)


def swap_kernel(query_ref, out_ref, held, send_sem, recv_sem):
    g = lax.axis_index("grp")
    e = lax.axis_index("ep")
    mate = g + 1 - 2 * (g % 2)
    barrier = pltpu.get_barrier_semaphore()
    pl.semaphore_signal(barrier, inc=1, device_id=(mate, e), device_id_type=MESH)
    pl.semaphore_wait(barrier, 1)
    copy = pltpu.make_async_remote_copy(
        src_ref=query_ref, dst_ref=held, send_sem=send_sem, recv_sem=recv_sem,
        device_id=(mate, e), device_id_type=MESH)
    copy.start()
    copy.wait()
    out_ref[...] = held[...]


def swap_call(query):
    return pl.pallas_call(
        swap_kernel,
        out_shape=jax.ShapeDtypeStruct(query.shape, query.dtype),
        in_specs=[pl.BlockSpec(memory_space=pltpu.VMEM)],
        out_specs=pl.BlockSpec(memory_space=pltpu.VMEM),
        scratch_shapes=[
            pltpu.VMEM(query.shape, query.dtype),
            pltpu.SemaphoreType.DMA(()),
            pltpu.SemaphoreType.DMA(()),
        ],
        compiler_params=pltpu.CompilerParams(collective_id=1, has_side_effects=True),
    )(query)


def from_partner(block, axis, apart):
    count = lax.axis_size(axis)
    route = []
    for low in range(count):
        high = low | 1 << apart
        if high != low and high < count:
            route += [(low, high), (high, low)]
    return lax.ppermute(block, axis, route)


def per_device(
    hidden,
    query,
    new_kv,
    key_cache,
    value_cache,
    page_owner,
    page_fill,
    out_weight,
    norm_gain,
    gate_up,
    down,
    routes,
    route_weight,
):
    row_count = query.shape[0]
    group_count = lax.axis_size("grp")
    head_group = HEADS // KV_HEADS
    page_count = page_owner.shape[0]
    token_count = key_cache.shape[0]
    page_length = token_count // page_count
    both_rows = 2 * row_count
    scale = HD ** (-0.5)
    partner_query = swap_call(query)
    feature_share = hidden.shape[1]
    layer_out, attn_out = layer_call(
        query, partner_query, key_cache, value_cache, page_owner.reshape(1, -1),
        page_fill.reshape(1, -1), new_kv.reshape(row_count, -1), out_weight, hidden, norm_gain.reshape(1, feature_share),
        routes, route_weight, gate_up[0], down[0],
    )
    return (layer_out, attn_out)


def solution(mesh):
    placed = (
        P("grp", "ep"),
        P("grp", None),
        P("grp", None, None),
        P(("grp", "ep"), None),
        P(("grp", "ep"), None),
        P(("grp", "ep")),
        P(("grp", "ep")),
        P("grp", "ep"),
        P("ep"),
        P("grp", None, None),
        P("grp", None, None),
        P("grp", None),
        P("grp", None),
    )
    return jax.shard_map(
        per_device,
        mesh=mesh,
        in_specs=placed,
        out_specs=(P("grp", "ep"), P("grp", None)),
        check_vma=False,
    )
```

```python
import jax
import jax.numpy as jnp
from jax import lax
from jax.experimental import pallas as pl
from jax.experimental.pallas import tpu as pltpu
from jax.sharding import PartitionSpec as P
import functools

D = 1536
HEADS = 24
KV_HEADS = 8
HD = 64
FF = 512
TOP = 8


masked_score = -1e30
norm_epsilon = 1e-05

MESH = pl.DeviceIdType.MESH


def layer_kernel(
    rows, n_ep, n_grp, width,
    query_ref, key_ref, value_ref, owner_ref, fill_ref,
    fresh_ref, block_ref, hidden_ref, gain_ref, routes_ref, route_weight_ref, up_ref, down_ref,
    out_ref, attn_ref,
    part_ref, own_ref, mate_query, s_q, r_q, got, final, blocks, squares, outgoing, incoming, results, returned,
    s1, r1, s2, r2, s3, r3, s_sq, r_sq, s_out, r_in, s_res, r_ret,
):
    g = lax.axis_index("grp")
    e = lax.axis_index("ep")
    mate = g + 1 - 2 * (g % 2)
    home = g // 2
    serving = home == e
    share = width // n_ep
    barrier = pltpu.get_barrier_semaphore()
    for peer in range(n_ep):
        @pl.when(e != peer)
        def _():
            pl.semaphore_signal(barrier, inc=1, device_id=(g, peer), device_id_type=MESH)
            pl.semaphore_signal(barrier, inc=1, device_id=(g, peer), device_id_type=MESH)
        pl.semaphore_signal(barrier, inc=1, device_id=(mate, peer), device_id_type=MESH)
    for step in range(1, n_grp):
        pl.semaphore_signal(
            barrier, inc=1, device_id=(lax.rem(g + step, n_grp), e), device_id_type=MESH
        )
    for expert in range(n_grp):
        @pl.when(jnp.logical_not(serving & (g == expert)))
        def _():
            pl.semaphore_signal(barrier, inc=1, device_id=(expert, home), device_id_type=MESH)
    for half in range(2):
        for peer in range(n_ep):
            @pl.when(jnp.logical_not(serving & (g == 2 * e + half) & (e == peer)))
            def _():
                pl.semaphore_signal(
                    barrier, inc=1, device_id=(2 * e + half, peer), device_id_type=MESH
                )
    common = 2 * (n_ep - 1) + n_ep + n_grp - 1

    heads = width // HD
    both = 2 * rows
    pages = owner_ref.shape[1]
    tokens = key_ref.shape[0]
    kv_width = key_ref.shape[1]
    group_size = heads // (kv_width // HD)
    kv_lane = lax.broadcasted_iota(jnp.int32, (kv_width, width), 0)
    head_lane = lax.broadcasted_iota(jnp.int32, (kv_width, width), 1)
    widen = (
        (kv_lane % HD == head_lane % HD) & (kv_lane // HD == head_lane // (HD * group_size))
    ).astype(jnp.bfloat16)
    wide_keys = jnp.dot(key_ref[...], widen, preferred_element_type=jnp.float32).astype(jnp.bfloat16)
    wide_values = jnp.dot(value_ref[...], widen, preferred_element_type=jnp.float32).astype(jnp.bfloat16)
    fresh_keys = jnp.dot(
        fresh_ref[:, :kv_width], widen, preferred_element_type=jnp.float32).astype(jnp.bfloat16)
    fresh_values = jnp.dot(fresh_ref[:, kv_width:], widen, preferred_element_type=jnp.float32)
    page_length = tokens // pages
    lane_head = lax.broadcasted_iota(jnp.int32, (rows, width), 1) // HD
    token_of = lax.broadcasted_iota(jnp.int32, (tokens, pages), 0)
    page_of = lax.broadcasted_iota(jnp.int32, (tokens, pages), 1)
    filled = (
        (token_of // page_length == page_of) & (token_of % page_length < fill_ref[...])
    ).astype(jnp.float32)

    def attend(queries, first_row):
        stacked = jnp.concatenate(
            [jnp.where(lane_head == h, queries.astype(jnp.float32), 0.0) for h in range(heads)], 0
        ).astype(jnp.bfloat16)
        row_of = lax.broadcasted_iota(jnp.int32, (rows, pages), 0) + first_row
        owns = (owner_ref[...] == row_of).astype(jnp.float32)
        usable = lax.dot_general(
            owns, filled, (((1,), (1,)), ((), ())), preferred_element_type=jnp.float32
        ) > 0.5
        usable = jnp.concatenate([usable] * heads, 0)
        scores = lax.dot_general(
            stacked, wide_keys, (((1,), (1,)), ((), ())), preferred_element_type=jnp.float32
        ) * (HD ** -0.5)
        local_top = jnp.max(jnp.where(usable, scores, masked_score), 1, keepdims=True)
        weights = jnp.where(usable, jnp.exp(scores - local_top), 0.0)
        local_total = jnp.sum(weights, 1, keepdims=True)
        local_accum = jnp.dot(
            weights.astype(jnp.bfloat16), wide_values, preferred_element_type=jnp.float32
        )
        accum_rows = jnp.zeros((rows, width), jnp.float32)
        top_rows = jnp.zeros((rows, width), jnp.float32)
        total_rows = jnp.zeros((rows, width), jnp.float32)
        for h in range(heads):
            mine = lane_head == h
            block = slice(h * rows, (h + 1) * rows)
            accum_rows = jnp.where(mine, local_accum[block], accum_rows)
            top_rows = jnp.where(mine, jnp.broadcast_to(local_top[block], (rows, width)), top_rows)
            total_rows = jnp.where(mine, jnp.broadcast_to(local_total[block], (rows, width)), total_rows)
        for row in range(rows):
            part_ref[first_row + row, 0:1, :] = accum_rows[row:row + 1]
            part_ref[first_row + row, 1:2, :] = top_rows[row:row + 1]
            part_ref[first_row + row, 2:3, :] = total_rows[row:row + 1]
        return stacked

    stacked = attend(query_ref[...], 0)
    own_scores = lax.dot_general(
        stacked, fresh_keys, (((1,), (1,)), ((), ())), preferred_element_type=jnp.float32
    ) * (HD ** -0.5)
    own_column = lax.broadcasted_iota(jnp.int32, own_scores.shape, 1)
    own_row = lax.broadcasted_iota(jnp.int32, own_scores.shape, 0) % rows
    own_top = jnp.sum(jnp.where(own_column == own_row, own_scores, 0.0), 1, keepdims=True)
    own_rows = jnp.zeros((rows, width), jnp.float32)
    for h in range(heads):
        own_rows = jnp.where(
            lane_head == h, jnp.broadcast_to(own_top[h * rows:(h + 1) * rows], (rows, width)), own_rows)
    for row in range(rows):
        own_ref[row, 0:1, :] = fresh_values[row:row + 1]
        own_ref[row, 1:2, :] = own_rows[row:row + 1]
        own_ref[row, 2:3, :] = jnp.ones((1, width), jnp.float32)

    choices = routes_ref.shape[1]
    expert_of = lax.broadcasted_iota(jnp.int32, (rows, n_grp), 1)
    chosen = jnp.zeros((rows, n_grp), jnp.float32)
    weight_at = jnp.zeros((rows, n_grp), jnp.float32)
    for choice in range(choices):
        hit = routes_ref[:, choice:choice + 1] == expert_of
        chosen = chosen + hit.astype(jnp.float32)
        weight_at = weight_at + jnp.where(
            hit, route_weight_ref[:, choice:choice + 1].astype(jnp.float32), 0.0)
    earlier = (
        lax.broadcasted_iota(jnp.int32, (rows, rows), 1)
        < lax.broadcasted_iota(jnp.int32, (rows, rows), 0)
    ).astype(jnp.float32)
    position = jnp.dot(earlier, chosen, preferred_element_type=jnp.float32)
    slot_count = rows * n_grp
    spread_out = (
        lax.broadcasted_iota(jnp.int32, (n_grp, slot_count), 1) // rows
        == lax.broadcasted_iota(jnp.int32, (n_grp, slot_count), 0)
    ).astype(jnp.bfloat16)
    chosen_wide = jnp.dot(chosen.astype(jnp.bfloat16), spread_out, preferred_element_type=jnp.float32)
    position_wide = jnp.dot(position.astype(jnp.bfloat16), spread_out, preferred_element_type=jnp.float32)
    weight_wide = jnp.dot(weight_at.astype(jnp.bfloat16), spread_out, preferred_element_type=jnp.float32)
    slot_of = (lax.broadcasted_iota(jnp.int32, (rows, slot_count), 1) % rows).astype(jnp.float32)
    placed = (chosen_wide > 0.5) & (position_wide == slot_of)
    combine = jnp.where(placed, weight_wide, 0.0).astype(jnp.bfloat16)
    picker = jnp.transpose(placed.astype(jnp.float32)).astype(jnp.bfloat16)

    @pl.when(serving)
    def _():
        pl.semaphore_wait(barrier, common + n_grp - 1 + 2 * n_ep - 1)

    @pl.when(jnp.logical_not(serving))
    def _():
        pl.semaphore_wait(barrier, common + n_grp + 2 * n_ep)

    def first(row):
        if row < rows:
            target = (g, row)
            slot = e
        else:
            target = (mate, row - rows)
            slot = n_ep + e
        return pltpu.make_async_remote_copy(
            src_ref=part_ref.at[row], dst_ref=got.at[slot], send_sem=s1.at[row],
            recv_sem=r1.at[slot], device_id=target, device_id_type=MESH)

    swap = pltpu.make_async_remote_copy(
        src_ref=query_ref, dst_ref=mate_query, send_sem=s_q, recv_sem=r_q,
        device_id=(mate, e), device_id_type=MESH)
    swap.start()
    for row in range(rows):
        @pl.when(e != row)
        def _():
            first(row).start()

        @pl.when(e == row)
        def _():
            got[e] = part_ref[row]

    def spread(step):
        return pltpu.make_async_remote_copy(
            src_ref=block_ref, dst_ref=blocks.at[g], send_sem=s3.at[step],
            recv_sem=r3.at[g], device_id=(lax.rem(g + step, n_grp), e), device_id_type=MESH)

    def gathered_block(step):
        source = lax.rem(g + n_grp - step, n_grp)
        return pltpu.make_async_remote_copy(
            src_ref=block_ref, dst_ref=blocks.at[source], send_sem=s3.at[step],
            recv_sem=r3.at[source], device_id=(source, e), device_id_type=MESH)

    for step in range(1, n_grp):
        spread(step).start()
    blocks[g] = block_ref[...]

    swap.wait()
    attend(mate_query[...], rows)
    for row in range(rows, 2 * rows):
        first(row).start()

    def incoming_part(slot):
        return pltpu.make_async_remote_copy(
            src_ref=part_ref.at[0], dst_ref=got.at[slot], send_sem=s1.at[0],
            recv_sem=r1.at[slot], device_id=(g, 0), device_id_type=MESH)

    def second(target):
        return pltpu.make_async_remote_copy(
            src_ref=final.at[e], dst_ref=final.at[e], send_sem=s2.at[target],
            recv_sem=r2.at[e], device_id=(g, target), device_id_type=MESH)

    @pl.when(e < rows)
    def _():
        for slot in range(2 * n_ep):
            if slot < n_ep:
                @pl.when(e != slot)
                def _():
                    incoming_part(slot).wait_recv()
            else:
                incoming_part(slot).wait_recv()
        stack = got[...]
        own = own_ref[e]
        maxes = jnp.maximum(jnp.max(stack[:, 1:2, :], 0), own[1:2, :])
        factors = jnp.exp(stack[:, 1:2, :] - maxes[None])
        own_factor = jnp.exp(own[1:2, :] - maxes)
        total = jnp.sum(stack[:, 2:3, :] * factors, 0) + own_factor
        accum = jnp.sum(stack[:, 0:1, :] * factors, 0) + own[0:1, :] * own_factor
        final[e] = (accum / total).astype(jnp.bfloat16).astype(jnp.float32)
        for target in range(n_ep):
            @pl.when(e != target)
            def _():
                second(target).start()

    def arriving(row):
        return pltpu.make_async_remote_copy(
            src_ref=final.at[row], dst_ref=final.at[row], send_sem=s2.at[0],
            recv_sem=r2.at[row], device_id=(g, row), device_id_type=MESH)

    for row in range(rows):
        @pl.when(e != row)
        def _():
            arriving(row).wait_recv()

    row_ids = lax.broadcasted_iota(jnp.int32, (rows, width), 0)
    attn = jnp.zeros((rows, width), jnp.float32)
    for row in range(rows):
        attn = jnp.where(row_ids == row, jnp.broadcast_to(final[row], (rows, width)), attn)
    attn = attn.astype(jnp.bfloat16)
    attn_ref[...] = attn

    for step in range(1, n_grp):
        gathered_block(step).wait_recv()
    columns = blocks[...].reshape(n_grp * blocks.shape[1], share)
    projected = jnp.dot(attn, columns, preferred_element_type=jnp.float32)
    mixed = hidden_ref[...].astype(jnp.float32) + projected

    scaled = mixed * gain_ref[...]
    lanes = outgoing.shape[2]
    place = (
        lax.broadcasted_iota(jnp.int32, (share, lanes), 0)
        == lax.broadcasted_iota(jnp.int32, (share, lanes), 1)
    ).astype(jnp.float32)
    lane_of = lax.broadcasted_iota(jnp.int32, (rows, lanes), 1)
    carried = jnp.dot(
        scaled, place, precision=lax.Precision.HIGHEST, preferred_element_type=jnp.float32
    ) + jnp.where(lane_of == share, jnp.sum(mixed * mixed, axis=1, keepdims=True), 0.0)
    slots = outgoing.shape[1]
    picked = jnp.dot(
        picker.astype(jnp.float32), carried, precision=lax.Precision.HIGHEST,
        preferred_element_type=jnp.float32)
    outgoing[...] = picked.reshape(outgoing.shape)

    def dispatch(expert):
        return pltpu.make_async_remote_copy(
            src_ref=outgoing.at[expert], dst_ref=incoming.at[e, g % 2], send_sem=s_out.at[expert],
            recv_sem=r_in.at[g % 2, e], device_id=(expert, home), device_id_type=MESH)

    for expert in range(n_grp):
        @pl.when(jnp.logical_not(serving & (g == expert)))
        def _():
            dispatch(expert).start()

    @pl.when(serving)
    def _():
        incoming[e, g % 2] = outgoing[g]

    def gathered(half, peer):
        return pltpu.make_async_remote_copy(
            src_ref=outgoing.at[0], dst_ref=incoming.at[peer, half], send_sem=s_out.at[0],
            recv_sem=r_in.at[half, peer], device_id=(2 * e + half, peer), device_id_type=MESH)

    for half in range(2):
        for peer in range(n_ep):
            @pl.when(jnp.logical_not(serving & (g == 2 * e + half) & (e == peer)))
            def _():
                gathered(half, peer).wait_recv()

    arrived = incoming[...]
    row_total = jnp.sum(arrived[:, :, :, share:share + 1], 0)
    factor = lax.rsqrt(row_total / width + norm_epsilon)
    pre = jnp.zeros((2 * slots, up_ref.shape[1]), jnp.float32)
    for peer in range(n_ep):
        lhs = (arrived[peer][:, :, :share] * factor).astype(jnp.bfloat16).reshape(2 * slots, share)
        pre = pre + jnp.dot(
            lhs, up_ref[peer * share:(peer + 1) * share, :], preferred_element_type=jnp.float32)
    hidden_units = up_ref.shape[1] // 2
    gate = pre[:, :hidden_units]
    act = (gate / (1.0 + jnp.exp(-gate)) * pre[:, hidden_units:]).astype(jnp.bfloat16)
    for peer in range(n_ep):
        piece = jnp.dot(
            act, down_ref[:, peer * share:(peer + 1) * share], preferred_element_type=jnp.float32)
        results[peer] = piece.astype(jnp.bfloat16).astype(jnp.float32).reshape(results.shape[1:])

    def give_back(half, peer):
        return pltpu.make_async_remote_copy(
            src_ref=results.at[peer, half], dst_ref=returned.at[g], send_sem=s_res.at[half, peer],
            recv_sem=r_ret.at[g], device_id=(2 * e + half, peer), device_id_type=MESH)

    for half in range(2):
        for peer in range(n_ep):
            @pl.when(jnp.logical_not(serving & (g == 2 * e + half) & (e == peer)))
            def _():
                give_back(half, peer).start()

    @pl.when(serving)
    def _():
        returned[g] = results[e, g % 2]

    def coming_back(expert):
        return pltpu.make_async_remote_copy(
            src_ref=results.at[0, 0], dst_ref=returned.at[expert], send_sem=s_res.at[0, 0],
            recv_sem=r_ret.at[expert], device_id=(expert, home), device_id_type=MESH)

    for expert in range(n_grp):
        @pl.when(jnp.logical_not(serving & (g == expert)))
        def _():
            coming_back(expert).wait_recv()

    back = returned[...].reshape(n_grp * slots, share).astype(jnp.bfloat16)
    mix = jnp.dot(combine, back, preferred_element_type=jnp.float32)
    out_ref[...] = (mixed + mix).astype(out_ref.dtype)

    for row in range(2 * rows):
        if row < rows:
            @pl.when(e != row)
            def _():
                first(row).wait_send()
        else:
            first(row).wait_send()

    @pl.when(e < rows)
    def _():
        for target in range(n_ep):
            @pl.when(e != target)
            def _():
                second(target).wait_send()

    for step in range(1, n_grp):
        spread(step).wait_send()
    for expert in range(n_grp):
        @pl.when(jnp.logical_not(serving & (g == expert)))
        def _():
            dispatch(expert).wait_send()
    for half in range(2):
        for peer in range(n_ep):
            @pl.when(jnp.logical_not(serving & (g == 2 * e + half) & (e == peer)))
            def _():
                give_back(half, peer).wait_send()


def layer_call(query, keys, values, owner, fill, fresh, block, hidden, gain, routes, route_weight, up, down):
    n_ep = lax.axis_size("ep")
    n_grp = lax.axis_size("grp")
    rows, share = hidden.shape
    width = share * n_ep
    slots = rows
    return pl.pallas_call(
        functools.partial(layer_kernel, rows, n_ep, n_grp, width),
        out_shape=(
            jax.ShapeDtypeStruct((rows, share), jnp.bfloat16),
            jax.ShapeDtypeStruct((rows, width), jnp.bfloat16),
        ),
        in_specs=[pl.BlockSpec(memory_space=pltpu.VMEM)] * 13,
        out_specs=(pl.BlockSpec(memory_space=pltpu.VMEM),) * 2,
        scratch_shapes=[
            pltpu.VMEM((2 * rows, 3, width), jnp.float32),
            pltpu.VMEM((rows, 3, width), jnp.float32),
            pltpu.VMEM((rows, width), jnp.bfloat16),
            pltpu.SemaphoreType.DMA(()),
            pltpu.SemaphoreType.DMA(()),
            pltpu.VMEM((2 * n_ep, 3, width), jnp.float32),
            pltpu.VMEM((rows, 1, width), jnp.float32),
            pltpu.VMEM((n_grp,) + block.shape, block.dtype),
            pltpu.VMEM((n_ep, rows, 128), jnp.float32),
            pltpu.VMEM((n_grp, slots, 128), jnp.float32),
            pltpu.VMEM((n_ep, 2, slots, 128), jnp.float32),
            pltpu.VMEM((n_ep, 2, slots, share), jnp.float32),
            pltpu.VMEM((n_grp, slots, share), jnp.float32),
            pltpu.SemaphoreType.DMA((2 * rows,)),
            pltpu.SemaphoreType.DMA((2 * n_ep,)),
            pltpu.SemaphoreType.DMA((n_ep,)),
            pltpu.SemaphoreType.DMA((rows,)),
            pltpu.SemaphoreType.DMA((n_grp,)),
            pltpu.SemaphoreType.DMA((n_grp,)),
            pltpu.SemaphoreType.DMA((n_ep,)),
            pltpu.SemaphoreType.DMA((n_ep,)),
            pltpu.SemaphoreType.DMA((n_grp,)),
            pltpu.SemaphoreType.DMA((2, n_ep)),
            pltpu.SemaphoreType.DMA((2, n_ep)),
            pltpu.SemaphoreType.DMA((n_grp,)),
        ],
        compiler_params=pltpu.CompilerParams(collective_id=0, has_side_effects=True),
    )(query, keys, values, owner, fill, fresh, block, hidden, gain, routes, route_weight, up, down)


def swap_kernel(query_ref, out_ref, held, send_sem, recv_sem):
    g = lax.axis_index("grp")
    e = lax.axis_index("ep")
    mate = g + 1 - 2 * (g % 2)
    barrier = pltpu.get_barrier_semaphore()
    pl.semaphore_signal(barrier, inc=1, device_id=(mate, e), device_id_type=MESH)
    pl.semaphore_wait(barrier, 1)
    copy = pltpu.make_async_remote_copy(
        src_ref=query_ref, dst_ref=held, send_sem=send_sem, recv_sem=recv_sem,
        device_id=(mate, e), device_id_type=MESH)
    copy.start()
    copy.wait()
    out_ref[...] = held[...]


def swap_call(query):
    return pl.pallas_call(
        swap_kernel,
        out_shape=jax.ShapeDtypeStruct(query.shape, query.dtype),
        in_specs=[pl.BlockSpec(memory_space=pltpu.VMEM)],
        out_specs=pl.BlockSpec(memory_space=pltpu.VMEM),
        scratch_shapes=[
            pltpu.VMEM(query.shape, query.dtype),
            pltpu.SemaphoreType.DMA(()),
            pltpu.SemaphoreType.DMA(()),
        ],
        compiler_params=pltpu.CompilerParams(collective_id=1, has_side_effects=True),
    )(query)


def from_partner(block, axis, apart):
    count = lax.axis_size(axis)
    route = []
    for low in range(count):
        high = low | 1 << apart
        if high != low and high < count:
            route += [(low, high), (high, low)]
    return lax.ppermute(block, axis, route)


def per_device(
    hidden,
    query,
    new_kv,
    key_cache,
    value_cache,
    page_owner,
    page_fill,
    out_weight,
    norm_gain,
    gate_up,
    down,
    routes,
    route_weight,
):
    row_count = query.shape[0]
    group_count = lax.axis_size("grp")
    head_group = HEADS // KV_HEADS
    page_count = page_owner.shape[0]
    token_count = key_cache.shape[0]
    page_length = token_count // page_count
    both_rows = 2 * row_count
    scale = HD ** (-0.5)
    feature_share = hidden.shape[1]
    layer_out, attn_out = layer_call(
        query, key_cache, value_cache, page_owner.reshape(1, -1),
        page_fill.reshape(1, -1), new_kv.reshape(row_count, -1), out_weight, hidden, norm_gain.reshape(1, feature_share),
        routes, route_weight, gate_up[0], down[0],
    )
    return (layer_out, attn_out)


def solution(mesh):
    placed = (
        P("grp", "ep"),
        P("grp", None),
        P("grp", None, None),
        P(("grp", "ep"), None),
        P(("grp", "ep"), None),
        P(("grp", "ep")),
        P(("grp", "ep")),
        P("grp", "ep"),
        P("ep"),
        P("grp", None, None),
        P("grp", None, None),
        P("grp", None),
        P("grp", None),
    )
    return jax.shard_map(
        per_device,
        mesh=mesh,
        in_specs=placed,
        out_specs=(P("grp", "ep"), P("grp", None)),
        check_vma=False,
    )
```

```python
import jax
import jax.numpy as jnp
from jax import lax
from jax.experimental import pallas as pl
from jax.experimental.pallas import tpu as pltpu
from jax.sharding import PartitionSpec as P
import functools

D = 1536
HEADS = 24
KV_HEADS = 8
HD = 64
FF = 512
TOP = 8


masked_score = -1e30
norm_epsilon = 1e-05

MESH = pl.DeviceIdType.MESH


def layer_kernel(
    rows, n_ep, n_grp, width,
    query_ref, key_ref, value_ref, owner_ref, fill_ref,
    fresh_ref, block_ref, hidden_ref, gain_ref, routes_ref, route_weight_ref, up_ref, down_ref,
    out_ref, attn_ref,
    part_ref, own_ref, mate_query, s_q, r_q, got, final, blocks, squares, outgoing, incoming, results, returned,
    s1, r1, s2, r2, s3, r3, s_sq, r_sq, s_out, r_in, s_res, r_ret,
):
    g = lax.axis_index("grp")
    e = lax.axis_index("ep")
    mate = g + 1 - 2 * (g % 2)
    home = g // 2
    serving = home == e
    share = width // n_ep
    barrier = pltpu.get_barrier_semaphore()
    for peer in range(n_ep):
        @pl.when(e != peer)
        def _():
            pl.semaphore_signal(barrier, inc=1, device_id=(g, peer), device_id_type=MESH)
            pl.semaphore_signal(barrier, inc=1, device_id=(g, peer), device_id_type=MESH)
        pl.semaphore_signal(barrier, inc=1, device_id=(mate, peer), device_id_type=MESH)
    for step in range(1, n_grp):
        pl.semaphore_signal(
            barrier, inc=1, device_id=(lax.rem(g + step, n_grp), e), device_id_type=MESH
        )
    for expert in range(n_grp):
        @pl.when(jnp.logical_not(serving & (g == expert)))
        def _():
            pl.semaphore_signal(barrier, inc=1, device_id=(expert, home), device_id_type=MESH)
    for half in range(2):
        for peer in range(n_ep):
            @pl.when(jnp.logical_not(serving & (g == 2 * e + half) & (e == peer)))
            def _():
                pl.semaphore_signal(
                    barrier, inc=1, device_id=(2 * e + half, peer), device_id_type=MESH
                )
    common = 2 * (n_ep - 1) + n_ep + n_grp - 1

    heads = width // HD
    both = 2 * rows
    pages = owner_ref.shape[1]
    tokens = key_ref.shape[0]
    kv_width = key_ref.shape[1]
    group_size = heads // (kv_width // HD)
    kv_lane = lax.broadcasted_iota(jnp.int32, (kv_width, width), 0)
    head_lane = lax.broadcasted_iota(jnp.int32, (kv_width, width), 1)
    widen = (
        (kv_lane % HD == head_lane % HD) & (kv_lane // HD == head_lane // (HD * group_size))
    ).astype(jnp.bfloat16)
    wide_keys = jnp.dot(key_ref[...], widen, preferred_element_type=jnp.float32).astype(jnp.bfloat16)
    wide_values = jnp.dot(value_ref[...], widen, preferred_element_type=jnp.float32).astype(jnp.bfloat16)
    fresh_keys = jnp.dot(
        fresh_ref[:, 0, :], widen, preferred_element_type=jnp.float32).astype(jnp.bfloat16)
    fresh_values = jnp.dot(fresh_ref[:, 1, :], widen, preferred_element_type=jnp.float32)
    page_length = tokens // pages
    lane_head = lax.broadcasted_iota(jnp.int32, (rows, width), 1) // HD
    token_of = lax.broadcasted_iota(jnp.int32, (tokens, pages), 0)
    page_of = lax.broadcasted_iota(jnp.int32, (tokens, pages), 1)
    filled = (
        (token_of // page_length == page_of) & (token_of % page_length < fill_ref[...])
    ).astype(jnp.float32)

    def attend(queries, first_row):
        stacked = jnp.concatenate(
            [jnp.where(lane_head == h, queries.astype(jnp.float32), 0.0) for h in range(heads)], 0
        ).astype(jnp.bfloat16)
        row_of = lax.broadcasted_iota(jnp.int32, (rows, pages), 0) + first_row
        owns = (owner_ref[...] == row_of).astype(jnp.float32)
        usable = lax.dot_general(
            owns, filled, (((1,), (1,)), ((), ())), preferred_element_type=jnp.float32
        ) > 0.5
        usable = jnp.concatenate([usable] * heads, 0)
        scores = lax.dot_general(
            stacked, wide_keys, (((1,), (1,)), ((), ())), preferred_element_type=jnp.float32
        ) * (HD ** -0.5)
        local_top = jnp.max(jnp.where(usable, scores, masked_score), 1, keepdims=True)
        weights = jnp.where(usable, jnp.exp(scores - local_top), 0.0)
        local_total = jnp.sum(weights, 1, keepdims=True)
        local_accum = jnp.dot(
            weights.astype(jnp.bfloat16), wide_values, preferred_element_type=jnp.float32
        )
        accum_rows = jnp.zeros((rows, width), jnp.float32)
        top_rows = jnp.zeros((rows, width), jnp.float32)
        total_rows = jnp.zeros((rows, width), jnp.float32)
        for h in range(heads):
            mine = lane_head == h
            block = slice(h * rows, (h + 1) * rows)
            accum_rows = jnp.where(mine, local_accum[block], accum_rows)
            top_rows = jnp.where(mine, jnp.broadcast_to(local_top[block], (rows, width)), top_rows)
            total_rows = jnp.where(mine, jnp.broadcast_to(local_total[block], (rows, width)), total_rows)
        for row in range(rows):
            part_ref[first_row + row, 0:1, :] = accum_rows[row:row + 1]
            part_ref[first_row + row, 1:2, :] = top_rows[row:row + 1]
            part_ref[first_row + row, 2:3, :] = total_rows[row:row + 1]
        return stacked

    stacked = attend(query_ref[...], 0)
    own_scores = lax.dot_general(
        stacked, fresh_keys, (((1,), (1,)), ((), ())), preferred_element_type=jnp.float32
    ) * (HD ** -0.5)
    own_column = lax.broadcasted_iota(jnp.int32, own_scores.shape, 1)
    own_row = lax.broadcasted_iota(jnp.int32, own_scores.shape, 0) % rows
    own_top = jnp.sum(jnp.where(own_column == own_row, own_scores, 0.0), 1, keepdims=True)
    own_rows = jnp.zeros((rows, width), jnp.float32)
    for h in range(heads):
        own_rows = jnp.where(
            lane_head == h, jnp.broadcast_to(own_top[h * rows:(h + 1) * rows], (rows, width)), own_rows)
    for row in range(rows):
        own_ref[row, 0:1, :] = fresh_values[row:row + 1]
        own_ref[row, 1:2, :] = own_rows[row:row + 1]
        own_ref[row, 2:3, :] = jnp.ones((1, width), jnp.float32)

    choices = routes_ref.shape[1]
    expert_of = lax.broadcasted_iota(jnp.int32, (rows, n_grp), 1)
    chosen = jnp.zeros((rows, n_grp), jnp.float32)
    weight_at = jnp.zeros((rows, n_grp), jnp.float32)
    for choice in range(choices):
        hit = routes_ref[:, choice:choice + 1] == expert_of
        chosen = chosen + hit.astype(jnp.float32)
        weight_at = weight_at + jnp.where(
            hit, route_weight_ref[:, choice:choice + 1].astype(jnp.float32), 0.0)
    earlier = (
        lax.broadcasted_iota(jnp.int32, (rows, rows), 1)
        < lax.broadcasted_iota(jnp.int32, (rows, rows), 0)
    ).astype(jnp.float32)
    position = jnp.dot(earlier, chosen, preferred_element_type=jnp.float32)
    slot_count = rows * n_grp
    spread_out = (
        lax.broadcasted_iota(jnp.int32, (n_grp, slot_count), 1) // rows
        == lax.broadcasted_iota(jnp.int32, (n_grp, slot_count), 0)
    ).astype(jnp.bfloat16)
    chosen_wide = jnp.dot(chosen.astype(jnp.bfloat16), spread_out, preferred_element_type=jnp.float32)
    position_wide = jnp.dot(position.astype(jnp.bfloat16), spread_out, preferred_element_type=jnp.float32)
    weight_wide = jnp.dot(weight_at.astype(jnp.bfloat16), spread_out, preferred_element_type=jnp.float32)
    slot_of = (lax.broadcasted_iota(jnp.int32, (rows, slot_count), 1) % rows).astype(jnp.float32)
    placed = (chosen_wide > 0.5) & (position_wide == slot_of)
    combine = jnp.where(placed, weight_wide, 0.0).astype(jnp.bfloat16)
    picker = jnp.transpose(placed.astype(jnp.float32)).astype(jnp.bfloat16)

    @pl.when(serving)
    def _():
        pl.semaphore_wait(barrier, common + n_grp - 1 + 2 * n_ep - 1)

    @pl.when(jnp.logical_not(serving))
    def _():
        pl.semaphore_wait(barrier, common + n_grp + 2 * n_ep)

    def first(row):
        if row < rows:
            target = (g, row)
            slot = e
        else:
            target = (mate, row - rows)
            slot = n_ep + e
        return pltpu.make_async_remote_copy(
            src_ref=part_ref.at[row], dst_ref=got.at[slot], send_sem=s1.at[row],
            recv_sem=r1.at[slot], device_id=target, device_id_type=MESH)

    swap = pltpu.make_async_remote_copy(
        src_ref=query_ref, dst_ref=mate_query, send_sem=s_q, recv_sem=r_q,
        device_id=(mate, e), device_id_type=MESH)
    swap.start()
    for row in range(rows):
        @pl.when(e != row)
        def _():
            first(row).start()

        @pl.when(e == row)
        def _():
            got[e] = part_ref[row]

    def spread(step):
        return pltpu.make_async_remote_copy(
            src_ref=block_ref, dst_ref=blocks.at[g], send_sem=s3.at[step],
            recv_sem=r3.at[g], device_id=(lax.rem(g + step, n_grp), e), device_id_type=MESH)

    def gathered_block(step):
        source = lax.rem(g + n_grp - step, n_grp)
        return pltpu.make_async_remote_copy(
            src_ref=block_ref, dst_ref=blocks.at[source], send_sem=s3.at[step],
            recv_sem=r3.at[source], device_id=(source, e), device_id_type=MESH)

    for step in range(1, n_grp):
        spread(step).start()
    blocks[g] = block_ref[...]

    swap.wait()
    attend(mate_query[...], rows)
    for row in range(rows, 2 * rows):
        first(row).start()

    def incoming_part(slot):
        return pltpu.make_async_remote_copy(
            src_ref=part_ref.at[0], dst_ref=got.at[slot], send_sem=s1.at[0],
            recv_sem=r1.at[slot], device_id=(g, 0), device_id_type=MESH)

    def second(target):
        return pltpu.make_async_remote_copy(
            src_ref=final.at[e], dst_ref=final.at[e], send_sem=s2.at[target],
            recv_sem=r2.at[e], device_id=(g, target), device_id_type=MESH)

    @pl.when(e < rows)
    def _():
        for slot in range(2 * n_ep):
            if slot < n_ep:
                @pl.when(e != slot)
                def _():
                    incoming_part(slot).wait_recv()
            else:
                incoming_part(slot).wait_recv()
        stack = got[...]
        own = own_ref[e]
        maxes = jnp.maximum(jnp.max(stack[:, 1:2, :], 0), own[1:2, :])
        factors = jnp.exp(stack[:, 1:2, :] - maxes[None])
        own_factor = jnp.exp(own[1:2, :] - maxes)
        total = jnp.sum(stack[:, 2:3, :] * factors, 0) + own_factor
        accum = jnp.sum(stack[:, 0:1, :] * factors, 0) + own[0:1, :] * own_factor
        final[e] = (accum / total).astype(jnp.bfloat16).astype(jnp.float32)
        for target in range(n_ep):
            @pl.when(e != target)
            def _():
                second(target).start()

    def arriving(row):
        return pltpu.make_async_remote_copy(
            src_ref=final.at[row], dst_ref=final.at[row], send_sem=s2.at[0],
            recv_sem=r2.at[row], device_id=(g, row), device_id_type=MESH)

    for row in range(rows):
        @pl.when(e != row)
        def _():
            arriving(row).wait_recv()

    row_ids = lax.broadcasted_iota(jnp.int32, (rows, width), 0)
    attn = jnp.zeros((rows, width), jnp.float32)
    for row in range(rows):
        attn = jnp.where(row_ids == row, jnp.broadcast_to(final[row], (rows, width)), attn)
    attn = attn.astype(jnp.bfloat16)
    attn_ref[...] = attn

    for step in range(1, n_grp):
        gathered_block(step).wait_recv()
    columns = blocks[...].reshape(n_grp * blocks.shape[1], share)
    projected = jnp.dot(attn, columns, preferred_element_type=jnp.float32)
    mixed = hidden_ref[...].astype(jnp.float32) + projected

    scaled = mixed * gain_ref[...]
    lanes = outgoing.shape[2]
    place = (
        lax.broadcasted_iota(jnp.int32, (share, lanes), 0)
        == lax.broadcasted_iota(jnp.int32, (share, lanes), 1)
    ).astype(jnp.float32)
    lane_of = lax.broadcasted_iota(jnp.int32, (rows, lanes), 1)
    carried = jnp.dot(
        scaled, place, precision=lax.Precision.HIGHEST, preferred_element_type=jnp.float32
    ) + jnp.where(lane_of == share, jnp.sum(mixed * mixed, axis=1, keepdims=True), 0.0)
    slots = outgoing.shape[1]
    picked = jnp.dot(
        picker.astype(jnp.float32), carried, precision=lax.Precision.HIGHEST,
        preferred_element_type=jnp.float32)
    outgoing[...] = picked.reshape(outgoing.shape)

    def dispatch(expert):
        return pltpu.make_async_remote_copy(
            src_ref=outgoing.at[expert], dst_ref=incoming.at[e, g % 2], send_sem=s_out.at[expert],
            recv_sem=r_in.at[g % 2, e], device_id=(expert, home), device_id_type=MESH)

    for expert in range(n_grp):
        @pl.when(jnp.logical_not(serving & (g == expert)))
        def _():
            dispatch(expert).start()

    @pl.when(serving)
    def _():
        incoming[e, g % 2] = outgoing[g]

    def gathered(half, peer):
        return pltpu.make_async_remote_copy(
            src_ref=outgoing.at[0], dst_ref=incoming.at[peer, half], send_sem=s_out.at[0],
            recv_sem=r_in.at[half, peer], device_id=(2 * e + half, peer), device_id_type=MESH)

    for half in range(2):
        for peer in range(n_ep):
            @pl.when(jnp.logical_not(serving & (g == 2 * e + half) & (e == peer)))
            def _():
                gathered(half, peer).wait_recv()

    arrived = incoming[...]
    row_total = jnp.sum(arrived[:, :, :, share:share + 1], 0)
    factor = lax.rsqrt(row_total / width + norm_epsilon)
    pre = jnp.zeros((2 * slots, up_ref.shape[1]), jnp.float32)
    for peer in range(n_ep):
        lhs = (arrived[peer][:, :, :share] * factor).astype(jnp.bfloat16).reshape(2 * slots, share)
        pre = pre + jnp.dot(
            lhs, up_ref[peer * share:(peer + 1) * share, :], preferred_element_type=jnp.float32)
    hidden_units = up_ref.shape[1] // 2
    gate = pre[:, :hidden_units]
    act = (gate / (1.0 + jnp.exp(-gate)) * pre[:, hidden_units:]).astype(jnp.bfloat16)
    for peer in range(n_ep):
        piece = jnp.dot(
            act, down_ref[:, peer * share:(peer + 1) * share], preferred_element_type=jnp.float32)
        results[peer] = piece.astype(jnp.bfloat16).astype(jnp.float32).reshape(results.shape[1:])

    def give_back(half, peer):
        return pltpu.make_async_remote_copy(
            src_ref=results.at[peer, half], dst_ref=returned.at[g], send_sem=s_res.at[half, peer],
            recv_sem=r_ret.at[g], device_id=(2 * e + half, peer), device_id_type=MESH)

    for half in range(2):
        for peer in range(n_ep):
            @pl.when(jnp.logical_not(serving & (g == 2 * e + half) & (e == peer)))
            def _():
                give_back(half, peer).start()

    @pl.when(serving)
    def _():
        returned[g] = results[e, g % 2]

    def coming_back(expert):
        return pltpu.make_async_remote_copy(
            src_ref=results.at[0, 0], dst_ref=returned.at[expert], send_sem=s_res.at[0, 0],
            recv_sem=r_ret.at[expert], device_id=(expert, home), device_id_type=MESH)

    for expert in range(n_grp):
        @pl.when(jnp.logical_not(serving & (g == expert)))
        def _():
            coming_back(expert).wait_recv()

    back = returned[...].reshape(n_grp * slots, share).astype(jnp.bfloat16)
    mix = jnp.dot(combine, back, preferred_element_type=jnp.float32)
    out_ref[...] = (mixed + mix).astype(out_ref.dtype)

    for row in range(2 * rows):
        if row < rows:
            @pl.when(e != row)
            def _():
                first(row).wait_send()
        else:
            first(row).wait_send()

    @pl.when(e < rows)
    def _():
        for target in range(n_ep):
            @pl.when(e != target)
            def _():
                second(target).wait_send()

    for step in range(1, n_grp):
        spread(step).wait_send()
    for expert in range(n_grp):
        @pl.when(jnp.logical_not(serving & (g == expert)))
        def _():
            dispatch(expert).wait_send()
    for half in range(2):
        for peer in range(n_ep):
            @pl.when(jnp.logical_not(serving & (g == 2 * e + half) & (e == peer)))
            def _():
                give_back(half, peer).wait_send()


def layer_call(query, keys, values, owner, fill, fresh, block, hidden, gain, routes, route_weight, up, down):
    n_ep = lax.axis_size("ep")
    n_grp = lax.axis_size("grp")
    rows, share = hidden.shape
    width = share * n_ep
    slots = rows
    return pl.pallas_call(
        functools.partial(layer_kernel, rows, n_ep, n_grp, width),
        out_shape=(
            jax.ShapeDtypeStruct((rows, share), jnp.bfloat16),
            jax.ShapeDtypeStruct((rows, width), jnp.bfloat16),
        ),
        in_specs=[pl.BlockSpec(memory_space=pltpu.VMEM)] * 13,
        out_specs=(pl.BlockSpec(memory_space=pltpu.VMEM),) * 2,
        scratch_shapes=[
            pltpu.VMEM((2 * rows, 3, width), jnp.float32),
            pltpu.VMEM((rows, 3, width), jnp.float32),
            pltpu.VMEM((rows, width), jnp.bfloat16),
            pltpu.SemaphoreType.DMA(()),
            pltpu.SemaphoreType.DMA(()),
            pltpu.VMEM((2 * n_ep, 3, width), jnp.float32),
            pltpu.VMEM((rows, 1, width), jnp.float32),
            pltpu.VMEM((n_grp,) + block.shape, block.dtype),
            pltpu.VMEM((n_ep, rows, 128), jnp.float32),
            pltpu.VMEM((n_grp, slots, 128), jnp.float32),
            pltpu.VMEM((n_ep, 2, slots, 128), jnp.float32),
            pltpu.VMEM((n_ep, 2, slots, share), jnp.float32),
            pltpu.VMEM((n_grp, slots, share), jnp.float32),
            pltpu.SemaphoreType.DMA((2 * rows,)),
            pltpu.SemaphoreType.DMA((2 * n_ep,)),
            pltpu.SemaphoreType.DMA((n_ep,)),
            pltpu.SemaphoreType.DMA((rows,)),
            pltpu.SemaphoreType.DMA((n_grp,)),
            pltpu.SemaphoreType.DMA((n_grp,)),
            pltpu.SemaphoreType.DMA((n_ep,)),
            pltpu.SemaphoreType.DMA((n_ep,)),
            pltpu.SemaphoreType.DMA((n_grp,)),
            pltpu.SemaphoreType.DMA((2, n_ep)),
            pltpu.SemaphoreType.DMA((2, n_ep)),
            pltpu.SemaphoreType.DMA((n_grp,)),
        ],
        compiler_params=pltpu.CompilerParams(collective_id=0, has_side_effects=True),
    )(query, keys, values, owner, fill, fresh, block, hidden, gain, routes, route_weight, up, down)


def swap_kernel(query_ref, out_ref, held, send_sem, recv_sem):
    g = lax.axis_index("grp")
    e = lax.axis_index("ep")
    mate = g + 1 - 2 * (g % 2)
    barrier = pltpu.get_barrier_semaphore()
    pl.semaphore_signal(barrier, inc=1, device_id=(mate, e), device_id_type=MESH)
    pl.semaphore_wait(barrier, 1)
    copy = pltpu.make_async_remote_copy(
        src_ref=query_ref, dst_ref=held, send_sem=send_sem, recv_sem=recv_sem,
        device_id=(mate, e), device_id_type=MESH)
    copy.start()
    copy.wait()
    out_ref[...] = held[...]


def swap_call(query):
    return pl.pallas_call(
        swap_kernel,
        out_shape=jax.ShapeDtypeStruct(query.shape, query.dtype),
        in_specs=[pl.BlockSpec(memory_space=pltpu.VMEM)],
        out_specs=pl.BlockSpec(memory_space=pltpu.VMEM),
        scratch_shapes=[
            pltpu.VMEM(query.shape, query.dtype),
            pltpu.SemaphoreType.DMA(()),
            pltpu.SemaphoreType.DMA(()),
        ],
        compiler_params=pltpu.CompilerParams(collective_id=1, has_side_effects=True),
    )(query)


def from_partner(block, axis, apart):
    count = lax.axis_size(axis)
    route = []
    for low in range(count):
        high = low | 1 << apart
        if high != low and high < count:
            route += [(low, high), (high, low)]
    return lax.ppermute(block, axis, route)


def per_device(
    hidden,
    query,
    new_kv,
    key_cache,
    value_cache,
    page_owner,
    page_fill,
    out_weight,
    norm_gain,
    gate_up,
    down,
    routes,
    route_weight,
):
    row_count = query.shape[0]
    group_count = lax.axis_size("grp")
    head_group = HEADS // KV_HEADS
    page_count = page_owner.shape[0]
    token_count = key_cache.shape[0]
    page_length = token_count // page_count
    both_rows = 2 * row_count
    scale = HD ** (-0.5)
    feature_share = hidden.shape[1]
    layer_out, attn_out = layer_call(
        query, key_cache, value_cache, page_owner.reshape(1, -1),
        page_fill.reshape(1, -1), new_kv, out_weight, hidden, norm_gain.reshape(1, feature_share),
        routes, route_weight, gate_up[0], down[0],
    )
    return (layer_out, attn_out)


def solution(mesh):
    placed = (
        P("grp", "ep"),
        P("grp", None),
        P("grp", None, None),
        P(("grp", "ep"), None),
        P(("grp", "ep"), None),
        P(("grp", "ep")),
        P(("grp", "ep")),
        P("grp", "ep"),
        P("ep"),
        P("grp", None, None),
        P("grp", None, None),
        P("grp", None),
        P("grp", None),
    )
    return jax.shard_map(
        per_device,
        mesh=mesh,
        in_specs=placed,
        out_specs=(P("grp", "ep"), P("grp", None)),
        check_vma=False,
    )
```

```python
import jax
import jax.numpy as jnp
from jax import lax
from jax.experimental import pallas as pl
from jax.experimental.pallas import tpu as pltpu
from jax.sharding import PartitionSpec as P
import functools

D = 1536
HEADS = 24
KV_HEADS = 8
HD = 64
FF = 512
TOP = 8


masked_score = -1e30
norm_epsilon = 1e-05

MESH = pl.DeviceIdType.MESH


def layer_kernel(
    rows, n_ep, n_grp, width,
    query_ref, key_ref, value_ref, owner_ref, fill_ref,
    fresh_ref, block_ref, hidden_ref, gain_ref, routes_ref, route_weight_ref, up_ref, down_ref,
    out_ref, attn_ref,
    part_ref, own_ref, mate_query, s_q, r_q, got, final, blocks, squares, outgoing, incoming, results, returned,
    s1, r1, s2, r2, s3, r3, s_sq, r_sq, s_out, r_in, s_res, r_ret,
):
    g = lax.axis_index("grp")
    e = lax.axis_index("ep")
    mate = g + 1 - 2 * (g % 2)
    home = g // 2
    serving = home == e
    share = width // n_ep
    barrier = pltpu.get_barrier_semaphore()
    for peer in range(n_ep):
        @pl.when(e != peer)
        def _():
            pl.semaphore_signal(barrier, inc=1, device_id=(g, peer), device_id_type=MESH)
            pl.semaphore_signal(barrier, inc=1, device_id=(g, peer), device_id_type=MESH)
        pl.semaphore_signal(barrier, inc=1, device_id=(mate, peer), device_id_type=MESH)
    for step in range(1, n_grp):
        pl.semaphore_signal(
            barrier, inc=1, device_id=(lax.rem(g + step, n_grp), e), device_id_type=MESH
        )
    for expert in range(n_grp):
        @pl.when(jnp.logical_not(serving & (g == expert)))
        def _():
            pl.semaphore_signal(barrier, inc=1, device_id=(expert, home), device_id_type=MESH)
    for half in range(2):
        for peer in range(n_ep):
            @pl.when(jnp.logical_not(serving & (g == 2 * e + half) & (e == peer)))
            def _():
                pl.semaphore_signal(
                    barrier, inc=1, device_id=(2 * e + half, peer), device_id_type=MESH
                )
    common = 2 * (n_ep - 1) + n_ep + n_grp - 1

    heads = width // HD
    both = 2 * rows
    pages = owner_ref.shape[1]
    tokens = key_ref.shape[0]
    kv_width = key_ref.shape[1]
    group_size = heads // (kv_width // HD)
    kv_lane = lax.broadcasted_iota(jnp.int32, (kv_width, width), 0)
    head_lane = lax.broadcasted_iota(jnp.int32, (kv_width, width), 1)
    widen = (
        (kv_lane % HD == head_lane % HD) & (kv_lane // HD == head_lane // (HD * group_size))
    ).astype(jnp.bfloat16)
    wide_keys = jnp.dot(key_ref[...], widen, preferred_element_type=jnp.float32).astype(jnp.bfloat16)
    wide_values = jnp.dot(value_ref[...], widen, preferred_element_type=jnp.float32).astype(jnp.bfloat16)
    fresh_keys = jnp.dot(
        fresh_ref[:, 0, :], widen, preferred_element_type=jnp.float32).astype(jnp.bfloat16)
    fresh_values = jnp.dot(fresh_ref[:, 1, :], widen, preferred_element_type=jnp.float32)
    page_length = tokens // pages
    lane_head = lax.broadcasted_iota(jnp.int32, (rows, width), 1) // HD
    token_of = lax.broadcasted_iota(jnp.int32, (tokens, pages), 0)
    page_of = lax.broadcasted_iota(jnp.int32, (tokens, pages), 1)
    filled = (
        (token_of // page_length == page_of) & (token_of % page_length < fill_ref[...])
    ).astype(jnp.float32)

    def attend(queries, first_row):
        stacked = jnp.concatenate(
            [jnp.where(lane_head == h, queries.astype(jnp.float32), 0.0) for h in range(heads)], 0
        ).astype(jnp.bfloat16)
        row_of = lax.broadcasted_iota(jnp.int32, (rows, pages), 0) + first_row
        owns = (owner_ref[...] == row_of).astype(jnp.float32)
        usable = lax.dot_general(
            owns, filled, (((1,), (1,)), ((), ())), preferred_element_type=jnp.float32
        ) > 0.5
        usable = jnp.concatenate([usable] * heads, 0)
        scores = lax.dot_general(
            stacked, wide_keys, (((1,), (1,)), ((), ())), preferred_element_type=jnp.float32
        ) * (HD ** -0.5)
        local_top = jnp.max(jnp.where(usable, scores, masked_score), 1, keepdims=True)
        weights = jnp.where(usable, jnp.exp(scores - local_top), 0.0)
        local_total = jnp.sum(weights, 1, keepdims=True)
        local_accum = jnp.dot(
            weights.astype(jnp.bfloat16), wide_values, preferred_element_type=jnp.float32
        )
        accum_rows = jnp.zeros((rows, width), jnp.float32)
        top_rows = jnp.zeros((rows, width), jnp.float32)
        total_rows = jnp.zeros((rows, width), jnp.float32)
        for h in range(heads):
            mine = lane_head == h
            block = slice(h * rows, (h + 1) * rows)
            accum_rows = jnp.where(mine, local_accum[block], accum_rows)
            top_rows = jnp.where(mine, jnp.broadcast_to(local_top[block], (rows, width)), top_rows)
            total_rows = jnp.where(mine, jnp.broadcast_to(local_total[block], (rows, width)), total_rows)
        for row in range(rows):
            part_ref[first_row + row, 0:1, :] = accum_rows[row:row + 1]
            part_ref[first_row + row, 1:2, :] = top_rows[row:row + 1]
            part_ref[first_row + row, 2:3, :] = total_rows[row:row + 1]
        return stacked

    stacked = attend(query_ref[...], 0)
    own_scores = lax.dot_general(
        stacked, fresh_keys, (((1,), (1,)), ((), ())), preferred_element_type=jnp.float32
    ) * (HD ** -0.5)
    own_column = lax.broadcasted_iota(jnp.int32, own_scores.shape, 1)
    own_row = lax.broadcasted_iota(jnp.int32, own_scores.shape, 0) % rows
    own_top = jnp.sum(jnp.where(own_column == own_row, own_scores, 0.0), 1, keepdims=True)
    own_rows = jnp.zeros((rows, width), jnp.float32)
    for h in range(heads):
        own_rows = jnp.where(
            lane_head == h, jnp.broadcast_to(own_top[h * rows:(h + 1) * rows], (rows, width)), own_rows)
    for row in range(rows):
        own_ref[row, 0:1, :] = fresh_values[row:row + 1]
        own_ref[row, 1:2, :] = own_rows[row:row + 1]
        own_ref[row, 2:3, :] = jnp.ones((1, width), jnp.float32)

    choices = routes_ref.shape[1]
    expert_of = lax.broadcasted_iota(jnp.int32, (rows, n_grp), 1)
    chosen = jnp.zeros((rows, n_grp), jnp.float32)
    weight_at = jnp.zeros((rows, n_grp), jnp.float32)
    for choice in range(choices):
        hit = routes_ref[:, choice:choice + 1] == expert_of
        chosen = chosen + hit.astype(jnp.float32)
        weight_at = weight_at + jnp.where(
            hit, route_weight_ref[:, choice:choice + 1].astype(jnp.float32), 0.0)
    earlier = (
        lax.broadcasted_iota(jnp.int32, (rows, rows), 1)
        < lax.broadcasted_iota(jnp.int32, (rows, rows), 0)
    ).astype(jnp.float32)
    position = jnp.dot(earlier, chosen, preferred_element_type=jnp.float32)
    slot_count = rows * n_grp
    spread_out = (
        lax.broadcasted_iota(jnp.int32, (n_grp, slot_count), 1) // rows
        == lax.broadcasted_iota(jnp.int32, (n_grp, slot_count), 0)
    ).astype(jnp.bfloat16)
    chosen_wide = jnp.dot(chosen.astype(jnp.bfloat16), spread_out, preferred_element_type=jnp.float32)
    position_wide = jnp.dot(position.astype(jnp.bfloat16), spread_out, preferred_element_type=jnp.float32)
    weight_wide = jnp.dot(weight_at.astype(jnp.bfloat16), spread_out, preferred_element_type=jnp.float32)
    slot_of = (lax.broadcasted_iota(jnp.int32, (rows, slot_count), 1) % rows).astype(jnp.float32)
    placed = (chosen_wide > 0.5) & (position_wide == slot_of)
    combine = jnp.where(placed, weight_wide, 0.0).astype(jnp.bfloat16)
    picker = jnp.transpose(placed.astype(jnp.float32)).astype(jnp.bfloat16)

    @pl.when(serving)
    def _():
        pl.semaphore_wait(barrier, common + n_grp - 1 + 2 * n_ep - 1)

    @pl.when(jnp.logical_not(serving))
    def _():
        pl.semaphore_wait(barrier, common + n_grp + 2 * n_ep)

    def first(row):
        if row < rows:
            target = (g, row)
            slot = e
        else:
            target = (mate, row - rows)
            slot = n_ep + e
        return pltpu.make_async_remote_copy(
            src_ref=part_ref.at[row], dst_ref=got.at[slot], send_sem=s1.at[row],
            recv_sem=r1.at[slot], device_id=target, device_id_type=MESH)

    swap = pltpu.make_async_remote_copy(
        src_ref=query_ref, dst_ref=mate_query, send_sem=s_q, recv_sem=r_q,
        device_id=(mate, e), device_id_type=MESH)
    swap.start()
    for row in range(rows):
        @pl.when(e != row)
        def _():
            first(row).start()

        @pl.when(e == row)
        def _():
            got[e] = part_ref[row]

    def spread(step):
        return pltpu.make_async_remote_copy(
            src_ref=block_ref, dst_ref=blocks.at[g], send_sem=s3.at[step],
            recv_sem=r3.at[g], device_id=(lax.rem(g + step, n_grp), e), device_id_type=MESH)

    def gathered_block(step):
        source = lax.rem(g + n_grp - step, n_grp)
        return pltpu.make_async_remote_copy(
            src_ref=block_ref, dst_ref=blocks.at[source], send_sem=s3.at[step],
            recv_sem=r3.at[source], device_id=(source, e), device_id_type=MESH)

    for step in range(1, n_grp):
        spread(step).start()
    blocks[g] = block_ref[...]

    swap.wait()
    attend(mate_query[...], rows)
    for row in range(rows, 2 * rows):
        first(row).start()

    def incoming_part(slot):
        return pltpu.make_async_remote_copy(
            src_ref=part_ref.at[0], dst_ref=got.at[slot], send_sem=s1.at[0],
            recv_sem=r1.at[slot], device_id=(g, 0), device_id_type=MESH)

    def second(target):
        return pltpu.make_async_remote_copy(
            src_ref=final.at[e], dst_ref=final.at[e], send_sem=s2.at[target],
            recv_sem=r2.at[e], device_id=(g, target), device_id_type=MESH)

    @pl.when(e < rows)
    def _():
        for slot in range(2 * n_ep):
            if slot < n_ep:
                @pl.when(e != slot)
                def _():
                    incoming_part(slot).wait_recv()
            else:
                incoming_part(slot).wait_recv()
        stack = got[...]
        own = own_ref[e]
        maxes = jnp.maximum(jnp.max(stack[:, 1:2, :], 0), own[1:2, :])
        factors = jnp.exp(stack[:, 1:2, :] - maxes[None])
        own_factor = jnp.exp(own[1:2, :] - maxes)
        total = jnp.sum(stack[:, 2:3, :] * factors, 0) + own_factor
        accum = jnp.sum(stack[:, 0:1, :] * factors, 0) + own[0:1, :] * own_factor
        final[e] = (accum / total).astype(jnp.bfloat16).astype(jnp.float32)
        for target in range(n_ep):
            @pl.when(e != target)
            def _():
                second(target).start()

    def arriving(row):
        return pltpu.make_async_remote_copy(
            src_ref=final.at[row], dst_ref=final.at[row], send_sem=s2.at[0],
            recv_sem=r2.at[row], device_id=(g, row), device_id_type=MESH)

    for row in range(rows):
        @pl.when(e != row)
        def _():
            arriving(row).wait_recv()

    row_ids = lax.broadcasted_iota(jnp.int32, (rows, width), 0)
    attn = jnp.zeros((rows, width), jnp.float32)
    for row in range(rows):
        attn = jnp.where(row_ids == row, jnp.broadcast_to(final[row], (rows, width)), attn)
    attn = attn.astype(jnp.bfloat16)
    attn_ref[...] = attn

    for step in range(1, n_grp):
        gathered_block(step).wait_recv()
    columns = blocks[...].reshape(n_grp * blocks.shape[1], share)
    projected = jnp.dot(attn, columns, preferred_element_type=jnp.float32)
    mixed = hidden_ref[...].astype(jnp.float32) + projected

    scaled = mixed * gain_ref[...]
    lanes = outgoing.shape[2]
    place = (
        lax.broadcasted_iota(jnp.int32, (share, lanes), 0)
        == lax.broadcasted_iota(jnp.int32, (share, lanes), 1)
    ).astype(jnp.float32)
    lane_of = lax.broadcasted_iota(jnp.int32, (rows, lanes), 1)
    carried = jnp.dot(
        scaled, place, precision=lax.Precision.HIGHEST, preferred_element_type=jnp.float32
    ) + jnp.where(lane_of == share, jnp.sum(mixed * mixed, axis=1, keepdims=True), 0.0)
    slots = outgoing.shape[1]
    picked = jnp.dot(
        picker.astype(jnp.float32), carried, precision=lax.Precision.HIGHEST,
        preferred_element_type=jnp.float32)
    outgoing[...] = picked.reshape(outgoing.shape)

    def dispatch(expert):
        return pltpu.make_async_remote_copy(
            src_ref=outgoing.at[expert], dst_ref=incoming.at[e, g % 2], send_sem=s_out.at[expert],
            recv_sem=r_in.at[g % 2, e], device_id=(expert, home), device_id_type=MESH)

    for expert in range(n_grp):
        @pl.when(jnp.logical_not(serving & (g == expert)))
        def _():
            dispatch(expert).start()

    @pl.when(serving)
    def _():
        incoming[e, g % 2] = outgoing[g]

    def gathered(half, peer):
        return pltpu.make_async_remote_copy(
            src_ref=outgoing.at[0], dst_ref=incoming.at[peer, half], send_sem=s_out.at[0],
            recv_sem=r_in.at[half, peer], device_id=(2 * e + half, peer), device_id_type=MESH)

    for half in range(2):
        for peer in range(n_ep):
            @pl.when(jnp.logical_not(serving & (g == 2 * e + half) & (e == peer)))
            def _():
                gathered(half, peer).wait_recv()

    arrived = incoming[...]
    row_total = jnp.sum(arrived[:, :, :, share:share + 1], 0)
    factor = lax.rsqrt(row_total / width + norm_epsilon)
    pre = jnp.zeros((2 * slots, up_ref.shape[1]), jnp.float32)
    for peer in range(n_ep):
        lhs = (arrived[peer][:, :, :share] * factor).astype(jnp.bfloat16).reshape(2 * slots, share)
        pre = pre + jnp.dot(
            lhs, up_ref[peer * share:(peer + 1) * share, :], preferred_element_type=jnp.float32)
    hidden_units = up_ref.shape[1] // 2
    gate = pre[:, :hidden_units]
    act = (gate / (1.0 + jnp.exp(-gate)) * pre[:, hidden_units:]).astype(jnp.bfloat16)
    for peer in range(n_ep):
        piece = jnp.dot(
            act, down_ref[:, peer * share:(peer + 1) * share], preferred_element_type=jnp.float32)
        results[peer] = piece.astype(jnp.bfloat16).astype(jnp.float32).reshape(results.shape[1:])

    def give_back(half, peer):
        return pltpu.make_async_remote_copy(
            src_ref=results.at[peer, half], dst_ref=returned.at[g], send_sem=s_res.at[half, peer],
            recv_sem=r_ret.at[g], device_id=(2 * e + half, peer), device_id_type=MESH)

    for half in range(2):
        for peer in range(n_ep):
            @pl.when(jnp.logical_not(serving & (g == 2 * e + half) & (e == peer)))
            def _():
                give_back(half, peer).start()

    @pl.when(serving)
    def _():
        returned[g] = results[e, g % 2]

    def coming_back(expert):
        return pltpu.make_async_remote_copy(
            src_ref=results.at[0, 0], dst_ref=returned.at[expert], send_sem=s_res.at[0, 0],
            recv_sem=r_ret.at[expert], device_id=(expert, home), device_id_type=MESH)

    for expert in range(n_grp):
        @pl.when(jnp.logical_not(serving & (g == expert)))
        def _():
            coming_back(expert).wait_recv()

    back = returned[...].reshape(n_grp * slots, share).astype(jnp.bfloat16)
    mix = jnp.dot(combine, back, preferred_element_type=jnp.float32)
    out_ref[...] = (mixed + mix).astype(out_ref.dtype)

    for row in range(2 * rows):
        if row < rows:
            @pl.when(e != row)
            def _():
                first(row).wait_send()
        else:
            first(row).wait_send()

    @pl.when(e < rows)
    def _():
        for target in range(n_ep):
            @pl.when(e != target)
            def _():
                second(target).wait_send()

    for step in range(1, n_grp):
        spread(step).wait_send()
    for expert in range(n_grp):
        @pl.when(jnp.logical_not(serving & (g == expert)))
        def _():
            dispatch(expert).wait_send()
    for half in range(2):
        for peer in range(n_ep):
            @pl.when(jnp.logical_not(serving & (g == 2 * e + half) & (e == peer)))
            def _():
                give_back(half, peer).wait_send()


def layer_call(query, keys, values, owner, fill, fresh, block, hidden, gain, routes, route_weight, up, down):
    n_ep = lax.axis_size("ep")
    n_grp = lax.axis_size("grp")
    rows, share = hidden.shape
    width = share * n_ep
    slots = rows
    return pl.pallas_call(
        functools.partial(layer_kernel, rows, n_ep, n_grp, width),
        out_shape=(
            jax.ShapeDtypeStruct((rows, share), jnp.bfloat16),
            jax.ShapeDtypeStruct((rows, width), jnp.bfloat16),
        ),
        in_specs=[pl.BlockSpec(memory_space=pltpu.VMEM)] * 13,
        out_specs=(pl.BlockSpec(memory_space=pltpu.VMEM),) * 2,
        scratch_shapes=[
            pltpu.VMEM((2 * rows, 3, width), jnp.float32),
            pltpu.VMEM((rows, 3, width), jnp.float32),
            pltpu.VMEM((rows, width), jnp.bfloat16),
            pltpu.SemaphoreType.DMA(()),
            pltpu.SemaphoreType.DMA(()),
            pltpu.VMEM((2 * n_ep, 3, width), jnp.float32),
            pltpu.VMEM((rows, 1, width), jnp.float32),
            pltpu.VMEM((n_grp,) + block.shape, block.dtype),
            pltpu.VMEM((n_ep, rows, 128), jnp.float32),
            pltpu.VMEM((n_grp, slots, 128), jnp.float32),
            pltpu.VMEM((n_ep, 2, slots, 128), jnp.float32),
            pltpu.VMEM((n_ep, 2, slots, share), jnp.float32),
            pltpu.VMEM((n_grp, slots, share), jnp.float32),
            pltpu.SemaphoreType.DMA((2 * rows,)),
            pltpu.SemaphoreType.DMA((2 * n_ep,)),
            pltpu.SemaphoreType.DMA((n_ep,)),
            pltpu.SemaphoreType.DMA((rows,)),
            pltpu.SemaphoreType.DMA((n_grp,)),
            pltpu.SemaphoreType.DMA((n_grp,)),
            pltpu.SemaphoreType.DMA((n_ep,)),
            pltpu.SemaphoreType.DMA((n_ep,)),
            pltpu.SemaphoreType.DMA((n_grp,)),
            pltpu.SemaphoreType.DMA((2, n_ep)),
            pltpu.SemaphoreType.DMA((2, n_ep)),
            pltpu.SemaphoreType.DMA((n_grp,)),
        ],
        compiler_params=pltpu.CompilerParams(collective_id=0, has_side_effects=True),
    )(query, keys, values, owner, fill, fresh, block, hidden, gain, routes, route_weight, up, down)


def per_device(
    hidden,
    query,
    new_kv,
    key_cache,
    value_cache,
    page_owner,
    page_fill,
    out_weight,
    norm_gain,
    gate_up,
    down,
    routes,
    route_weight,
):
    row_count = query.shape[0]
    feature_share = hidden.shape[1]
    layer_out, attn_out = layer_call(
        query, key_cache, value_cache, page_owner.reshape(1, -1),
        page_fill.reshape(1, -1), new_kv, out_weight, hidden, norm_gain.reshape(1, feature_share),
        routes, route_weight, gate_up[0], down[0],
    )
    return (layer_out, attn_out)


def solution(mesh):
    placed = (
        P("grp", "ep"),
        P("grp", None),
        P("grp", None, None),
        P(("grp", "ep"), None),
        P(("grp", "ep"), None),
        P(("grp", "ep")),
        P(("grp", "ep")),
        P("grp", "ep"),
        P("ep"),
        P("grp", None, None),
        P("grp", None, None),
        P("grp", None),
        P("grp", None),
    )
    return jax.shard_map(
        per_device,
        mesh=mesh,
        in_specs=placed,
        out_specs=(P("grp", "ep"), P("grp", None)),
        check_vma=False,
    )
```

```python
import jax
import jax.numpy as jnp
from jax import lax
from jax.experimental import pallas as pl
from jax.experimental.pallas import tpu as pltpu
from jax.sharding import PartitionSpec as P
import functools

D = 1536
HEADS = 24
KV_HEADS = 8
HD = 64
FF = 512
TOP = 8


masked_score = -1e30
norm_epsilon = 1e-05

MESH = pl.DeviceIdType.MESH


def layer_kernel(
    rows, n_ep, n_grp, width,
    query_ref, key_ref, value_ref, owner_ref, fill_ref,
    fresh_ref, block_ref, hidden_ref, gain_ref, routes_ref, route_weight_ref, up_ref, down_ref,
    out_ref, attn_ref,
    part_ref, own_ref, mate_query, s_q, r_q, got, final, blocks, squares, outgoing, incoming, results, returned,
    s1, r1, s2, r2, s3, r3, s_sq, r_sq, s_out, r_in, s_res, r_ret,
):
    g = lax.axis_index("grp")
    e = lax.axis_index("ep")
    mate = g + 1 - 2 * (g % 2)
    home = g // 2
    serving = home == e
    share = width // n_ep
    barrier = pltpu.get_barrier_semaphore()
    for peer in range(n_ep):
        @pl.when(e != peer)
        def _():
            pl.semaphore_signal(barrier, inc=1, device_id=(g, peer), device_id_type=MESH)
            pl.semaphore_signal(barrier, inc=1, device_id=(g, peer), device_id_type=MESH)
        pl.semaphore_signal(barrier, inc=1, device_id=(mate, peer), device_id_type=MESH)
    for step in range(1, n_grp):
        pl.semaphore_signal(
            barrier, inc=1, device_id=(lax.rem(g + step, n_grp), e), device_id_type=MESH
        )
    for expert in range(n_grp):
        @pl.when(jnp.logical_not(serving & (g == expert)))
        def _():
            pl.semaphore_signal(barrier, inc=1, device_id=(expert, home), device_id_type=MESH)
    for half in range(2):
        for peer in range(n_ep):
            @pl.when(jnp.logical_not(serving & (g == 2 * e + half) & (e == peer)))
            def _():
                pl.semaphore_signal(
                    barrier, inc=1, device_id=(2 * e + half, peer), device_id_type=MESH
                )
    common = 2 * (n_ep - 1) + n_ep + n_grp - 1

    heads = width // HD
    both = 2 * rows
    pages = owner_ref.shape[1]
    tokens = key_ref.shape[0]
    kv_width = key_ref.shape[1]
    group_size = heads // (kv_width // HD)
    kv_lane = lax.broadcasted_iota(jnp.int32, (kv_width, width), 0)
    head_lane = lax.broadcasted_iota(jnp.int32, (kv_width, width), 1)
    widen = (
        (kv_lane % HD == head_lane % HD) & (kv_lane // HD == head_lane // (HD * group_size))
    ).astype(jnp.bfloat16)
    wide_keys = jnp.dot(key_ref[...], widen, preferred_element_type=jnp.float32).astype(jnp.bfloat16)
    wide_values = jnp.dot(value_ref[...], widen, preferred_element_type=jnp.float32).astype(jnp.bfloat16)
    fresh_keys = jnp.dot(
        fresh_ref[:, 0, :], widen, preferred_element_type=jnp.float32).astype(jnp.bfloat16)
    fresh_values = jnp.dot(fresh_ref[:, 1, :], widen, preferred_element_type=jnp.float32)
    page_length = tokens // pages
    lane_head = lax.broadcasted_iota(jnp.int32, (rows, width), 1) // HD
    token_of = lax.broadcasted_iota(jnp.int32, (tokens, pages), 0)
    page_of = lax.broadcasted_iota(jnp.int32, (tokens, pages), 1)
    filled = (
        (token_of // page_length == page_of) & (token_of % page_length < fill_ref[...])
    ).astype(jnp.float32)

    def attend(queries, first_row):
        stacked = jnp.concatenate(
            [jnp.where(lane_head == h, queries.astype(jnp.float32), 0.0) for h in range(heads)], 0
        ).astype(jnp.bfloat16)
        row_of = lax.broadcasted_iota(jnp.int32, (rows, pages), 0) + first_row
        owns = (owner_ref[...] == row_of).astype(jnp.float32)
        usable = lax.dot_general(
            owns, filled, (((1,), (1,)), ((), ())), preferred_element_type=jnp.float32
        ) > 0.5
        usable = jnp.concatenate([usable] * heads, 0)
        scores = lax.dot_general(
            stacked, wide_keys, (((1,), (1,)), ((), ())), preferred_element_type=jnp.float32
        ) * (HD ** -0.5)
        local_top = jnp.max(jnp.where(usable, scores, masked_score), 1, keepdims=True)
        weights = jnp.where(usable, jnp.exp(scores - local_top), 0.0)
        local_total = jnp.sum(weights, 1, keepdims=True)
        local_accum = jnp.dot(
            weights.astype(jnp.bfloat16), wide_values, preferred_element_type=jnp.float32
        )
        accum_rows = jnp.zeros((rows, width), jnp.float32)
        top_rows = jnp.zeros((rows, width), jnp.float32)
        total_rows = jnp.zeros((rows, width), jnp.float32)
        for h in range(heads):
            mine = lane_head == h
            block = slice(h * rows, (h + 1) * rows)
            accum_rows = jnp.where(mine, local_accum[block], accum_rows)
            top_rows = jnp.where(mine, jnp.broadcast_to(local_top[block], (rows, width)), top_rows)
            total_rows = jnp.where(mine, jnp.broadcast_to(local_total[block], (rows, width)), total_rows)
        for row in range(rows):
            part_ref[first_row + row, 0:1, :] = accum_rows[row:row + 1]
            part_ref[first_row + row, 1:2, :] = top_rows[row:row + 1]
            part_ref[first_row + row, 2:3, :] = total_rows[row:row + 1]
        return stacked

    stacked = attend(query_ref[...], 0)
    own_scores = lax.dot_general(
        stacked, fresh_keys, (((1,), (1,)), ((), ())), preferred_element_type=jnp.float32
    ) * (HD ** -0.5)
    own_column = lax.broadcasted_iota(jnp.int32, own_scores.shape, 1)
    own_row = lax.broadcasted_iota(jnp.int32, own_scores.shape, 0) % rows
    own_top = jnp.sum(jnp.where(own_column == own_row, own_scores, 0.0), 1, keepdims=True)
    own_rows = jnp.zeros((rows, width), jnp.float32)
    for h in range(heads):
        own_rows = jnp.where(
            lane_head == h, jnp.broadcast_to(own_top[h * rows:(h + 1) * rows], (rows, width)), own_rows)
    for row in range(rows):
        own_ref[row, 0:1, :] = fresh_values[row:row + 1]
        own_ref[row, 1:2, :] = own_rows[row:row + 1]
        own_ref[row, 2:3, :] = jnp.ones((1, width), jnp.float32)

    choices = routes_ref.shape[1]
    expert_of = lax.broadcasted_iota(jnp.int32, (rows, n_grp), 1)
    chosen = jnp.zeros((rows, n_grp), jnp.float32)
    weight_at = jnp.zeros((rows, n_grp), jnp.float32)
    for choice in range(choices):
        hit = routes_ref[:, choice:choice + 1] == expert_of
        chosen = chosen + hit.astype(jnp.float32)
        weight_at = weight_at + jnp.where(
            hit, route_weight_ref[:, choice:choice + 1].astype(jnp.float32), 0.0)
    earlier = (
        lax.broadcasted_iota(jnp.int32, (rows, rows), 1)
        < lax.broadcasted_iota(jnp.int32, (rows, rows), 0)
    ).astype(jnp.float32)
    position = jnp.dot(earlier, chosen, preferred_element_type=jnp.float32)
    slot_count = rows * n_grp
    spread_out = (
        lax.broadcasted_iota(jnp.int32, (n_grp, slot_count), 1) // rows
        == lax.broadcasted_iota(jnp.int32, (n_grp, slot_count), 0)
    ).astype(jnp.bfloat16)
    chosen_wide = jnp.dot(chosen.astype(jnp.bfloat16), spread_out, preferred_element_type=jnp.float32)
    position_wide = jnp.dot(position.astype(jnp.bfloat16), spread_out, preferred_element_type=jnp.float32)
    weight_wide = jnp.dot(weight_at.astype(jnp.bfloat16), spread_out, preferred_element_type=jnp.float32)
    slot_of = (lax.broadcasted_iota(jnp.int32, (rows, slot_count), 1) % rows).astype(jnp.float32)
    placed = (chosen_wide > 0.5) & (position_wide == slot_of)
    combine = jnp.where(placed, weight_wide, 0.0).astype(jnp.bfloat16)
    picker = jnp.transpose(placed.astype(jnp.float32)).astype(jnp.bfloat16)

    @pl.when(serving)
    def _():
        pl.semaphore_wait(barrier, common + n_grp - 1 + 2 * n_ep - 1)

    @pl.when(jnp.logical_not(serving))
    def _():
        pl.semaphore_wait(barrier, common + n_grp + 2 * n_ep)

    def first(row):
        if row < rows:
            target = (g, row)
            slot = e
        else:
            target = (mate, row - rows)
            slot = n_ep + e
        return pltpu.make_async_remote_copy(
            src_ref=part_ref.at[row], dst_ref=got.at[slot], send_sem=s1.at[row],
            recv_sem=r1.at[slot], device_id=target, device_id_type=MESH)

    swap = pltpu.make_async_remote_copy(
        src_ref=query_ref, dst_ref=mate_query, send_sem=s_q, recv_sem=r_q,
        device_id=(mate, e), device_id_type=MESH)
    swap.start()
    for row in range(rows):
        @pl.when(e != row)
        def _():
            first(row).start()

        @pl.when(e == row)
        def _():
            got[e] = part_ref[row]

    def spread(step):
        return pltpu.make_async_remote_copy(
            src_ref=block_ref, dst_ref=blocks.at[g], send_sem=s3.at[step],
            recv_sem=r3.at[g], device_id=(lax.rem(g + step, n_grp), e), device_id_type=MESH)

    def gathered_block(step):
        source = lax.rem(g + n_grp - step, n_grp)
        return pltpu.make_async_remote_copy(
            src_ref=block_ref, dst_ref=blocks.at[source], send_sem=s3.at[step],
            recv_sem=r3.at[source], device_id=(source, e), device_id_type=MESH)

    for step in range(1, n_grp):
        spread(step).start()
    blocks[g] = block_ref[...]

    swap.wait()
    attend(mate_query[...], rows)
    for row in range(rows, 2 * rows):
        first(row).start()

    def incoming_part(slot):
        return pltpu.make_async_remote_copy(
            src_ref=part_ref.at[0], dst_ref=got.at[slot], send_sem=s1.at[0],
            recv_sem=r1.at[slot], device_id=(g, 0), device_id_type=MESH)

    def second(target):
        return pltpu.make_async_remote_copy(
            src_ref=final.at[e], dst_ref=final.at[e], send_sem=s2.at[target],
            recv_sem=r2.at[e], device_id=(g, target), device_id_type=MESH)

    @pl.when(e < rows)
    def _():
        for slot in range(2 * n_ep):
            if slot < n_ep:
                @pl.when(e != slot)
                def _():
                    incoming_part(slot).wait_recv()
            else:
                incoming_part(slot).wait_recv()
        stack = got[...]
        own = own_ref[e]
        maxes = jnp.maximum(jnp.max(stack[:, 1:2, :], 0), own[1:2, :])
        factors = jnp.exp(stack[:, 1:2, :] - maxes[None])
        own_factor = jnp.exp(own[1:2, :] - maxes)
        total = jnp.sum(stack[:, 2:3, :] * factors, 0) + own_factor
        accum = jnp.sum(stack[:, 0:1, :] * factors, 0) + own[0:1, :] * own_factor
        final[e] = (accum / total).astype(jnp.bfloat16).astype(jnp.float32)
        for target in range(n_ep):
            @pl.when(e != target)
            def _():
                second(target).start()

    def arriving(row):
        return pltpu.make_async_remote_copy(
            src_ref=final.at[row], dst_ref=final.at[row], send_sem=s2.at[0],
            recv_sem=r2.at[row], device_id=(g, row), device_id_type=MESH)

    for row in range(rows):
        @pl.when(e != row)
        def _():
            arriving(row).wait_recv()

    row_ids = lax.broadcasted_iota(jnp.int32, (rows, width), 0)
    attn = jnp.zeros((rows, width), jnp.float32)
    for row in range(rows):
        attn = jnp.where(row_ids == row, jnp.broadcast_to(final[row], (rows, width)), attn)
    attn_ref[...] = attn
    attn = attn.astype(jnp.bfloat16)

    for step in range(1, n_grp):
        gathered_block(step).wait_recv()
    columns = blocks[...].reshape(n_grp * blocks.shape[1], share)
    projected = jnp.dot(attn, columns, preferred_element_type=jnp.float32)
    mixed = hidden_ref[...].astype(jnp.float32) + projected

    scaled = mixed * gain_ref[...]
    lanes = outgoing.shape[2]
    place = (
        lax.broadcasted_iota(jnp.int32, (share, lanes), 0)
        == lax.broadcasted_iota(jnp.int32, (share, lanes), 1)
    ).astype(jnp.float32)
    lane_of = lax.broadcasted_iota(jnp.int32, (rows, lanes), 1)
    carried = jnp.dot(
        scaled, place, precision=lax.Precision.HIGHEST, preferred_element_type=jnp.float32
    ) + jnp.where(lane_of == share, jnp.sum(mixed * mixed, axis=1, keepdims=True), 0.0)
    slots = outgoing.shape[1]
    picked = jnp.dot(
        picker.astype(jnp.float32), carried, precision=lax.Precision.HIGHEST,
        preferred_element_type=jnp.float32)
    outgoing[...] = picked.reshape(outgoing.shape)

    def dispatch(expert):
        return pltpu.make_async_remote_copy(
            src_ref=outgoing.at[expert], dst_ref=incoming.at[e, g % 2], send_sem=s_out.at[expert],
            recv_sem=r_in.at[g % 2, e], device_id=(expert, home), device_id_type=MESH)

    for expert in range(n_grp):
        @pl.when(jnp.logical_not(serving & (g == expert)))
        def _():
            dispatch(expert).start()

    @pl.when(serving)
    def _():
        incoming[e, g % 2] = outgoing[g]

    def gathered(half, peer):
        return pltpu.make_async_remote_copy(
            src_ref=outgoing.at[0], dst_ref=incoming.at[peer, half], send_sem=s_out.at[0],
            recv_sem=r_in.at[half, peer], device_id=(2 * e + half, peer), device_id_type=MESH)

    for half in range(2):
        for peer in range(n_ep):
            @pl.when(jnp.logical_not(serving & (g == 2 * e + half) & (e == peer)))
            def _():
                gathered(half, peer).wait_recv()

    arrived = incoming[...]
    row_total = jnp.sum(arrived[:, :, :, share:share + 1], 0)
    factor = lax.rsqrt(row_total / width + norm_epsilon)
    pre = jnp.zeros((2 * slots, up_ref.shape[1]), jnp.float32)
    for peer in range(n_ep):
        lhs = (arrived[peer][:, :, :share] * factor).astype(jnp.bfloat16).reshape(2 * slots, share)
        pre = pre + jnp.dot(
            lhs, up_ref[peer * share:(peer + 1) * share, :], preferred_element_type=jnp.float32)
    hidden_units = up_ref.shape[1] // 2
    gate = pre[:, :hidden_units]
    act = (gate / (1.0 + jnp.exp(-gate)) * pre[:, hidden_units:]).astype(jnp.bfloat16)
    for peer in range(n_ep):
        piece = jnp.dot(
            act, down_ref[:, peer * share:(peer + 1) * share], preferred_element_type=jnp.float32)
        results[peer] = piece.astype(jnp.bfloat16).astype(jnp.float32).reshape(results.shape[1:])

    def give_back(half, peer):
        return pltpu.make_async_remote_copy(
            src_ref=results.at[peer, half], dst_ref=returned.at[g], send_sem=s_res.at[half, peer],
            recv_sem=r_ret.at[g], device_id=(2 * e + half, peer), device_id_type=MESH)

    for half in range(2):
        for peer in range(n_ep):
            @pl.when(jnp.logical_not(serving & (g == 2 * e + half) & (e == peer)))
            def _():
                give_back(half, peer).start()

    @pl.when(serving)
    def _():
        returned[g] = results[e, g % 2]

    def coming_back(expert):
        return pltpu.make_async_remote_copy(
            src_ref=results.at[0, 0], dst_ref=returned.at[expert], send_sem=s_res.at[0, 0],
            recv_sem=r_ret.at[expert], device_id=(expert, home), device_id_type=MESH)

    for expert in range(n_grp):
        @pl.when(jnp.logical_not(serving & (g == expert)))
        def _():
            coming_back(expert).wait_recv()

    back = returned[...].reshape(n_grp * slots, share).astype(jnp.bfloat16)
    mix = jnp.dot(combine, back, preferred_element_type=jnp.float32)
    out_ref[...] = mixed + mix

    for row in range(2 * rows):
        if row < rows:
            @pl.when(e != row)
            def _():
                first(row).wait_send()
        else:
            first(row).wait_send()

    @pl.when(e < rows)
    def _():
        for target in range(n_ep):
            @pl.when(e != target)
            def _():
                second(target).wait_send()

    for step in range(1, n_grp):
        spread(step).wait_send()
    for expert in range(n_grp):
        @pl.when(jnp.logical_not(serving & (g == expert)))
        def _():
            dispatch(expert).wait_send()
    for half in range(2):
        for peer in range(n_ep):
            @pl.when(jnp.logical_not(serving & (g == 2 * e + half) & (e == peer)))
            def _():
                give_back(half, peer).wait_send()


def layer_call(query, keys, values, owner, fill, fresh, block, hidden, gain, routes, route_weight, up, down):
    n_ep = lax.axis_size("ep")
    n_grp = lax.axis_size("grp")
    rows, share = hidden.shape
    width = share * n_ep
    slots = rows
    return pl.pallas_call(
        functools.partial(layer_kernel, rows, n_ep, n_grp, width),
        out_shape=(
            jax.ShapeDtypeStruct((rows, share), jnp.float32),
            jax.ShapeDtypeStruct((rows, width), jnp.float32),
        ),
        in_specs=[pl.BlockSpec(memory_space=pltpu.VMEM)] * 13,
        out_specs=(pl.BlockSpec(memory_space=pltpu.VMEM),) * 2,
        scratch_shapes=[
            pltpu.VMEM((2 * rows, 3, width), jnp.float32),
            pltpu.VMEM((rows, 3, width), jnp.float32),
            pltpu.VMEM((rows, width), jnp.bfloat16),
            pltpu.SemaphoreType.DMA(()),
            pltpu.SemaphoreType.DMA(()),
            pltpu.VMEM((2 * n_ep, 3, width), jnp.float32),
            pltpu.VMEM((rows, 1, width), jnp.float32),
            pltpu.VMEM((n_grp,) + block.shape, block.dtype),
            pltpu.VMEM((n_ep, rows, 128), jnp.float32),
            pltpu.VMEM((n_grp, slots, 128), jnp.float32),
            pltpu.VMEM((n_ep, 2, slots, 128), jnp.float32),
            pltpu.VMEM((n_ep, 2, slots, share), jnp.float32),
            pltpu.VMEM((n_grp, slots, share), jnp.float32),
            pltpu.SemaphoreType.DMA((2 * rows,)),
            pltpu.SemaphoreType.DMA((2 * n_ep,)),
            pltpu.SemaphoreType.DMA((n_ep,)),
            pltpu.SemaphoreType.DMA((rows,)),
            pltpu.SemaphoreType.DMA((n_grp,)),
            pltpu.SemaphoreType.DMA((n_grp,)),
            pltpu.SemaphoreType.DMA((n_ep,)),
            pltpu.SemaphoreType.DMA((n_ep,)),
            pltpu.SemaphoreType.DMA((n_grp,)),
            pltpu.SemaphoreType.DMA((2, n_ep)),
            pltpu.SemaphoreType.DMA((2, n_ep)),
            pltpu.SemaphoreType.DMA((n_grp,)),
        ],
        compiler_params=pltpu.CompilerParams(collective_id=0, has_side_effects=True),
    )(query, keys, values, owner, fill, fresh, block, hidden, gain, routes, route_weight, up, down)


def per_device(
    hidden,
    query,
    new_kv,
    key_cache,
    value_cache,
    page_owner,
    page_fill,
    out_weight,
    norm_gain,
    gate_up,
    down,
    routes,
    route_weight,
):
    row_count = query.shape[0]
    feature_share = hidden.shape[1]
    layer_out, attn_out = layer_call(
        query, key_cache, value_cache, page_owner.reshape(1, -1),
        page_fill.reshape(1, -1), new_kv, out_weight, hidden, norm_gain.reshape(1, feature_share),
        routes, route_weight, gate_up[0], down[0],
    )
    return (layer_out.astype(jnp.bfloat16), attn_out.astype(jnp.bfloat16))


def solution(mesh):
    placed = (
        P("grp", "ep"),
        P("grp", None),
        P("grp", None, None),
        P(("grp", "ep"), None),
        P(("grp", "ep"), None),
        P(("grp", "ep")),
        P(("grp", "ep")),
        P("grp", "ep"),
        P("ep"),
        P("grp", None, None),
        P("grp", None, None),
        P("grp", None),
        P("grp", None),
    )
    return jax.shard_map(
        per_device,
        mesh=mesh,
        in_specs=placed,
        out_specs=(P("grp", "ep"), P("grp", None)),
        check_vma=False,
    )
```

```python
import jax
import jax.numpy as jnp
from jax import lax
from jax.experimental import pallas as pl
from jax.experimental.pallas import tpu as pltpu
from jax.sharding import PartitionSpec as P
import functools

D = 1536
HEADS = 24
KV_HEADS = 8
HD = 64
FF = 512
TOP = 8


masked_score = -1e30
norm_epsilon = 1e-05

MESH = pl.DeviceIdType.MESH


def layer_kernel(
    rows, n_ep, n_grp, width,
    query_ref, key_ref, value_ref, owner_ref, fill_ref,
    fresh_ref, block_ref, hidden_ref, gain_ref, routes_ref, route_weight_ref, up_ref, down_ref,
    out_ref, attn_ref,
    part_ref, own_ref, mate_query, s_q, r_q, got, final, blocks, squares, outgoing, incoming, results, returned,
    s1, r1, s2, r2, s3, r3, s_sq, r_sq, s_out, r_in, s_res, r_ret,
):
    g = lax.axis_index("grp")
    e = lax.axis_index("ep")
    mate = g + 1 - 2 * (g % 2)
    home = g // 2
    serving = home == e
    share = width // n_ep
    barrier = pltpu.get_barrier_semaphore()
    for step in range(1, n_grp):
        pl.semaphore_signal(
            barrier, inc=1, device_id=(lax.rem(g + step, n_grp), e), device_id_type=MESH
        )
    for expert in range(n_grp):
        @pl.when(jnp.logical_not(serving & (g == expert)))
        def _():
            pl.semaphore_signal(barrier, inc=1, device_id=(expert, home), device_id_type=MESH)
    for half in range(2):
        for peer in range(n_ep):
            @pl.when(jnp.logical_not(serving & (g == 2 * e + half) & (e == peer)))
            def _():
                pl.semaphore_signal(
                    barrier, inc=1, device_id=(2 * e + half, peer), device_id_type=MESH
                )
    for peer in range(n_ep):
        @pl.when(e != peer)
        def _():
            pl.semaphore_signal(barrier, inc=1, device_id=(g, peer), device_id_type=MESH)
        pl.semaphore_signal(barrier, inc=1, device_id=(mate, peer), device_id_type=MESH)
    common = n_ep - 1 + n_ep + n_grp - 1

    heads = width // HD
    both = 2 * rows
    pages = owner_ref.shape[1]
    tokens = key_ref.shape[0]
    kv_width = key_ref.shape[1]
    group_size = heads // (kv_width // HD)
    kv_lane = lax.broadcasted_iota(jnp.int32, (kv_width, width), 0)
    head_lane = lax.broadcasted_iota(jnp.int32, (kv_width, width), 1)
    widen = (
        (kv_lane % HD == head_lane % HD) & (kv_lane // HD == head_lane // (HD * group_size))
    ).astype(jnp.bfloat16)
    wide_keys = jnp.dot(key_ref[...], widen, preferred_element_type=jnp.float32).astype(jnp.bfloat16)
    wide_values = jnp.dot(value_ref[...], widen, preferred_element_type=jnp.float32).astype(jnp.bfloat16)
    fresh_keys = jnp.dot(
        fresh_ref[:, 0, :], widen, preferred_element_type=jnp.float32).astype(jnp.bfloat16)
    fresh_values = jnp.dot(fresh_ref[:, 1, :], widen, preferred_element_type=jnp.float32)
    page_length = tokens // pages
    lane_head = lax.broadcasted_iota(jnp.int32, (rows, width), 1) // HD
    token_of = lax.broadcasted_iota(jnp.int32, (tokens, pages), 0)
    page_of = lax.broadcasted_iota(jnp.int32, (tokens, pages), 1)
    filled = (
        (token_of // page_length == page_of) & (token_of % page_length < fill_ref[...])
    ).astype(jnp.float32)

    def attend(queries, first_row):
        stacked = jnp.concatenate(
            [jnp.where(lane_head == h, queries.astype(jnp.float32), 0.0) for h in range(heads)], 0
        ).astype(jnp.bfloat16)
        row_of = lax.broadcasted_iota(jnp.int32, (rows, pages), 0) + first_row
        owns = (owner_ref[...] == row_of).astype(jnp.float32)
        usable = lax.dot_general(
            owns, filled, (((1,), (1,)), ((), ())), preferred_element_type=jnp.float32
        ) > 0.5
        usable = jnp.concatenate([usable] * heads, 0)
        scores = lax.dot_general(
            stacked, wide_keys, (((1,), (1,)), ((), ())), preferred_element_type=jnp.float32
        ) * (HD ** -0.5)
        local_top = jnp.max(jnp.where(usable, scores, masked_score), 1, keepdims=True)
        weights = jnp.where(usable, jnp.exp(scores - local_top), 0.0)
        local_total = jnp.sum(weights, 1, keepdims=True)
        local_accum = jnp.dot(
            weights.astype(jnp.bfloat16), wide_values, preferred_element_type=jnp.float32
        )
        accum_rows = jnp.zeros((rows, width), jnp.float32)
        top_rows = jnp.zeros((rows, width), jnp.float32)
        total_rows = jnp.zeros((rows, width), jnp.float32)
        for h in range(heads):
            mine = lane_head == h
            block = slice(h * rows, (h + 1) * rows)
            accum_rows = jnp.where(mine, local_accum[block], accum_rows)
            top_rows = jnp.where(mine, jnp.broadcast_to(local_top[block], (rows, width)), top_rows)
            total_rows = jnp.where(mine, jnp.broadcast_to(local_total[block], (rows, width)), total_rows)
        for row in range(rows):
            part_ref[first_row + row, 0:1, :] = accum_rows[row:row + 1]
            part_ref[first_row + row, 1:2, :] = top_rows[row:row + 1]
            part_ref[first_row + row, 2:3, :] = total_rows[row:row + 1]
        return stacked

    stacked = attend(query_ref[...], 0)
    own_scores = lax.dot_general(
        stacked, fresh_keys, (((1,), (1,)), ((), ())), preferred_element_type=jnp.float32
    ) * (HD ** -0.5)
    own_column = lax.broadcasted_iota(jnp.int32, own_scores.shape, 1)
    own_row = lax.broadcasted_iota(jnp.int32, own_scores.shape, 0) % rows
    own_top = jnp.sum(jnp.where(own_column == own_row, own_scores, 0.0), 1, keepdims=True)
    own_rows = jnp.zeros((rows, width), jnp.float32)
    for h in range(heads):
        own_rows = jnp.where(
            lane_head == h, jnp.broadcast_to(own_top[h * rows:(h + 1) * rows], (rows, width)), own_rows)
    for row in range(rows):
        own_ref[row, 0:1, :] = fresh_values[row:row + 1]
        own_ref[row, 1:2, :] = own_rows[row:row + 1]
        own_ref[row, 2:3, :] = jnp.ones((1, width), jnp.float32)

    choices = routes_ref.shape[1]
    expert_of = lax.broadcasted_iota(jnp.int32, (rows, n_grp), 1)
    chosen = jnp.zeros((rows, n_grp), jnp.float32)
    weight_at = jnp.zeros((rows, n_grp), jnp.float32)
    for choice in range(choices):
        hit = routes_ref[:, choice:choice + 1] == expert_of
        chosen = chosen + hit.astype(jnp.float32)
        weight_at = weight_at + jnp.where(
            hit, route_weight_ref[:, choice:choice + 1].astype(jnp.float32), 0.0)
    earlier = (
        lax.broadcasted_iota(jnp.int32, (rows, rows), 1)
        < lax.broadcasted_iota(jnp.int32, (rows, rows), 0)
    ).astype(jnp.float32)
    position = jnp.dot(earlier, chosen, preferred_element_type=jnp.float32)
    slot_count = rows * n_grp
    spread_out = (
        lax.broadcasted_iota(jnp.int32, (n_grp, slot_count), 1) // rows
        == lax.broadcasted_iota(jnp.int32, (n_grp, slot_count), 0)
    ).astype(jnp.bfloat16)
    chosen_wide = jnp.dot(chosen.astype(jnp.bfloat16), spread_out, preferred_element_type=jnp.float32)
    position_wide = jnp.dot(position.astype(jnp.bfloat16), spread_out, preferred_element_type=jnp.float32)
    weight_wide = jnp.dot(weight_at.astype(jnp.bfloat16), spread_out, preferred_element_type=jnp.float32)
    slot_of = (lax.broadcasted_iota(jnp.int32, (rows, slot_count), 1) % rows).astype(jnp.float32)
    placed = (chosen_wide > 0.5) & (position_wide == slot_of)
    combine = jnp.where(placed, weight_wide, 0.0).astype(jnp.bfloat16)
    picker = jnp.transpose(placed.astype(jnp.float32)).astype(jnp.bfloat16)

    @pl.when(serving)
    def _():
        pl.semaphore_wait(barrier, common + n_grp - 1 + 2 * n_ep - 1)

    @pl.when(jnp.logical_not(serving))
    def _():
        pl.semaphore_wait(barrier, common + n_grp + 2 * n_ep)

    def first(row):
        if row < rows:
            target = (g, row)
            slot = e
        else:
            target = (mate, row - rows)
            slot = n_ep + e
        return pltpu.make_async_remote_copy(
            src_ref=part_ref.at[row], dst_ref=got.at[slot], send_sem=s1.at[row],
            recv_sem=r1.at[slot], device_id=target, device_id_type=MESH)

    swap = pltpu.make_async_remote_copy(
        src_ref=query_ref, dst_ref=mate_query, send_sem=s_q, recv_sem=r_q,
        device_id=(mate, e), device_id_type=MESH)
    swap.start()
    for row in range(rows):
        @pl.when(e != row)
        def _():
            first(row).start()

        @pl.when(e == row)
        def _():
            got[e] = part_ref[row]

    def spread(step):
        return pltpu.make_async_remote_copy(
            src_ref=block_ref, dst_ref=blocks.at[g], send_sem=s3.at[step],
            recv_sem=r3.at[g], device_id=(lax.rem(g + step, n_grp), e), device_id_type=MESH)

    def gathered_block(step):
        source = lax.rem(g + n_grp - step, n_grp)
        return pltpu.make_async_remote_copy(
            src_ref=block_ref, dst_ref=blocks.at[source], send_sem=s3.at[step],
            recv_sem=r3.at[source], device_id=(source, e), device_id_type=MESH)

    for step in range(1, n_grp):
        spread(step).start()
    blocks[g] = block_ref[...]

    swap.wait()
    attend(mate_query[...], rows)
    for row in range(rows, 2 * rows):
        first(row).start()

    def incoming_part(slot):
        return pltpu.make_async_remote_copy(
            src_ref=part_ref.at[0], dst_ref=got.at[slot], send_sem=s1.at[0],
            recv_sem=r1.at[slot], device_id=(g, 0), device_id_type=MESH)

    def second(target):
        return pltpu.make_async_remote_copy(
            src_ref=final.at[e], dst_ref=final.at[e], send_sem=s2.at[target],
            recv_sem=r2.at[e], device_id=(g, target), device_id_type=MESH)

    @pl.when(e < rows)
    def _():
        for slot in range(2 * n_ep):
            if slot < n_ep:
                @pl.when(e != slot)
                def _():
                    incoming_part(slot).wait_recv()
            else:
                incoming_part(slot).wait_recv()
        stack = got[...]
        own = own_ref[e]
        maxes = jnp.maximum(jnp.max(stack[:, 1:2, :], 0), own[1:2, :])
        factors = jnp.exp(stack[:, 1:2, :] - maxes[None])
        own_factor = jnp.exp(own[1:2, :] - maxes)
        total = jnp.sum(stack[:, 2:3, :] * factors, 0) + own_factor
        accum = jnp.sum(stack[:, 0:1, :] * factors, 0) + own[0:1, :] * own_factor
        final[e] = (accum / total).astype(jnp.bfloat16).astype(jnp.float32)
        for target in range(n_ep):
            @pl.when(e != target)
            def _():
                second(target).start()

    def arriving(row):
        return pltpu.make_async_remote_copy(
            src_ref=final.at[row], dst_ref=final.at[row], send_sem=s2.at[0],
            recv_sem=r2.at[row], device_id=(g, row), device_id_type=MESH)

    for row in range(rows):
        @pl.when(e != row)
        def _():
            arriving(row).wait_recv()

    row_ids = lax.broadcasted_iota(jnp.int32, (rows, width), 0)
    attn = jnp.zeros((rows, width), jnp.float32)
    for row in range(rows):
        attn = jnp.where(row_ids == row, jnp.broadcast_to(final[row], (rows, width)), attn)
    attn_ref[...] = attn
    attn = attn.astype(jnp.bfloat16)

    for step in range(1, n_grp):
        gathered_block(step).wait_recv()
    columns = blocks[...].reshape(n_grp * blocks.shape[1], share)
    projected = jnp.dot(attn, columns, preferred_element_type=jnp.float32)
    mixed = hidden_ref[...].astype(jnp.float32) + projected

    scaled = mixed * gain_ref[...]
    lanes = outgoing.shape[2]
    place = (
        lax.broadcasted_iota(jnp.int32, (share, lanes), 0)
        == lax.broadcasted_iota(jnp.int32, (share, lanes), 1)
    ).astype(jnp.float32)
    lane_of = lax.broadcasted_iota(jnp.int32, (rows, lanes), 1)
    carried = jnp.dot(
        scaled, place, precision=lax.Precision.HIGHEST, preferred_element_type=jnp.float32
    ) + jnp.where(lane_of == share, jnp.sum(mixed * mixed, axis=1, keepdims=True), 0.0)
    slots = outgoing.shape[1]
    picked = jnp.dot(
        picker.astype(jnp.float32), carried, precision=lax.Precision.HIGHEST,
        preferred_element_type=jnp.float32)
    outgoing[...] = picked.reshape(outgoing.shape)

    def dispatch(expert):
        return pltpu.make_async_remote_copy(
            src_ref=outgoing.at[expert], dst_ref=incoming.at[e, g % 2], send_sem=s_out.at[expert],
            recv_sem=r_in.at[g % 2, e], device_id=(expert, home), device_id_type=MESH)

    for expert in range(n_grp):
        @pl.when(jnp.logical_not(serving & (g == expert)))
        def _():
            dispatch(expert).start()

    @pl.when(serving)
    def _():
        incoming[e, g % 2] = outgoing[g]

    def gathered(half, peer):
        return pltpu.make_async_remote_copy(
            src_ref=outgoing.at[0], dst_ref=incoming.at[peer, half], send_sem=s_out.at[0],
            recv_sem=r_in.at[half, peer], device_id=(2 * e + half, peer), device_id_type=MESH)

    for half in range(2):
        for peer in range(n_ep):
            @pl.when(jnp.logical_not(serving & (g == 2 * e + half) & (e == peer)))
            def _():
                gathered(half, peer).wait_recv()

    arrived = incoming[...]
    row_total = jnp.sum(arrived[:, :, :, share:share + 1], 0)
    factor = lax.rsqrt(row_total / width + norm_epsilon)
    pre = jnp.zeros((2 * slots, up_ref.shape[1]), jnp.float32)
    for peer in range(n_ep):
        lhs = (arrived[peer][:, :, :share] * factor).astype(jnp.bfloat16).reshape(2 * slots, share)
        pre = pre + jnp.dot(
            lhs, up_ref[peer * share:(peer + 1) * share, :], preferred_element_type=jnp.float32)
    hidden_units = up_ref.shape[1] // 2
    gate = pre[:, :hidden_units]
    act = (gate / (1.0 + jnp.exp(-gate)) * pre[:, hidden_units:]).astype(jnp.bfloat16)
    for peer in range(n_ep):
        piece = jnp.dot(
            act, down_ref[:, peer * share:(peer + 1) * share], preferred_element_type=jnp.float32)
        results[peer] = piece.astype(jnp.bfloat16).astype(jnp.float32).reshape(results.shape[1:])

    def give_back(half, peer):
        return pltpu.make_async_remote_copy(
            src_ref=results.at[peer, half], dst_ref=returned.at[g], send_sem=s_res.at[half, peer],
            recv_sem=r_ret.at[g], device_id=(2 * e + half, peer), device_id_type=MESH)

    for half in range(2):
        for peer in range(n_ep):
            @pl.when(jnp.logical_not(serving & (g == 2 * e + half) & (e == peer)))
            def _():
                give_back(half, peer).start()

    @pl.when(serving)
    def _():
        returned[g] = results[e, g % 2]

    def coming_back(expert):
        return pltpu.make_async_remote_copy(
            src_ref=results.at[0, 0], dst_ref=returned.at[expert], send_sem=s_res.at[0, 0],
            recv_sem=r_ret.at[expert], device_id=(expert, home), device_id_type=MESH)

    for expert in range(n_grp):
        @pl.when(jnp.logical_not(serving & (g == expert)))
        def _():
            coming_back(expert).wait_recv()

    back = returned[...].reshape(n_grp * slots, share).astype(jnp.bfloat16)
    mix = jnp.dot(combine, back, preferred_element_type=jnp.float32)
    out_ref[...] = mixed + mix

    for row in range(2 * rows):
        if row < rows:
            @pl.when(e != row)
            def _():
                first(row).wait_send()
        else:
            first(row).wait_send()

    @pl.when(e < rows)
    def _():
        for target in range(n_ep):
            @pl.when(e != target)
            def _():
                second(target).wait_send()

    for step in range(1, n_grp):
        spread(step).wait_send()
    for expert in range(n_grp):
        @pl.when(jnp.logical_not(serving & (g == expert)))
        def _():
            dispatch(expert).wait_send()
    for half in range(2):
        for peer in range(n_ep):
            @pl.when(jnp.logical_not(serving & (g == 2 * e + half) & (e == peer)))
            def _():
                give_back(half, peer).wait_send()


def layer_call(query, keys, values, owner, fill, fresh, block, hidden, gain, routes, route_weight, up, down):
    n_ep = lax.axis_size("ep")
    n_grp = lax.axis_size("grp")
    rows, share = hidden.shape
    width = share * n_ep
    slots = rows
    return pl.pallas_call(
        functools.partial(layer_kernel, rows, n_ep, n_grp, width),
        out_shape=(
            jax.ShapeDtypeStruct((rows, share), jnp.float32),
            jax.ShapeDtypeStruct((rows, width), jnp.float32),
        ),
        in_specs=[pl.BlockSpec(memory_space=pltpu.VMEM)] * 13,
        out_specs=(pl.BlockSpec(memory_space=pltpu.VMEM),) * 2,
        scratch_shapes=[
            pltpu.VMEM((2 * rows, 3, width), jnp.float32),
            pltpu.VMEM((rows, 3, width), jnp.float32),
            pltpu.VMEM((rows, width), jnp.bfloat16),
            pltpu.SemaphoreType.DMA(()),
            pltpu.SemaphoreType.DMA(()),
            pltpu.VMEM((2 * n_ep, 3, width), jnp.float32),
            pltpu.VMEM((rows, 1, width), jnp.float32),
            pltpu.VMEM((n_grp,) + block.shape, block.dtype),
            pltpu.VMEM((n_ep, rows, 128), jnp.float32),
            pltpu.VMEM((n_grp, slots, 128), jnp.float32),
            pltpu.VMEM((n_ep, 2, slots, 128), jnp.float32),
            pltpu.VMEM((n_ep, 2, slots, share), jnp.float32),
            pltpu.VMEM((n_grp, slots, share), jnp.float32),
            pltpu.SemaphoreType.DMA((2 * rows,)),
            pltpu.SemaphoreType.DMA((2 * n_ep,)),
            pltpu.SemaphoreType.DMA((n_ep,)),
            pltpu.SemaphoreType.DMA((rows,)),
            pltpu.SemaphoreType.DMA((n_grp,)),
            pltpu.SemaphoreType.DMA((n_grp,)),
            pltpu.SemaphoreType.DMA((n_ep,)),
            pltpu.SemaphoreType.DMA((n_ep,)),
            pltpu.SemaphoreType.DMA((n_grp,)),
            pltpu.SemaphoreType.DMA((2, n_ep)),
            pltpu.SemaphoreType.DMA((2, n_ep)),
            pltpu.SemaphoreType.DMA((n_grp,)),
        ],
        compiler_params=pltpu.CompilerParams(collective_id=0, has_side_effects=True),
    )(query, keys, values, owner, fill, fresh, block, hidden, gain, routes, route_weight, up, down)


def per_device(
    hidden,
    query,
    new_kv,
    key_cache,
    value_cache,
    page_owner,
    page_fill,
    out_weight,
    norm_gain,
    gate_up,
    down,
    routes,
    route_weight,
):
    row_count = query.shape[0]
    feature_share = hidden.shape[1]
    layer_out, attn_out = layer_call(
        query, key_cache, value_cache, page_owner.reshape(1, -1),
        page_fill.reshape(1, -1), new_kv, out_weight, hidden, norm_gain.reshape(1, feature_share),
        routes, route_weight, gate_up[0], down[0],
    )
    return (layer_out.astype(jnp.bfloat16), attn_out.astype(jnp.bfloat16))


def solution(mesh):
    placed = (
        P("grp", "ep"),
        P("grp", None),
        P("grp", None, None),
        P(("grp", "ep"), None),
        P(("grp", "ep"), None),
        P(("grp", "ep")),
        P(("grp", "ep")),
        P("grp", "ep"),
        P("ep"),
        P("grp", None, None),
        P("grp", None, None),
        P("grp", None),
        P("grp", None),
    )
    return jax.shard_map(
        per_device,
        mesh=mesh,
        in_specs=placed,
        out_specs=(P("grp", "ep"), P("grp", None)),
        check_vma=False,
    )
```

```python
import jax
import jax.numpy as jnp
from jax import lax
from jax.experimental import pallas as pl
from jax.experimental.pallas import tpu as pltpu
from jax.sharding import PartitionSpec as P
import functools

D = 1536
HEADS = 24
KV_HEADS = 8
HD = 64
FF = 512
TOP = 8


masked_score = -1e30
norm_epsilon = 1e-05

MESH = pl.DeviceIdType.MESH


def layer_kernel(
    rows, n_ep, n_grp, width,
    query_ref, key_ref, value_ref, owner_ref, fill_ref,
    fresh_ref, block_ref, hidden_ref, gain_ref, routes_ref, route_weight_ref, up_ref, down_ref,
    out_ref, attn_ref,
    part_ref, own_ref, mate_query, s_q, r_q, got, final, blocks, squares, outgoing, incoming, results, returned,
    s1, r1, s2, r2, s3, r3, s_sq, r_sq, s_out, r_in, s_res, r_ret,
):
    g = lax.axis_index("grp")
    e = lax.axis_index("ep")
    mate = g + 1 - 2 * (g % 2)
    home = g // 2
    serving = home == e
    share = width // n_ep
    barrier = pltpu.get_barrier_semaphore()
    for step in range(1, n_grp):
        pl.semaphore_signal(
            barrier, inc=1, device_id=(lax.rem(g + step, n_grp), e), device_id_type=MESH
        )
    for expert in range(n_grp):
        @pl.when(jnp.logical_not(serving & (g == expert)))
        def _():
            pl.semaphore_signal(barrier, inc=1, device_id=(expert, home), device_id_type=MESH)
    for half in range(2):
        for peer in range(n_ep):
            @pl.when(jnp.logical_not(serving & (g == 2 * e + half) & (e == peer)))
            def _():
                pl.semaphore_signal(
                    barrier, inc=1, device_id=(2 * e + half, peer), device_id_type=MESH
                )
    for peer in range(n_ep):
        @pl.when(e != peer)
        def _():
            pl.semaphore_signal(barrier, inc=1, device_id=(g, peer), device_id_type=MESH)
        pl.semaphore_signal(barrier, inc=1, device_id=(mate, peer), device_id_type=MESH)
    common = n_ep - 1 + n_ep + n_grp - 1

    heads = width // HD
    both = 2 * rows
    pages = owner_ref.shape[1]
    tokens = key_ref.shape[0]
    kv_width = key_ref.shape[1]
    group_size = heads // (kv_width // HD)
    kv_lane = lax.broadcasted_iota(jnp.int32, (kv_width, width), 0)
    head_lane = lax.broadcasted_iota(jnp.int32, (kv_width, width), 1)
    widen = (
        (kv_lane % HD == head_lane % HD) & (kv_lane // HD == head_lane // (HD * group_size))
    ).astype(jnp.bfloat16)
    wide_keys = jnp.dot(key_ref[...], widen, preferred_element_type=jnp.float32).astype(jnp.bfloat16)
    wide_values = jnp.dot(value_ref[...], widen, preferred_element_type=jnp.float32).astype(jnp.bfloat16)
    fresh_keys = jnp.dot(
        fresh_ref[:, 0, :], widen, preferred_element_type=jnp.float32).astype(jnp.bfloat16)
    fresh_values = jnp.dot(fresh_ref[:, 1, :], widen, preferred_element_type=jnp.float32)
    page_length = tokens // pages
    lane_head = lax.broadcasted_iota(jnp.int32, (rows, width), 1) // HD
    token_of = lax.broadcasted_iota(jnp.int32, (tokens, pages), 0)
    page_of = lax.broadcasted_iota(jnp.int32, (tokens, pages), 1)
    filled = (
        (token_of // page_length == page_of) & (token_of % page_length < fill_ref[...])
    ).astype(jnp.float32)

    def attend(queries, first_row):
        stacked = jnp.concatenate(
            [jnp.where(lane_head == h, queries.astype(jnp.float32), 0.0) for h in range(heads)], 0
        ).astype(jnp.bfloat16)
        row_of = lax.broadcasted_iota(jnp.int32, (rows, pages), 0) + first_row
        owns = (owner_ref[...] == row_of).astype(jnp.float32)
        usable = lax.dot_general(
            owns, filled, (((1,), (1,)), ((), ())), preferred_element_type=jnp.float32
        ) > 0.5
        usable = jnp.concatenate([usable] * heads, 0)
        scores = lax.dot_general(
            stacked, wide_keys, (((1,), (1,)), ((), ())), preferred_element_type=jnp.float32
        ) * (HD ** -0.5)
        local_top = jnp.max(jnp.where(usable, scores, masked_score), 1, keepdims=True)
        weights = jnp.where(usable, jnp.exp(scores - local_top), 0.0)
        local_total = jnp.sum(weights, 1, keepdims=True)
        local_accum = jnp.dot(
            weights.astype(jnp.bfloat16), wide_values, preferred_element_type=jnp.float32
        )
        accum_rows = jnp.zeros((rows, width), jnp.float32)
        top_rows = jnp.zeros((rows, width), jnp.float32)
        total_rows = jnp.zeros((rows, width), jnp.float32)
        for h in range(heads):
            mine = lane_head == h
            block = slice(h * rows, (h + 1) * rows)
            accum_rows = jnp.where(mine, local_accum[block], accum_rows)
            top_rows = jnp.where(mine, jnp.broadcast_to(local_top[block], (rows, width)), top_rows)
            total_rows = jnp.where(mine, jnp.broadcast_to(local_total[block], (rows, width)), total_rows)
        for row in range(rows):
            part_ref[first_row + row, 0:1, :] = accum_rows[row:row + 1]
            part_ref[first_row + row, 1:2, :] = top_rows[row:row + 1]
            part_ref[first_row + row, 2:3, :] = total_rows[row:row + 1]
        return stacked

    stacked = attend(query_ref[...], 0)
    own_scores = lax.dot_general(
        stacked, fresh_keys, (((1,), (1,)), ((), ())), preferred_element_type=jnp.float32
    ) * (HD ** -0.5)
    own_column = lax.broadcasted_iota(jnp.int32, own_scores.shape, 1)
    own_row = lax.broadcasted_iota(jnp.int32, own_scores.shape, 0) % rows
    own_top = jnp.sum(jnp.where(own_column == own_row, own_scores, 0.0), 1, keepdims=True)
    own_rows = jnp.zeros((rows, width), jnp.float32)
    for h in range(heads):
        own_rows = jnp.where(
            lane_head == h, jnp.broadcast_to(own_top[h * rows:(h + 1) * rows], (rows, width)), own_rows)
    for row in range(rows):
        own_ref[row, 0:1, :] = fresh_values[row:row + 1]
        own_ref[row, 1:2, :] = own_rows[row:row + 1]
        own_ref[row, 2:3, :] = jnp.ones((1, width), jnp.float32)

    choices = routes_ref.shape[1]
    expert_of = lax.broadcasted_iota(jnp.int32, (rows, n_grp), 1)
    chosen = jnp.zeros((rows, n_grp), jnp.float32)
    weight_at = jnp.zeros((rows, n_grp), jnp.float32)
    for choice in range(choices):
        hit = routes_ref[:, choice:choice + 1] == expert_of
        chosen = chosen + hit.astype(jnp.float32)
        weight_at = weight_at + jnp.where(
            hit, route_weight_ref[:, choice:choice + 1].astype(jnp.float32), 0.0)
    earlier = (
        lax.broadcasted_iota(jnp.int32, (rows, rows), 1)
        < lax.broadcasted_iota(jnp.int32, (rows, rows), 0)
    ).astype(jnp.float32)
    position = jnp.dot(earlier, chosen, preferred_element_type=jnp.float32)
    slot_count = rows * n_grp
    spread_out = (
        lax.broadcasted_iota(jnp.int32, (n_grp, slot_count), 1) // rows
        == lax.broadcasted_iota(jnp.int32, (n_grp, slot_count), 0)
    ).astype(jnp.bfloat16)
    chosen_wide = jnp.dot(chosen.astype(jnp.bfloat16), spread_out, preferred_element_type=jnp.float32)
    position_wide = jnp.dot(position.astype(jnp.bfloat16), spread_out, preferred_element_type=jnp.float32)
    weight_wide = jnp.dot(weight_at.astype(jnp.bfloat16), spread_out, preferred_element_type=jnp.float32)
    slot_of = (lax.broadcasted_iota(jnp.int32, (rows, slot_count), 1) % rows).astype(jnp.float32)
    placed = (chosen_wide > 0.5) & (position_wide == slot_of)
    combine = jnp.where(placed, weight_wide, 0.0).astype(jnp.bfloat16)
    picker = jnp.transpose(placed.astype(jnp.float32)).astype(jnp.bfloat16)

    @pl.when(serving)
    def _():
        pl.semaphore_wait(barrier, common + n_grp - 1 + 2 * n_ep - 1)

    @pl.when(jnp.logical_not(serving))
    def _():
        pl.semaphore_wait(barrier, common + n_grp + 2 * n_ep)

    def first(row):
        if row < rows:
            target = (g, row)
            slot = e
        else:
            target = (mate, row - rows)
            slot = n_ep + e
        return pltpu.make_async_remote_copy(
            src_ref=part_ref.at[row], dst_ref=got.at[slot], send_sem=s1.at[row],
            recv_sem=r1.at[slot], device_id=target, device_id_type=MESH)

    def spread(step):
        return pltpu.make_async_remote_copy(
            src_ref=block_ref, dst_ref=blocks.at[g], send_sem=s3.at[step],
            recv_sem=r3.at[g], device_id=(lax.rem(g + step, n_grp), e), device_id_type=MESH)

    def gathered_block(step):
        source = lax.rem(g + n_grp - step, n_grp)
        return pltpu.make_async_remote_copy(
            src_ref=block_ref, dst_ref=blocks.at[source], send_sem=s3.at[step],
            recv_sem=r3.at[source], device_id=(source, e), device_id_type=MESH)

    for step in range(1, n_grp):
        spread(step).start()
    swap = pltpu.make_async_remote_copy(
        src_ref=query_ref, dst_ref=mate_query, send_sem=s_q, recv_sem=r_q,
        device_id=(mate, e), device_id_type=MESH)
    swap.start()
    for row in range(rows):
        @pl.when(e != row)
        def _():
            first(row).start()

        @pl.when(e == row)
        def _():
            got[e] = part_ref[row]

    blocks[g] = block_ref[...]

    swap.wait()
    attend(mate_query[...], rows)
    for row in range(rows, 2 * rows):
        first(row).start()

    def incoming_part(slot):
        return pltpu.make_async_remote_copy(
            src_ref=part_ref.at[0], dst_ref=got.at[slot], send_sem=s1.at[0],
            recv_sem=r1.at[slot], device_id=(g, 0), device_id_type=MESH)

    def second(target):
        return pltpu.make_async_remote_copy(
            src_ref=final.at[e], dst_ref=final.at[e], send_sem=s2.at[target],
            recv_sem=r2.at[e], device_id=(g, target), device_id_type=MESH)

    @pl.when(e < rows)
    def _():
        for slot in range(2 * n_ep):
            if slot < n_ep:
                @pl.when(e != slot)
                def _():
                    incoming_part(slot).wait_recv()
            else:
                incoming_part(slot).wait_recv()
        stack = got[...]
        own = own_ref[e]
        maxes = jnp.maximum(jnp.max(stack[:, 1:2, :], 0), own[1:2, :])
        factors = jnp.exp(stack[:, 1:2, :] - maxes[None])
        own_factor = jnp.exp(own[1:2, :] - maxes)
        total = jnp.sum(stack[:, 2:3, :] * factors, 0) + own_factor
        accum = jnp.sum(stack[:, 0:1, :] * factors, 0) + own[0:1, :] * own_factor
        final[e] = (accum / total).astype(jnp.bfloat16).astype(jnp.float32)
        for target in range(n_ep):
            @pl.when(e != target)
            def _():
                second(target).start()

    def arriving(row):
        return pltpu.make_async_remote_copy(
            src_ref=final.at[row], dst_ref=final.at[row], send_sem=s2.at[0],
            recv_sem=r2.at[row], device_id=(g, row), device_id_type=MESH)

    for row in range(rows):
        @pl.when(e != row)
        def _():
            arriving(row).wait_recv()

    row_ids = lax.broadcasted_iota(jnp.int32, (rows, width), 0)
    attn = jnp.zeros((rows, width), jnp.float32)
    for row in range(rows):
        attn = jnp.where(row_ids == row, jnp.broadcast_to(final[row], (rows, width)), attn)
    attn_ref[...] = attn
    attn = attn.astype(jnp.bfloat16)

    for step in range(1, n_grp):
        gathered_block(step).wait_recv()
    columns = blocks[...].reshape(n_grp * blocks.shape[1], share)
    projected = jnp.dot(attn, columns, preferred_element_type=jnp.float32)
    mixed = hidden_ref[...].astype(jnp.float32) + projected

    scaled = mixed * gain_ref[...]
    lanes = outgoing.shape[2]
    place = (
        lax.broadcasted_iota(jnp.int32, (share, lanes), 0)
        == lax.broadcasted_iota(jnp.int32, (share, lanes), 1)
    ).astype(jnp.float32)
    lane_of = lax.broadcasted_iota(jnp.int32, (rows, lanes), 1)
    carried = jnp.dot(
        scaled, place, precision=lax.Precision.HIGHEST, preferred_element_type=jnp.float32
    ) + jnp.where(lane_of == share, jnp.sum(mixed * mixed, axis=1, keepdims=True), 0.0)
    slots = outgoing.shape[1]
    picked = jnp.dot(
        picker.astype(jnp.float32), carried, precision=lax.Precision.HIGHEST,
        preferred_element_type=jnp.float32)
    outgoing[...] = picked.reshape(outgoing.shape)

    def dispatch(expert):
        return pltpu.make_async_remote_copy(
            src_ref=outgoing.at[expert], dst_ref=incoming.at[e, g % 2], send_sem=s_out.at[expert],
            recv_sem=r_in.at[g % 2, e], device_id=(expert, home), device_id_type=MESH)

    for expert in range(n_grp):
        @pl.when(jnp.logical_not(serving & (g == expert)))
        def _():
            dispatch(expert).start()

    @pl.when(serving)
    def _():
        incoming[e, g % 2] = outgoing[g]

    def gathered(half, peer):
        return pltpu.make_async_remote_copy(
            src_ref=outgoing.at[0], dst_ref=incoming.at[peer, half], send_sem=s_out.at[0],
            recv_sem=r_in.at[half, peer], device_id=(2 * e + half, peer), device_id_type=MESH)

    for half in range(2):
        for peer in range(n_ep):
            @pl.when(jnp.logical_not(serving & (g == 2 * e + half) & (e == peer)))
            def _():
                gathered(half, peer).wait_recv()

    arrived = incoming[...]
    row_total = jnp.sum(arrived[:, :, :, share:share + 1], 0)
    factor = lax.rsqrt(row_total / width + norm_epsilon)
    pre = jnp.zeros((2 * slots, up_ref.shape[1]), jnp.float32)
    for peer in range(n_ep):
        lhs = (arrived[peer][:, :, :share] * factor).astype(jnp.bfloat16).reshape(2 * slots, share)
        pre = pre + jnp.dot(
            lhs, up_ref[peer * share:(peer + 1) * share, :], preferred_element_type=jnp.float32)
    hidden_units = up_ref.shape[1] // 2
    gate = pre[:, :hidden_units]
    act = (gate / (1.0 + jnp.exp(-gate)) * pre[:, hidden_units:]).astype(jnp.bfloat16)
    for peer in range(n_ep):
        piece = jnp.dot(
            act, down_ref[:, peer * share:(peer + 1) * share], preferred_element_type=jnp.float32)
        results[peer] = piece.astype(jnp.bfloat16).astype(jnp.float32).reshape(results.shape[1:])

    def give_back(half, peer):
        return pltpu.make_async_remote_copy(
            src_ref=results.at[peer, half], dst_ref=returned.at[g], send_sem=s_res.at[half, peer],
            recv_sem=r_ret.at[g], device_id=(2 * e + half, peer), device_id_type=MESH)

    for half in range(2):
        for peer in range(n_ep):
            @pl.when(jnp.logical_not(serving & (g == 2 * e + half) & (e == peer)))
            def _():
                give_back(half, peer).start()

    @pl.when(serving)
    def _():
        returned[g] = results[e, g % 2]

    def coming_back(expert):
        return pltpu.make_async_remote_copy(
            src_ref=results.at[0, 0], dst_ref=returned.at[expert], send_sem=s_res.at[0, 0],
            recv_sem=r_ret.at[expert], device_id=(expert, home), device_id_type=MESH)

    for expert in range(n_grp):
        @pl.when(jnp.logical_not(serving & (g == expert)))
        def _():
            coming_back(expert).wait_recv()

    back = returned[...].reshape(n_grp * slots, share).astype(jnp.bfloat16)
    mix = jnp.dot(combine, back, preferred_element_type=jnp.float32)
    out_ref[...] = mixed + mix

    for row in range(2 * rows):
        if row < rows:
            @pl.when(e != row)
            def _():
                first(row).wait_send()
        else:
            first(row).wait_send()

    @pl.when(e < rows)
    def _():
        for target in range(n_ep):
            @pl.when(e != target)
            def _():
                second(target).wait_send()

    for step in range(1, n_grp):
        spread(step).wait_send()
    for expert in range(n_grp):
        @pl.when(jnp.logical_not(serving & (g == expert)))
        def _():
            dispatch(expert).wait_send()
    for half in range(2):
        for peer in range(n_ep):
            @pl.when(jnp.logical_not(serving & (g == 2 * e + half) & (e == peer)))
            def _():
                give_back(half, peer).wait_send()


def layer_call(query, keys, values, owner, fill, fresh, block, hidden, gain, routes, route_weight, up, down):
    n_ep = lax.axis_size("ep")
    n_grp = lax.axis_size("grp")
    rows, share = hidden.shape
    width = share * n_ep
    slots = rows
    return pl.pallas_call(
        functools.partial(layer_kernel, rows, n_ep, n_grp, width),
        out_shape=(
            jax.ShapeDtypeStruct((rows, share), jnp.float32),
            jax.ShapeDtypeStruct((rows, width), jnp.float32),
        ),
        in_specs=[pl.BlockSpec(memory_space=pltpu.VMEM)] * 13,
        out_specs=(pl.BlockSpec(memory_space=pltpu.VMEM),) * 2,
        scratch_shapes=[
            pltpu.VMEM((2 * rows, 3, width), jnp.float32),
            pltpu.VMEM((rows, 3, width), jnp.float32),
            pltpu.VMEM((rows, width), jnp.bfloat16),
            pltpu.SemaphoreType.DMA(()),
            pltpu.SemaphoreType.DMA(()),
            pltpu.VMEM((2 * n_ep, 3, width), jnp.float32),
            pltpu.VMEM((rows, 1, width), jnp.float32),
            pltpu.VMEM((n_grp,) + block.shape, block.dtype),
            pltpu.VMEM((n_ep, rows, 128), jnp.float32),
            pltpu.VMEM((n_grp, slots, 128), jnp.float32),
            pltpu.VMEM((n_ep, 2, slots, 128), jnp.float32),
            pltpu.VMEM((n_ep, 2, slots, share), jnp.float32),
            pltpu.VMEM((n_grp, slots, share), jnp.float32),
            pltpu.SemaphoreType.DMA((2 * rows,)),
            pltpu.SemaphoreType.DMA((2 * n_ep,)),
            pltpu.SemaphoreType.DMA((n_ep,)),
            pltpu.SemaphoreType.DMA((rows,)),
            pltpu.SemaphoreType.DMA((n_grp,)),
            pltpu.SemaphoreType.DMA((n_grp,)),
            pltpu.SemaphoreType.DMA((n_ep,)),
            pltpu.SemaphoreType.DMA((n_ep,)),
            pltpu.SemaphoreType.DMA((n_grp,)),
            pltpu.SemaphoreType.DMA((2, n_ep)),
            pltpu.SemaphoreType.DMA((2, n_ep)),
            pltpu.SemaphoreType.DMA((n_grp,)),
        ],
        compiler_params=pltpu.CompilerParams(collective_id=0, has_side_effects=True),
    )(query, keys, values, owner, fill, fresh, block, hidden, gain, routes, route_weight, up, down)


def per_device(
    hidden,
    query,
    new_kv,
    key_cache,
    value_cache,
    page_owner,
    page_fill,
    out_weight,
    norm_gain,
    gate_up,
    down,
    routes,
    route_weight,
):
    row_count = query.shape[0]
    feature_share = hidden.shape[1]
    layer_out, attn_out = layer_call(
        query, key_cache, value_cache, page_owner.reshape(1, -1),
        page_fill.reshape(1, -1), new_kv, out_weight, hidden, norm_gain.reshape(1, feature_share),
        routes, route_weight, gate_up[0], down[0],
    )
    return (layer_out.astype(jnp.bfloat16), attn_out.astype(jnp.bfloat16))


def solution(mesh):
    placed = (
        P("grp", "ep"),
        P("grp", None),
        P("grp", None, None),
        P(("grp", "ep"), None),
        P(("grp", "ep"), None),
        P(("grp", "ep")),
        P(("grp", "ep")),
        P("grp", "ep"),
        P("ep"),
        P("grp", None, None),
        P("grp", None, None),
        P("grp", None),
        P("grp", None),
    )
    return jax.shard_map(
        per_device,
        mesh=mesh,
        in_specs=placed,
        out_specs=(P("grp", "ep"), P("grp", None)),
        check_vma=False,
    )
```
